32 devices in a mesh: grp: 2 (over x), gx: 16 (over z, y, core).
Axes of the slice: x: 2, y: 2, z: 4, core: 2. Of those that a mesh axis runs over, the one named last changes fastest.
Arguments:
- grain_ids: int32 [96, 32, 512], P(('grp', 'gx')), parts along dimension 0, may hold values from 0 to 7
- jitter: bfloat16 [8, 96, 32, 512], P(None, ('grp', 'gx')), parts along dimension 1, may hold values from 0 to 0.5
- class_table: int32 [8, 8], replicated, may hold values from 0 to 3
- chosen: int32 [2], replicated, may hold values from 0 to 7
Outputs:
- order_params: float32 [8, 96, 32, 512], P(None, ('grp', 'gx')), parts along dimension 1
- correlation: float32 [2, 96, 32, 512], P(None, ('grp', 'gx')), parts along dimension 1
The draws below stay inside these ranges and needn't reach their ends.
There are 2 independent parts, one for each index of `grp`. The reference program is written for one: setup_inputs(seed, part) draws one part's arguments, and reference() takes and returns one part's arrays. A program takes and returns all parts, laid end to end along the dimension named above; an argument that names none is the same for every part. Nothing has to cross between parts.
All inputs are finite; a program needn't handle non-finite values.
Results may differ from the reference program's by a relative error of at most 0.0003.
Values sent between devices are 32-bit elements; how exact they have to be, the bound alone decides.
No kernel may reach another device: no remote copies, remote signals or barrier semaphores. Data moves between devices by JAX's collectives and lax.ppermute only.
A program may use at most 128 MiB of HBM per device.

```python
import jax
import jax.numpy as jnp
from jax import lax

NY = 512
NZ = 32
STEPS = 3
NX = 48


def touch_ends(entries, stream_key, low, top_value):
    longest = entries.shape.index(max(entries.shape))
    spots = []
    for shift in (0, 1):
        where = [jax.random.randint(jax.random.fold_in(stream_key, axis), (), 0, length) for axis, length in enumerate(entries.shape)]
        where[longest] = (where[longest] + shift) % entries.shape[longest]
        spots.append(tuple(where))
    return entries.at[spots[0]].set(low).at[spots[1]].set(top_value)


def steps_of(rng, shape, cuts, smallest, largest):
    def one(dim, blocks):
        heights = jax.random.uniform(jax.random.fold_in(jax.random.fold_in(rng, 6), dim), (blocks,), jnp.float32, smallest / len(cuts), largest / len(cuts))
        return jnp.repeat(jnp.exp(heights), shape[dim] // blocks).reshape((-1,) + (1,) * (len(shape) - dim - 1))

    loudness = one(*cuts[0])
    for cut in cuts[1:]:
        loudness = loudness * one(*cut)
    return loudness


def setup_inputs(seed: int = 0, part: int = 0) -> dict:
    key_list = jax.random.split(jax.random.key(seed), 5)
    own_keys = jax.random.split(jax.random.fold_in(key_list[4], part), 5)
    return {
        "grain_ids": touch_ends(jax.random.randint(own_keys[0], (NX, NZ, NY), 0, 8), jax.random.fold_in(own_keys[0], 1), 0, 7).astype(jnp.int32),
        "jitter": jnp.clip(0.5 * jax.random.uniform(own_keys[1], (8, NX, NZ, NY), jnp.float32) ** steps_of(own_keys[1], (8, NX, NZ, NY), ((1, 16),), -0.2, 0.2), 0.0, 0.5).astype(jnp.bfloat16),
        "class_table": touch_ends(jax.random.randint(key_list[2], (8, 8), 0, 4), jax.random.fold_in(key_list[2], 1), 0, 3).astype(jnp.int32),
        "chosen": jax.random.randint(key_list[3], (2,), 0, 8).astype(jnp.int32),
    }


def mobility_of(grain_ids, class_table):
    levels = 0.4 + 0.2 * class_table.astype(jnp.float32)
    onehot = (grain_ids[None] == jnp.arange(8, dtype=jnp.int32)[:, None, None, None]).astype(jnp.float32)
    return jnp.einsum('gi,gxzy->ixzy', levels, onehot, precision=lax.Precision.HIGHEST), onehot


def reference(grain_ids, jitter, class_table, chosen):
    mobility, onehot = mobility_of(grain_ids, class_table)
    eta = 0.6 * onehot + jitter.astype(jnp.float32)
    for step in range(STEPS):
        lap = jnp.roll(eta, -1, 1) + jnp.roll(eta, 1, 1)
        lap = lap + jnp.roll(eta, -1, 2) + jnp.roll(eta, 1, 2)
        lap = lap + jnp.roll(eta, -1, 3) + jnp.roll(eta, 1, 3)
        lap = lap - 6.0 * eta
        total = jnp.sum(eta * eta, axis=0)
        drive = -eta + eta * eta * eta + 3.0 * eta * (total[None] - eta * eta)
        eta = eta - 0.12 * mobility * (drive - lap)
    select = (chosen[:, None] == jnp.arange(8, dtype=jnp.int32)[None, :]).astype(jnp.float32)
    fields = jnp.einsum('ki,ixzy->kxzy', select, eta, precision=lax.Precision.HIGHEST)
    count = NX * NZ * NY
    spectrum_c = jnp.fft.fftn(fields, axes=(1, 2, 3))
    power = jnp.real(spectrum_c) ** 2 + jnp.imag(spectrum_c) ** 2
    power = power.at[:, 0, 0, 0].set(0.0)
    correlation = jnp.real(jnp.fft.ifftn(power, axes=(1, 2, 3))) / count
    return eta, correlation.astype(jnp.float32)
```

```python
import math

import jax
import jax.numpy as jnp
import ml_dtypes
import numpy as np
from jax import lax
from jax.experimental import pallas as pl
from jax.experimental.pallas import tpu as pltpu
from jax.sharding import PartitionSpec as P

STEPS = 3
GRAINS = 8
F32 = jnp.float32
BF16 = jnp.bfloat16
VMEM = pl.BlockSpec(memory_space=pltpu.VMEM)
SMEM = pl.BlockSpec(memory_space=pltpu.SMEM)
PARAMS = pltpu.CompilerParams(vmem_limit_bytes=48 * 2**20)


def halves(table):
    table = np.asarray(table, np.float32)
    high = table.astype(ml_dtypes.bfloat16)
    low = (table - high.astype(np.float32)).astype(ml_dtypes.bfloat16)
    return high, low


def phases(length, rows=None):
    index = np.arange(length)
    product = np.arange(length if rows is None else rows)[:, None] * index[None, :] % length
    angle = product * (2.0 * math.pi / length)
    return np.cos(angle), np.sin(angle)


def y_table(width):
    cos_y, sin_y = phases(width, width // 2)
    sin_y = -sin_y
    sin_y[0] = 1.0 - 2.0 * (np.arange(width) % 2)
    return np.concatenate([cos_y, sin_y], axis=0)


def z_tables(depth):
    cos_z, sin_z = phases(depth)
    two = np.eye(2)
    cos_z, sin_z = np.kron(two, cos_z), np.kron(two, sin_z)
    forward = np.block([[cos_z, -sin_z], [sin_z, cos_z]])
    half = 2 * depth
    forward_turned = np.concatenate([forward[:, half:], -forward[:, :half]], axis=1)
    inverse = np.block([[cos_z, sin_z], [-sin_z, cos_z]])
    inverse_turned = np.concatenate([-inverse[:, half:], inverse[:, :half]], axis=1)
    return (
        np.concatenate([forward, forward_turned], axis=1),
        np.concatenate([inverse, inverse_turned], axis=0),
    )


def split(value):
    high = value.astype(BF16)
    low = (value - high.astype(F32)).astype(BF16)
    return high, low


def dot3(left, right, contract=((1,), (0,))):
    def one(a, b):
        return lax.dot_general(a, b, (contract, ((), ())), preferred_element_type=F32)

    return one(left[0], right[0]) + (one(left[0], right[1]) + one(left[1], right[0]))


def start_kernel(chosen, jitter, grain_ids, p0, p1, p2, c0, c2):
    for plane, out in enumerate((p0, p1, p2)):
        ids = grain_ids[plane]

        def body(i, carry):
            base = jnp.where(ids == i, jnp.float32(0.6), jnp.float32(0.0))
            out[i] = base + jitter[i, plane].astype(F32)
            return carry

        lax.fori_loop(0, GRAINS, body, 0)
    for k in range(2):
        c0[k] = p0[chosen[k]]
        c2[k] = p2[chosen[k]]


def grain_of(start):
    ids = jnp.where(start[1] > 0.55, 1, 0)
    for g in range(2, GRAINS):
        ids = jnp.where(start[g] > 0.55, g, ids)
    return ids


def rate(classes, ids, i):
    def level(g):
        return 0.12 * (0.4 + 0.2 * classes[g, i].astype(F32))

    value = jnp.full(ids.shape, level(0), F32)
    for g in range(1, GRAINS):
        value = jnp.where(ids == g, level(g), value)
    return value


def squares(state):
    total = state[0] * state[0]
    for i in range(1, GRAINS):
        total = total + state[i] * state[i]
    return 5.0 + 3.0 * total


def update(e, before, after, total, mobility):
    depth, width = e.shape
    near = before + after
    near = near + (pltpu.roll(e, 1, 0) + pltpu.roll(e, depth - 1, 0))
    near = near + (pltpu.roll(e, 1, 1) + pltpu.roll(e, width - 1, 1))
    return e + mobility * (near - e * (total - 2.0 * (e * e)))


def step_plane(center, before, after, mobility, out):
    total = squares(center)

    def body(i, carry):
        out[i] = update(center[i], before[i], after[i], total, mobility[i])
        return carry

    lax.fori_loop(0, GRAINS, body, 0)


def rates_plane(classes, start, out):
    ids = grain_of(start)

    def body(i, carry):
        out[i] = rate(classes, ids, i)
        return carry

    lax.fori_loop(0, GRAINS, body, 0)


def main_kernel(
    chosen, classes, p0, p1, p2, prev1, next1, prev2, next2, prev3, next3, table_high, table_low,
    packed, eta1, eta2, rates, edge, fields,
):
    depth, width = p0.shape[1:]
    starts = (prev1, p0, p1, p2, next1)
    for k, start in enumerate(starts):
        rates_plane(classes, start, rates.at[k])
    row = (prev2,) + starts + (next2,)
    for k in range(5):
        step_plane(row[k + 1], row[k], row[k + 2], rates.at[k], eta1.at[k])
    for k in range(3):
        step_plane(eta1.at[k + 1], eta1.at[k], eta1.at[k + 2], rates.at[k + 1], eta2.at[k])
    for side, (far, mid, near, inner) in enumerate(((prev3, prev2, prev1, 0), (next3, next2, next1, 4))):
        ids = grain_of(mid)
        total0 = squares(mid)
        total1 = squares(eta1.at[inner])
        neighbour = 1 if side == 0 else 3
        for k in range(2):
            i = chosen[k]
            first = update(mid[i], far[k], near[i], total0, rate(classes, ids, i))
            edge[side, k] = update(eta1[inner, i], first, eta1[neighbour, i], total1, rates[inner, i])
    for k in range(3):
        total = squares(eta2.at[k])
        for f in range(2):
            i = chosen[f]
            before = edge[0, f] if k == 0 else eta2[k - 1, i]
            after = edge[1, f] if k == 2 else eta2[k + 1, i]
            value = update(eta2[k, i], before, after, total, rates[k + 1, i])
            base = k * 4 * depth + f * depth
            fields[base : base + depth] = value
            fields[base + 2 * depth : base + 3 * depth] = value
    full = dot3((table_high[...], table_low[...]), split(fields[...]), ((1,), (1,)))
    slots = width // 2
    lanes = 4 * depth
    real_lane = lax.broadcasted_iota(jnp.int32, (slots, lanes), 1) < 2 * depth
    for k in range(3):
        part = full[:, k * lanes : (k + 1) * lanes]
        part = jnp.where(real_lane, part[:slots], part[slots:])
        if len(packed.shape) == 3 and packed.shape[0] == 3:
            packed[k] = part
        else:
            devices, rows, _ = packed.shape
            rows = rows // 3
            packed[:, k * rows : (k + 1) * rows, :] = part.reshape(devices, rows, lanes)


def rest_kernel(
    classes, p0, p1, p2, prev1, next1, prev2, next2, prev3, next3, eta1, eta2, out, rates, edge, other
):
    for far, mid, near, inner, neighbour, side in (
        (prev3, prev2, prev1, 0, 1, 0),
        (next3, next2, next1, 4, 3, 1),
    ):
        rates_plane(classes, mid, rates)
        step_plane(mid, far, near, rates, other)
        rates_plane(classes, near, rates)
        step_plane(eta1.at[inner], other, eta1.at[neighbour], rates, edge.at[side])
    row = (edge.at[0], eta2.at[0], eta2.at[1], eta2.at[2], edge.at[1])
    for k, start in enumerate((p0, p1, p2)):
        rates_plane(classes, start, rates)
        step_plane(row[k + 1], row[k], row[k + 2], rates, out.at[:, k])


def line_kernel(
    lines, zf_high, zf_low, zi_high, zi_low, xf_high, xf_low, out, r1, r2, gathered, scale
):
    rows, lanes = lines.shape
    total_x = xf_high.shape[0]
    slots = rows // total_x
    half = lanes // 2
    zf = (zf_high[...], zf_low[...])
    xf = (xf_high[...], xf_low[...])
    turned = dot3(split(lines[...]), zf)
    r1[...] = turned[:, :lanes]
    r2[...] = turned[:, lanes:]
    real_lane = lax.broadcasted_iota(jnp.int32, (total_x, lanes), 1) < half
    mixed = lines[pl.ds(0, total_x, stride=slots), :]
    pair = jnp.concatenate(
        [jnp.where(real_lane, mixed, 0.0), jnp.where(real_lane, pltpu.roll(mixed, half, 1), 0.0)], axis=0
    )
    pair = dot3(split(pair), zf)
    for j in range(slots):
        at = slice(j * lanes, (j + 1) * lanes)
        gathered[:total_x, at] = r1[pl.ds(j, total_x, stride=slots), :]
        gathered[total_x:, at] = r2[pl.ds(j, total_x, stride=slots), :]
    for j in range(2):
        at = slice((slots + j) * lanes, (slots + j + 1) * lanes)
        gathered[:total_x, at] = pair[j * total_x : (j + 1) * total_x, :lanes]
        gathered[total_x:, at] = pair[j * total_x : (j + 1) * total_x, lanes:]
    spectrum = dot3(xf, split(gathered[...]))

    def power(j):
        part = spectrum[:, j * lanes : (j + 1) * lanes]
        part = part * part
        return part + pltpu.roll(part, half, 1)

    first = lax.axis_index("gx") == 0
    lane = lax.broadcasted_iota(jnp.int32, (total_x, lanes), 1)
    line = lax.broadcasted_iota(jnp.int32, (total_x, lanes), 0)
    constant = jnp.logical_and(line == 0, jnp.logical_or(lane == 0, lane == half // 2))
    powers = []
    for j in range(slots):
        value = jnp.where(real_lane, power(j), 0.0) * (2.0 * scale)
        if j == 0:
            special = jnp.where(real_lane, power(slots), power(slots + 1)) * scale
            special = jnp.where(constant, 0.0, special)
            value = jnp.where(first, special, value)
        powers.append(value)
    powers = split(jnp.concatenate(powers, axis=1))
    cos_x = (xf[0][:, :total_x], xf[1][:, :total_x])
    sin_x = (xf[0][:, total_x:], xf[1][:, total_x:])
    for target, matrix in ((r1, cos_x), (r2, sin_x)):
        back = dot3(matrix, powers)
        for j in range(slots):
            target[pl.ds(j, total_x, stride=slots), :] = back[:, j * lanes : (j + 1) * lanes]
    zi = (zi_high[...], zi_low[...])
    out[...] = dot3(split(r1[...]), (zi[0][:lanes], zi[1][:lanes])) + dot3(
        split(r2[...]), (zi[0][lanes:], zi[1][lanes:])
    )


def finish_kernel(returned, table_high, table_low, out):
    fields, planes, depth, width = out.shape
    lanes = 2 * fields * depth
    half = lanes // 2
    slots = width // 2
    stacked = []
    for k in range(planes):
        if returned.shape[0] == planes:
            part = returned[k]
        else:
            devices, rows, _ = returned.shape
            rows = rows // planes
            part = returned[:, k * rows : (k + 1) * rows, :].reshape(slots, lanes)
        part = part.T
        stacked.append(jnp.concatenate([part[:half], part[half:]], axis=1))
    stacked = split(jnp.concatenate(stacked, axis=0))
    result = dot3(stacked, (table_high[...], table_low[...]))
    for k in range(planes):
        for f in range(fields):
            base = k * half + f * depth
            out[f, k] = result[base : base + depth]


def call(kernel, outs, in_specs, *args, scratch=(), flops=0, moved=0):
    return pl.pallas_call(
        kernel,
        out_shape=outs,
        in_specs=in_specs,
        out_specs=jax.tree.map(lambda _: VMEM, outs),
        scratch_shapes=scratch,
        compiler_params=PARAMS,
        cost_estimate=pl.CostEstimate(flops=flops, bytes_accessed=moved, transcendentals=0),
    )(*args)


def shards(grain_ids, jitter, class_table, chosen):
    planes, depth, width = grain_ids.shape
    devices = lax.axis_size("gx")
    total_x = planes * devices
    count = float(total_x * depth * width)
    slots = width // 2
    share = slots // devices
    lanes = 4 * depth
    up = [(i, (i + 1) % devices) for i in range(devices)]
    down = [(j, i) for i, j in up]
    aligned = share % 8 == 0

    def shape(*dims):
        return jax.ShapeDtypeStruct(dims, F32)

    plane = (GRAINS, depth, width)
    table = [jnp.asarray(part) for part in halves(y_table(width))]
    z_forward, z_inverse = z_tables(depth)
    z_parts = [jnp.asarray(part) for matrix in (z_forward, z_inverse) for part in halves(matrix)]
    x_parts = [jnp.asarray(part) for part in halves(np.concatenate(phases(total_x), axis=1))]

    two = (2, depth, width)
    p0, p1, p2, c0, c2 = call(
        start_kernel,
        (shape(*plane), shape(*plane), shape(*plane), shape(*two), shape(*two)),
        [SMEM, VMEM, VMEM],
        chosen, jitter, grain_ids,
        flops=2**21, moved=2**22,
    )
    prev1 = lax.ppermute(p2, "gx", up)
    next1 = lax.ppermute(p0, "gx", down)
    prev2 = lax.ppermute(p1, "gx", up)
    next2 = lax.ppermute(p1, "gx", down)
    prev3 = lax.ppermute(c0, "gx", up)
    next3 = lax.ppermute(c2, "gx", down)
    late0, late2, prev3, next3 = lax.optimization_barrier((p0, p2, prev3, next3))
    prev3_all = lax.ppermute(late0, "gx", up)
    next3_all = lax.ppermute(late2, "gx", down)
    packed_shape = (devices, planes * share, lanes) if aligned else (planes, slots, lanes)
    packed, eta1, eta2 = call(
        main_kernel,
        (shape(*packed_shape), shape(5, *plane), shape(3, *plane)),
        [SMEM, SMEM] + [VMEM] * 11,
        chosen, class_table, p0, p1, p2, prev1, next1, prev2, next2, prev3, next3, *table,
        scratch=[
            pltpu.VMEM((5, *plane), F32),
            pltpu.VMEM((2, *two), F32),
            pltpu.VMEM((planes * lanes, width), F32),
        ],
        flops=2**28, moved=2**24,
    )
    if aligned:
        lines = lax.all_to_all(packed, "gx", split_axis=0, concat_axis=0, tiled=True)
    else:
        lines = lax.all_to_all(packed, "gx", split_axis=1, concat_axis=0, tiled=True)
    lines = lines.reshape(total_x * share, lanes)
    order_params = call(
        rest_kernel,
        shape(GRAINS, planes, depth, width),
        [SMEM] + [VMEM] * 11,
        class_table, p0, p1, p2, prev1, next1, prev2, next2, prev3_all, next3_all, eta1, eta2,
        scratch=[pltpu.VMEM(plane, F32), pltpu.VMEM((2, *plane), F32), pltpu.VMEM(plane, F32)],
        flops=2**26, moved=2**24,
    )

    def lines_body(*refs):
        line_kernel(*refs, scale=1.0 / (count * count))

    back = call(
        lines_body,
        shape(total_x * share, lanes),
        [VMEM] * 7,
        lines, *z_parts, *x_parts,
        scratch=[
            pltpu.VMEM((total_x * share, lanes), F32),
            pltpu.VMEM((total_x * share, lanes), F32),
            pltpu.VMEM((2 * total_x, (share + 2) * lanes), F32),
        ],
        flops=2**28, moved=2**22,
    )
    back = back.reshape(devices, planes * share, lanes)
    returned = lax.all_to_all(back, "gx", split_axis=0, concat_axis=0, tiled=True)
    if not aligned:
        returned = returned.reshape(devices, planes, share, lanes).transpose(1, 0, 2, 3)
        returned = returned.reshape(planes, slots, lanes)
    correlation = call(
        finish_kernel,
        shape(2, planes, depth, width),
        [VMEM] * 3,
        returned, *table,
        flops=2**28, moved=2**22,
    )
    return (order_params, correlation)


def solution(mesh):
    in_specs = (P(("grp", "gx"), None, None), P(None, ("grp", "gx"), None, None), P(), P())
    out_specs = (P(None, ("grp", "gx"), None, None), P(None, ("grp", "gx"), None, None))
    return jax.shard_map(shards, mesh=mesh, in_specs=in_specs, out_specs=out_specs, check_vma=False)
```

```python
import math

import jax
import jax.numpy as jnp
import ml_dtypes
import numpy as np
from jax import lax
from jax.experimental import pallas as pl
from jax.experimental.pallas import tpu as pltpu
from jax.sharding import PartitionSpec as P

STEPS = 3
GRAINS = 8
F32 = jnp.float32
BF16 = jnp.bfloat16
VMEM = pl.BlockSpec(memory_space=pltpu.VMEM)
ANY = pl.BlockSpec(memory_space=pl.ANY)
PARAMS = pltpu.CompilerParams(vmem_limit_bytes=28 * 2**20)


def halves(table):
    table = np.asarray(table, np.float32)
    high = table.astype(ml_dtypes.bfloat16)
    low = (table - high.astype(np.float32)).astype(ml_dtypes.bfloat16)
    return high, low


def phases(length, rows=None):
    index = np.arange(length)
    product = np.arange(length if rows is None else rows)[:, None] * index[None, :] % length
    angle = product * (2.0 * math.pi / length)
    return np.cos(angle), np.sin(angle)


def y_table(width):
    cos_y, sin_y = phases(width, width // 2)
    sin_y = -sin_y
    sin_y[0] = 1.0 - 2.0 * (np.arange(width) % 2)
    return np.concatenate([cos_y, sin_y], axis=0)


def z_tables(depth):
    cos_z, sin_z = phases(depth)
    two = np.eye(2)
    cos_z, sin_z = np.kron(two, cos_z), np.kron(two, sin_z)
    forward = np.block([[cos_z, -sin_z], [sin_z, cos_z]])
    half = 2 * depth
    forward_turned = np.concatenate([forward[:, half:], -forward[:, :half]], axis=1)
    inverse = np.block([[cos_z, sin_z], [-sin_z, cos_z]])
    inverse_turned = np.concatenate([-inverse[:, half:], inverse[:, :half]], axis=1)
    return (
        np.concatenate([forward, forward_turned], axis=1),
        np.concatenate([inverse, inverse_turned], axis=0),
    )


def split(value):
    high = value.astype(BF16)
    low = (value - high.astype(F32)).astype(BF16)
    return high, low


def dot3(left, right, contract=((1,), (0,))):
    def one(a, b):
        return lax.dot_general(a, b, (contract, ((), ())), preferred_element_type=F32)

    return one(left[0], right[0]) + (one(left[0], right[1]) + one(left[1], right[0]))


def fetch(pairs, semaphores):
    copies = [pltpu.make_async_copy(src, dst, semaphores.at[k]) for k, (src, dst) in enumerate(pairs)]
    for copy in copies:
        copy.start()
    return copies


def pair_of(chosen):
    first, second = chosen[0], chosen[1]
    second = jnp.where(second == first, lax.rem(first + 1, GRAINS), second)
    return first, second


def others_of(chosen):
    first, second = pair_of(chosen)
    low, high = jnp.minimum(first, second), jnp.maximum(first, second)

    def other(r):
        i = r + (r >= low).astype(jnp.int32)
        return i + (i >= high).astype(jnp.int32)

    return other


def start_kernel(chosen_any, jitter_any, ids_any, to_next, to_prev, c0, c2, chosen, jitter, grain_ids, semaphores):
    planes = grain_ids.shape[0]
    pairs = []
    for k in range(planes):
        pairs.append((jitter_any.at[:, k], jitter.at[:, k]))
        pairs.append((ids_any.at[k], grain_ids.at[k]))
    pairs.append((chosen_any, chosen))
    copies = fetch(pairs, semaphores)
    for plane, outs in enumerate(((to_prev.at[0],), (to_prev.at[1], to_next.at[0]), (to_next.at[1],))):
        copies[2 * plane].wait()
        copies[2 * plane + 1].wait()
        ids = grain_ids[plane]
        for i in range(GRAINS):
            base = jnp.where(ids == i, jnp.float32(0.6), jnp.float32(0.0))
            value = base + jitter[i, plane].astype(F32)
            for out in outs:
                out[i] = value
    copies[-1].wait()
    for k, i in enumerate(pair_of(chosen)):
        c0[k] = to_prev[0, i]
        c2[k] = to_next[1, i]


def grain_of(start):
    ids = jnp.where(start[1] > 0.55, 1, 0)
    for g in range(2, GRAINS):
        ids = jnp.where(start[g] > 0.55, g, ids)
    return ids


def rate(classes, ids, i):
    def level(g):
        return 0.12 * (0.4 + 0.2 * classes[g, i].astype(F32))

    value = jnp.full(ids.shape, level(0), F32)
    for g in range(1, GRAINS):
        value = jnp.where(ids == g, level(g), value)
    return value


def squares(state):
    total = state[0] * state[0]
    for i in range(1, GRAINS):
        total = total + state[i] * state[i]
    return 5.0 + 3.0 * total


def update(e, before, after, total, mobility):
    depth, width = e.shape
    near = before + after
    near = near + (pltpu.roll(e, 1, 0) + pltpu.roll(e, depth - 1, 0))
    near = near + (pltpu.roll(e, 1, 1) + pltpu.roll(e, width - 1, 1))
    return e + mobility * (near - e * (total - 2.0 * (e * e)))


def step_plane(center, before, after, mobility, out):
    total = squares(center)

    def body(i, carry):
        out[i] = update(center[i], before[i], after[i], total, mobility[i])
        return carry

    lax.fori_loop(0, GRAINS, body, 0)


def rates_plane(classes, start, out):
    ids = grain_of(start)

    def body(i, carry):
        out[i] = rate(classes, ids, i)
        return carry

    lax.fori_loop(0, GRAINS, body, 0)


def inner_kernel(chosen_any, classes_any, to_next, to_prev, rates, middle, r0, r2, chosen, classes, semaphores):
    copies = fetch(((chosen_any, chosen), (classes_any, classes)), semaphores)
    row = (to_prev.at[0], to_prev.at[1], to_next.at[1])
    for copy in copies:
        copy.wait()
    other = others_of(chosen)

    def body(r, carry):
        i = other(r)
        r0[r] = to_prev[0, i]
        r2[r] = to_next[1, i]
        return carry

    lax.fori_loop(0, GRAINS - 2, body, 0)
    for k in range(3):
        rates_plane(classes, row[k], rates.at[k])
    step_plane(row[1], row[0], row[2], rates.at[1], middle)


def near_kernel(
    classes_any, to_next, to_prev, prev, nxt, rates, middle, edge_rates, eta1, eta2, classes, semaphores
):
    copies = fetch(((classes_any, classes),), semaphores)
    p0, p1, p2 = to_prev.at[0], to_prev.at[1], to_next.at[1]
    step_plane(p0, prev.at[1], p1, rates.at[0], eta1.at[1])
    step_plane(p2, p1, nxt.at[0], rates.at[2], eta1.at[2])
    copies[0].wait()
    rates_plane(classes, prev.at[1], edge_rates.at[0])
    rates_plane(classes, nxt.at[0], edge_rates.at[1])
    step_plane(middle, eta1.at[1], eta1.at[2], rates.at[1], eta2.at[1])
    step_plane(prev.at[1], prev.at[0], p0, edge_rates.at[0], eta1.at[0])
    step_plane(nxt.at[0], p2, nxt.at[1], edge_rates.at[1], eta1.at[3])
    step_plane(eta1.at[1], eta1.at[0], middle, rates.at[0], eta2.at[0])
    step_plane(eta1.at[2], middle, eta1.at[3], rates.at[2], eta2.at[2])


def pair_kernel(
    chosen_any, classes_any, prev, nxt, prev3, next3, rates, edge_rates, eta1, eta2, high_any, low_any,
    packed, final, chosen, classes, high, low, edge, fields, semaphores,
):
    copies = fetch(
        ((chosen_any, chosen), (classes_any, classes), (high_any, high), (low_any, low)), semaphores
    )
    depth, width = final.shape[2:]
    totals = [squares(eta2.at[k]) for k in range(3)]
    copies[0].wait()
    copies[1].wait()
    pair = pair_of(chosen)
    for side, (far, mid, near) in enumerate(((prev3, prev.at[0], prev.at[1]), (next3, nxt.at[1], nxt.at[0]))):
        inner, neighbour = (0, 1) if side == 0 else (3, 2)
        ids = grain_of(mid)
        total0 = squares(mid)
        total1 = squares(eta1.at[inner])
        for k, i in enumerate(pair):
            first = update(mid[i], far[k], near[i], total0, rate(classes, ids, i))
            edge[side, k] = update(eta1[inner, i], first, eta1[neighbour, i], total1, edge_rates[side, i])
    repeated = chosen[1] == chosen[0]
    for k in range(3):
        values = []
        for f, i in enumerate(pair):
            before = edge[0, f] if k == 0 else eta2[k - 1, i]
            after = edge[1, f] if k == 2 else eta2[k + 1, i]
            value = update(eta2[k, i], before, after, totals[k], rates[k, i])
            final[f, k] = value
            values.append(value)
        values[1] = jnp.where(repeated, values[0], values[1])
        for f in range(2):
            base = k * 4 * depth + f * depth
            fields[base : base + depth] = values[f]
            fields[base + 2 * depth : base + 3 * depth] = values[f]
    copies[2].wait()
    copies[3].wait()
    full = dot3((high[...], low[...]), split(fields[...]), ((1,), (1,)))
    slots = width // 2
    lanes = 4 * depth
    real_lane = lax.broadcasted_iota(jnp.int32, (slots, lanes), 1) < 2 * depth
    for k in range(3):
        part = full[:, k * lanes : (k + 1) * lanes]
        part = jnp.where(real_lane, part[:slots], part[slots:])
        if packed.shape[0] == 3:
            packed[k] = part
        else:
            devices, rows, _ = packed.shape
            rows = rows // 3
            packed[:, k * rows : (k + 1) * rows, :] = part.reshape(devices, rows, lanes)


def rest_kernel(
    chosen_any, classes_any, prev, nxt, prev3, next3, rates, edge_rates, eta1, eta2, final,
    out, chosen, classes, edge, semaphores,
):
    copies = fetch(((chosen_any, chosen), (classes_any, classes)), semaphores)
    for copy in copies:
        copy.wait()
    other = others_of(chosen)
    rest = GRAINS - 2
    for side, (far, mid, near) in enumerate(((prev3, prev.at[0], prev.at[1]), (next3, nxt.at[1], nxt.at[0]))):
        inner, neighbour = (0, 1) if side == 0 else (3, 2)
        ids = grain_of(mid)
        total0 = squares(mid)
        total1 = squares(eta1.at[inner])

        def body(r, carry):
            i = other(r)
            first = update(mid[i], far[r], near[i], total0, rate(classes, ids, i))
            edge[side, r] = update(eta1[inner, i], first, eta1[neighbour, i], total1, edge_rates[side, i])
            return carry

        lax.fori_loop(0, rest, body, 0)
    for k in range(3):
        total = squares(eta2.at[k])

        def last(r, carry):
            i = other(r)
            before = edge[0, r] if k == 0 else eta2[k - 1, i]
            after = edge[1, r] if k == 2 else eta2[k + 1, i]
            out[i, k] = update(eta2[k, i], before, after, total, rates[k, i])
            return carry

        lax.fori_loop(0, rest, last, 0)
        for f, i in enumerate(pair_of(chosen)):
            out[i, k] = final[f, k]


def line_kernel(
    lines, zf_high, zf_low, zi_high, zi_low, xf_high, xf_low, out, r1, r2, gathered, scale
):
    rows, lanes = lines.shape
    total_x = xf_high.shape[0]
    slots = rows // total_x
    half = lanes // 2
    zf = (zf_high[...], zf_low[...])
    xf = (xf_high[...], xf_low[...])
    turned = dot3(split(lines[...]), zf)
    r1[...] = turned[:, :lanes]
    r2[...] = turned[:, lanes:]
    real_lane = lax.broadcasted_iota(jnp.int32, (total_x, lanes), 1) < half
    mixed = lines[pl.ds(0, total_x, stride=slots), :]
    pair = jnp.concatenate(
        [jnp.where(real_lane, mixed, 0.0), jnp.where(real_lane, pltpu.roll(mixed, half, 1), 0.0)], axis=0
    )
    pair = dot3(split(pair), zf)
    for j in range(slots):
        at = slice(j * lanes, (j + 1) * lanes)
        gathered[:total_x, at] = r1[pl.ds(j, total_x, stride=slots), :]
        gathered[total_x:, at] = r2[pl.ds(j, total_x, stride=slots), :]
    for j in range(2):
        at = slice((slots + j) * lanes, (slots + j + 1) * lanes)
        gathered[:total_x, at] = pair[j * total_x : (j + 1) * total_x, :lanes]
        gathered[total_x:, at] = pair[j * total_x : (j + 1) * total_x, lanes:]
    spectrum = dot3(xf, split(gathered[...]))

    def power(j):
        part = spectrum[:, j * lanes : (j + 1) * lanes]
        part = part * part
        return part + pltpu.roll(part, half, 1)

    first = lax.axis_index("gx") == 0
    lane = lax.broadcasted_iota(jnp.int32, (total_x, lanes), 1)
    line = lax.broadcasted_iota(jnp.int32, (total_x, lanes), 0)
    constant = jnp.logical_and(line == 0, jnp.logical_or(lane == 0, lane == half // 2))
    powers = []
    for j in range(slots):
        value = jnp.where(real_lane, power(j), 0.0) * (2.0 * scale)
        if j == 0:
            special = jnp.where(real_lane, power(slots), power(slots + 1)) * scale
            special = jnp.where(constant, 0.0, special)
            value = jnp.where(first, special, value)
        powers.append(value)
    powers = split(jnp.concatenate(powers, axis=1))
    cos_x = (xf[0][:, :total_x], xf[1][:, :total_x])
    sin_x = (xf[0][:, total_x:], xf[1][:, total_x:])
    for target, matrix in ((r1, cos_x), (r2, sin_x)):
        back = dot3(matrix, powers)
        for j in range(slots):
            target[pl.ds(j, total_x, stride=slots), :] = back[:, j * lanes : (j + 1) * lanes]
    zi = (zi_high[...], zi_low[...])
    out[...] = dot3(split(r1[...]), (zi[0][:lanes], zi[1][:lanes])) + dot3(
        split(r2[...]), (zi[0][lanes:], zi[1][lanes:])
    )


def finish_kernel(returned, table_high, table_low, out):
    fields, planes, depth, width = out.shape
    lanes = 2 * fields * depth
    half = lanes // 2
    slots = width // 2
    stacked = []
    for k in range(planes):
        if returned.shape[0] == planes:
            part = returned[k]
        else:
            devices, rows, _ = returned.shape
            rows = rows // planes
            part = returned[:, k * rows : (k + 1) * rows, :].reshape(slots, lanes)
        part = part.T
        stacked.append(jnp.concatenate([part[:half], part[half:]], axis=1))
    stacked = split(jnp.concatenate(stacked, axis=0))
    result = dot3(stacked, (table_high[...], table_low[...]))
    for k in range(planes):
        for f in range(fields):
            base = k * half + f * depth
            out[f, k] = result[base : base + depth]


def call(kernel, outs, in_specs, *args, scratch=(), flops=0, moved=0):
    return pl.pallas_call(
        kernel,
        out_shape=outs,
        in_specs=in_specs,
        out_specs=jax.tree.map(lambda _: VMEM, outs),
        scratch_shapes=scratch,
        compiler_params=PARAMS,
        cost_estimate=pl.CostEstimate(flops=flops, bytes_accessed=moved, transcendentals=0),
    )(*args)


def shards(grain_ids, jitter, class_table, chosen):
    planes, depth, width = grain_ids.shape
    devices = lax.axis_size("gx")
    total_x = planes * devices
    count = float(total_x * depth * width)
    slots = width // 2
    share = slots // devices
    lanes = 4 * depth
    up = [(i, (i + 1) % devices) for i in range(devices)]
    down = [(j, i) for i, j in up]
    aligned = share % 8 == 0

    def shape(*dims):
        return jax.ShapeDtypeStruct(dims, F32)

    plane = (GRAINS, depth, width)
    table = [jnp.asarray(part) for part in halves(y_table(width))]
    z_forward, z_inverse = z_tables(depth)
    z_parts = [jnp.asarray(part) for matrix in (z_forward, z_inverse) for part in halves(matrix)]
    x_parts = [jnp.asarray(part) for part in halves(np.concatenate(phases(total_x), axis=1))]

    two = (2, *plane)
    six = (GRAINS - 2, depth, width)
    small = [pltpu.SMEM((2,), jnp.int32), pltpu.SMEM((GRAINS, GRAINS), jnp.int32)]
    to_next, to_prev, c0, c2 = call(
        start_kernel,
        (shape(*two), shape(*two), shape(2, depth, width), shape(2, depth, width)),
        [ANY] * 3,
        chosen, jitter, grain_ids,
        scratch=[
            small[0],
            pltpu.VMEM(jitter.shape, jitter.dtype),
            pltpu.VMEM(grain_ids.shape, jnp.int32),
            pltpu.SemaphoreType.DMA((2 * planes + 1,)),
        ],
        flops=2**21, moved=2**22,
    )
    prev = lax.ppermute(to_next, "gx", up)
    nxt = lax.ppermute(to_prev, "gx", down)
    rates, middle, r0, r2 = call(
        inner_kernel,
        (shape(planes, *plane), shape(*plane), shape(*six), shape(*six)),
        [ANY] * 2 + [VMEM] * 2,
        chosen, class_table, to_next, to_prev,
        scratch=[*small, pltpu.SemaphoreType.DMA((2,))],
        flops=2**24, moved=2**22,
    )
    c0, c2, prev, nxt = lax.optimization_barrier((c0, c2, prev, nxt))
    prev3 = lax.ppermute(c0, "gx", up)
    next3 = lax.ppermute(c2, "gx", down)
    edge_rates, eta1, eta2 = call(
        near_kernel,
        (shape(*two), shape(4, *plane), shape(planes, *plane)),
        [ANY] + [VMEM] * 6,
        class_table, to_next, to_prev, prev, nxt, rates, middle,
        scratch=[small[1], pltpu.SemaphoreType.DMA((1,))],
        flops=2**25, moved=2**24,
    )
    r0, r2, prev3, next3 = lax.optimization_barrier((r0, r2, prev3, next3))
    prev3_rest = lax.ppermute(r0, "gx", up)
    next3_rest = lax.ppermute(r2, "gx", down)
    packed_shape = (devices, planes * share, lanes) if aligned else (planes, slots, lanes)
    packed, final = call(
        pair_kernel,
        (shape(*packed_shape), shape(2, planes, depth, width)),
        [ANY] * 2 + [VMEM] * 8 + [ANY] * 2,
        chosen, class_table, prev, nxt, prev3, next3, rates, edge_rates, eta1, eta2, *table,
        scratch=[
            *small,
            pltpu.VMEM(table[0].shape, BF16),
            pltpu.VMEM(table[1].shape, BF16),
            pltpu.VMEM((2, 2, depth, width), F32),
            pltpu.VMEM((planes * lanes, width), F32),
            pltpu.SemaphoreType.DMA((4,)),
        ],
        flops=2**28, moved=2**23,
    )
    if aligned:
        lines = lax.all_to_all(packed, "gx", split_axis=0, concat_axis=0, tiled=True)
    else:
        lines = lax.all_to_all(packed, "gx", split_axis=1, concat_axis=0, tiled=True)
    lines = lines.reshape(total_x * share, lanes)
    order_params = call(
        rest_kernel,
        shape(GRAINS, planes, depth, width),
        [ANY] * 2 + [VMEM] * 9,
        chosen, class_table, prev, nxt, prev3_rest, next3_rest, rates, edge_rates, eta1, eta2, final,
        scratch=[*small, pltpu.VMEM((2, *six), F32), pltpu.SemaphoreType.DMA((2,))],
        flops=2**26, moved=2**24,
    )
    lines, order_params = lax.optimization_barrier((lines, order_params))

    def lines_body(*refs):
        line_kernel(*refs, scale=1.0 / (count * count))

    back = call(
        lines_body,
        shape(total_x * share, lanes),
        [VMEM] * 7,
        lines, *z_parts, *x_parts,
        scratch=[
            pltpu.VMEM((total_x * share, lanes), F32),
            pltpu.VMEM((total_x * share, lanes), F32),
            pltpu.VMEM((2 * total_x, (share + 2) * lanes), F32),
        ],
        flops=2**28, moved=2**22,
    )
    back = back.reshape(devices, planes * share, lanes)
    returned = lax.all_to_all(back, "gx", split_axis=0, concat_axis=0, tiled=True)
    if not aligned:
        returned = returned.reshape(devices, planes, share, lanes).transpose(1, 0, 2, 3)
        returned = returned.reshape(planes, slots, lanes)
    correlation = call(
        finish_kernel,
        shape(2, planes, depth, width),
        [VMEM] * 3,
        returned, *table,
        flops=2**28, moved=2**22,
    )
    return (order_params, correlation)


def solution(mesh):
    in_specs = (P(("grp", "gx"), None, None), P(None, ("grp", "gx"), None, None), P(), P())
    out_specs = (P(None, ("grp", "gx"), None, None), P(None, ("grp", "gx"), None, None))
    return jax.shard_map(shards, mesh=mesh, in_specs=in_specs, out_specs=out_specs, check_vma=False)
```

```python
import math

import jax
import jax.numpy as jnp
import ml_dtypes
import numpy as np
from jax import lax
from jax.experimental import pallas as pl
from jax.experimental.pallas import tpu as pltpu
from jax.sharding import PartitionSpec as P

STEPS = 3
GRAINS = 8
F32 = jnp.float32
BF16 = jnp.bfloat16
VMEM = pl.BlockSpec(memory_space=pltpu.VMEM)
ANY = pl.BlockSpec(memory_space=pltpu.HBM)
MIB = 2**20


def halves(table):
    table = np.asarray(table, np.float32)
    high = table.astype(ml_dtypes.bfloat16)
    low = (table - high.astype(np.float32)).astype(ml_dtypes.bfloat16)
    return high, low


def phases(length, rows=None):
    index = np.arange(length)
    product = np.arange(length if rows is None else rows)[:, None] * index[None, :] % length
    angle = product * (2.0 * math.pi / length)
    return np.cos(angle), np.sin(angle)


def y_table(width):
    cos_y, sin_y = phases(width, width // 2)
    sin_y = -sin_y
    sin_y[0] = 1.0 - 2.0 * (np.arange(width) % 2)
    return np.concatenate([cos_y, sin_y], axis=0)


def z_tables(depth):
    cos_z, sin_z = phases(depth)
    two = np.eye(2)
    cos_z, sin_z = np.kron(two, cos_z), np.kron(two, sin_z)
    forward = np.block([[cos_z, -sin_z], [sin_z, cos_z]])
    half = 2 * depth
    forward_turned = np.concatenate([forward[:, half:], -forward[:, :half]], axis=1)
    inverse = np.block([[cos_z, sin_z], [-sin_z, cos_z]])
    inverse_turned = np.concatenate([-inverse[:, half:], inverse[:, :half]], axis=1)
    return (
        np.concatenate([forward, forward_turned], axis=1),
        np.concatenate([inverse, inverse_turned], axis=0),
    )


def split(value):
    high = value.astype(BF16)
    low = (value - high.astype(F32)).astype(BF16)
    return high, low


def dot3(left, right, contract=((1,), (0,))):
    def one(a, b):
        return lax.dot_general(a, b, (contract, ((), ())), preferred_element_type=F32)

    return one(left[0], right[0]) + (one(left[0], right[1]) + one(left[1], right[0]))


def fetch(pairs, semaphores):
    copies = [pltpu.make_async_copy(src, dst, semaphores.at[k]) for k, (src, dst) in enumerate(pairs)]
    for copy in copies:
        copy.start()
    return copies


def pair_of(chosen):
    first, second = chosen[0], chosen[1]
    second = jnp.where(second == first, lax.rem(first + 1, GRAINS), second)
    return first, second


def others_of(chosen):
    first, second = pair_of(chosen)
    low, high = jnp.minimum(first, second), jnp.maximum(first, second)

    def other(r):
        i = r + (r >= low).astype(jnp.int32)
        return i + (i >= high).astype(jnp.int32)

    return other


def start_kernel(chosen_any, jitter_any, ids_any, to_next, to_prev, c0, c2, chosen, jitter, grain_ids, semaphores):
    planes = grain_ids.shape[0]
    pairs = []
    for k in range(planes):
        pairs.append((jitter_any.at[:, k], jitter.at[:, k]))
        pairs.append((ids_any.at[k], grain_ids.at[k]))
    pairs.append((chosen_any, chosen))
    copies = fetch(pairs, semaphores)
    for plane, outs in enumerate(((to_prev.at[0],), (to_prev.at[1], to_next.at[0]), (to_next.at[1],))):
        copies[2 * plane].wait()
        copies[2 * plane + 1].wait()
        ids = grain_ids[plane]
        for i in range(GRAINS):
            base = jnp.where(ids == i, jnp.float32(0.6), jnp.float32(0.0))
            value = base + jitter[i, plane].astype(F32)
            for out in outs:
                out[i] = value
    copies[-1].wait()
    for k, i in enumerate(pair_of(chosen)):
        c0[k] = to_prev[0, i]
        c2[k] = to_next[1, i]


def grain_of(start):
    ids = jnp.where(start[1] > 0.55, 1, 0)
    for g in range(2, GRAINS):
        ids = jnp.where(start[g] > 0.55, g, ids)
    return ids


def rate(classes, ids, i):
    def level(g):
        return 0.12 * (0.4 + 0.2 * classes[g, i].astype(F32))

    value = jnp.full(ids.shape, level(0), F32)
    for g in range(1, GRAINS):
        value = jnp.where(ids == g, level(g), value)
    return value


def squares(state):
    total = state[0] * state[0]
    for i in range(1, GRAINS):
        total = total + state[i] * state[i]
    return 5.0 + 3.0 * total


def update(e, before, after, total, mobility):
    depth, width = e.shape
    near = before + after
    near = near + (pltpu.roll(e, 1, 0) + pltpu.roll(e, depth - 1, 0))
    near = near + (pltpu.roll(e, 1, 1) + pltpu.roll(e, width - 1, 1))
    return e + mobility * (near - e * (total - 2.0 * (e * e)))


def step_plane(center, before, after, mobility, out):
    total = squares(center)

    def body(i, carry):
        out[i] = update(center[i], before[i], after[i], total, mobility[i])
        return carry

    lax.fori_loop(0, GRAINS, body, 0)


def rates_plane(classes, start, out):
    ids = grain_of(start)

    def body(i, carry):
        out[i] = rate(classes, ids, i)
        return carry

    lax.fori_loop(0, GRAINS, body, 0)


def inner_kernel(chosen_any, classes_any, to_next, to_prev, rates, middle, r0, r2, chosen, classes, semaphores):
    copies = fetch(((chosen_any, chosen), (classes_any, classes)), semaphores)
    row = (to_prev.at[0], to_prev.at[1], to_next.at[1])
    for copy in copies:
        copy.wait()
    other = others_of(chosen)

    def body(r, carry):
        i = other(r)
        r0[r] = to_prev[0, i]
        r2[r] = to_next[1, i]
        return carry

    lax.fori_loop(0, GRAINS - 2, body, 0)
    for k in range(3):
        rates_plane(classes, row[k], rates.at[k])
    step_plane(row[1], row[0], row[2], rates.at[1], middle)


def near_kernel(
    classes_any, to_next, to_prev, prev, nxt, rates, middle, edge_rates, eta1, eta2, classes, semaphores
):
    copies = fetch(((classes_any, classes),), semaphores)
    p0, p1, p2 = to_prev.at[0], to_prev.at[1], to_next.at[1]
    step_plane(p0, prev.at[1], p1, rates.at[0], eta1.at[1])
    step_plane(p2, p1, nxt.at[0], rates.at[2], eta1.at[2])
    copies[0].wait()
    rates_plane(classes, prev.at[1], edge_rates.at[0])
    rates_plane(classes, nxt.at[0], edge_rates.at[1])
    step_plane(middle, eta1.at[1], eta1.at[2], rates.at[1], eta2.at[1])
    step_plane(prev.at[1], prev.at[0], p0, edge_rates.at[0], eta1.at[0])
    step_plane(nxt.at[0], p2, nxt.at[1], edge_rates.at[1], eta1.at[3])
    step_plane(eta1.at[1], eta1.at[0], middle, rates.at[0], eta2.at[0])
    step_plane(eta1.at[2], middle, eta1.at[3], rates.at[2], eta2.at[2])


def pair_kernel(
    chosen_any, classes_any, prev, nxt, prev3, next3, rates, edge_rates, eta1, eta2, high_any, low_any,
    packed, final, chosen, classes, high, low, edge, fields, semaphores,
):
    copies = fetch(
        ((chosen_any, chosen), (classes_any, classes), (high_any, high), (low_any, low)), semaphores
    )
    depth, width = final.shape[2:]
    totals = [squares(eta2.at[k]) for k in range(3)]
    copies[0].wait()
    copies[1].wait()
    pair = pair_of(chosen)
    for side, (far, mid, near) in enumerate(((prev3, prev.at[0], prev.at[1]), (next3, nxt.at[1], nxt.at[0]))):
        inner, neighbour = (0, 1) if side == 0 else (3, 2)
        ids = grain_of(mid)
        total0 = squares(mid)
        total1 = squares(eta1.at[inner])
        for k, i in enumerate(pair):
            first = update(mid[i], far[k], near[i], total0, rate(classes, ids, i))
            edge[side, k] = update(eta1[inner, i], first, eta1[neighbour, i], total1, edge_rates[side, i])
    repeated = chosen[1] == chosen[0]
    for k in range(3):
        values = []
        for f, i in enumerate(pair):
            before = edge[0, f] if k == 0 else eta2[k - 1, i]
            after = edge[1, f] if k == 2 else eta2[k + 1, i]
            value = update(eta2[k, i], before, after, totals[k], rates[k, i])
            final[f, k] = value
            values.append(value)
        values[1] = jnp.where(repeated, values[0], values[1])
        for f in range(2):
            base = k * 4 * depth + f * depth
            fields[base : base + depth] = values[f]
            fields[base + 2 * depth : base + 3 * depth] = values[f]
    copies[2].wait()
    copies[3].wait()
    full = dot3((high[...], low[...]), split(fields[...]), ((1,), (1,)))
    slots = width // 2
    lanes = 4 * depth
    real_lane = lax.broadcasted_iota(jnp.int32, (slots, lanes), 1) < 2 * depth
    for k in range(3):
        part = full[:, k * lanes : (k + 1) * lanes]
        part = jnp.where(real_lane, part[:slots], part[slots:])
        if packed.shape[0] == 3:
            packed[k] = part
        else:
            devices, rows, _ = packed.shape
            rows = rows // 3
            packed[:, k * rows : (k + 1) * rows, :] = part.reshape(devices, rows, lanes)


def rest_kernel(*refs):
    sources, out, targets, edge, semaphores = refs[:11], refs[11], refs[12:23], refs[23], refs[24]
    for copy in fetch(list(zip(sources, targets)), semaphores):
        copy.wait()
    chosen, classes, prev, nxt, prev3, next3, rates, edge_rates, eta1, eta2, final = targets
    other = others_of(chosen)
    rest = GRAINS - 2
    for side, (far, mid, near) in enumerate(((prev3, prev.at[0], prev.at[1]), (next3, nxt.at[1], nxt.at[0]))):
        inner, neighbour = (0, 1) if side == 0 else (3, 2)
        ids = grain_of(mid)
        total0 = squares(mid)
        total1 = squares(eta1.at[inner])

        def body(r, carry):
            i = other(r)
            first = update(mid[i], far[r], near[i], total0, rate(classes, ids, i))
            edge[side, r] = update(eta1[inner, i], first, eta1[neighbour, i], total1, edge_rates[side, i])
            return carry

        lax.fori_loop(0, rest, body, 0)
    for k in range(3):
        total = squares(eta2.at[k])

        def last(r, carry):
            i = other(r)
            before = edge[0, r] if k == 0 else eta2[k - 1, i]
            after = edge[1, r] if k == 2 else eta2[k + 1, i]
            out[i, k] = update(eta2[k, i], before, after, total, rates[k, i])
            return carry

        lax.fori_loop(0, rest, last, 0)
        for f, i in enumerate(pair_of(chosen)):
            out[i, k] = final[f, k]


def line_kernel(
    lines, zf_high, zf_low, zi_high, zi_low, xf_high, xf_low, out, r1, r2, gathered, scale
):
    rows, lanes = lines.shape
    total_x = xf_high.shape[0]
    slots = rows // total_x
    half = lanes // 2
    zf = (zf_high[...], zf_low[...])
    xf = (xf_high[...], xf_low[...])
    turned = dot3(split(lines[...]), zf)
    r1[...] = turned[:, :lanes]
    r2[...] = turned[:, lanes:]
    real_lane = lax.broadcasted_iota(jnp.int32, (total_x, lanes), 1) < half
    mixed = lines[pl.ds(0, total_x, stride=slots), :]
    pair = jnp.concatenate(
        [jnp.where(real_lane, mixed, 0.0), jnp.where(real_lane, pltpu.roll(mixed, half, 1), 0.0)], axis=0
    )
    pair = dot3(split(pair), zf)
    for j in range(slots):
        at = slice(j * lanes, (j + 1) * lanes)
        gathered[:total_x, at] = r1[pl.ds(j, total_x, stride=slots), :]
        gathered[total_x:, at] = r2[pl.ds(j, total_x, stride=slots), :]
    for j in range(2):
        at = slice((slots + j) * lanes, (slots + j + 1) * lanes)
        gathered[:total_x, at] = pair[j * total_x : (j + 1) * total_x, :lanes]
        gathered[total_x:, at] = pair[j * total_x : (j + 1) * total_x, lanes:]
    spectrum = dot3(xf, split(gathered[...]))

    def power(j):
        part = spectrum[:, j * lanes : (j + 1) * lanes]
        part = part * part
        return part + pltpu.roll(part, half, 1)

    first = lax.axis_index("gx") == 0
    lane = lax.broadcasted_iota(jnp.int32, (total_x, lanes), 1)
    line = lax.broadcasted_iota(jnp.int32, (total_x, lanes), 0)
    constant = jnp.logical_and(line == 0, jnp.logical_or(lane == 0, lane == half // 2))
    powers = []
    for j in range(slots):
        value = jnp.where(real_lane, power(j), 0.0) * (2.0 * scale)
        if j == 0:
            special = jnp.where(real_lane, power(slots), power(slots + 1)) * scale
            special = jnp.where(constant, 0.0, special)
            value = jnp.where(first, special, value)
        powers.append(value)
    powers = split(jnp.concatenate(powers, axis=1))
    cos_x = (xf[0][:, :total_x], xf[1][:, :total_x])
    sin_x = (xf[0][:, total_x:], xf[1][:, total_x:])
    for target, matrix in ((r1, cos_x), (r2, sin_x)):
        back = dot3(matrix, powers)
        for j in range(slots):
            target[pl.ds(j, total_x, stride=slots), :] = back[:, j * lanes : (j + 1) * lanes]
    zi = (zi_high[...], zi_low[...])
    out[...] = dot3(split(r1[...]), (zi[0][:lanes], zi[1][:lanes])) + dot3(
        split(r2[...]), (zi[0][lanes:], zi[1][lanes:])
    )


def finish_kernel(returned, high_any, low_any, out, high, low, semaphores):
    copies = fetch(((high_any, high), (low_any, low)), semaphores)
    fields, planes, depth, width = out.shape
    lanes = 2 * fields * depth
    half = lanes // 2
    slots = width // 2
    stacked = []
    for k in range(planes):
        if returned.shape[0] == planes:
            part = returned[k]
        else:
            devices, rows, _ = returned.shape
            rows = rows // planes
            part = returned[:, k * rows : (k + 1) * rows, :].reshape(slots, lanes)
        part = part.T
        stacked.append(jnp.concatenate([part[:half], part[half:]], axis=1))
    stacked = split(jnp.concatenate(stacked, axis=0))
    for copy in copies:
        copy.wait()
    result = dot3(stacked, (high[...], low[...]))
    for k in range(planes):
        for f in range(fields):
            base = k * half + f * depth
            out[f, k] = result[base : base + depth]


def call(kernel, outs, in_specs, *args, scratch=(), flops=0, moved=0, limit=12):
    return pl.pallas_call(
        kernel,
        out_shape=outs,
        in_specs=in_specs,
        out_specs=jax.tree.map(lambda _: VMEM, outs),
        scratch_shapes=scratch,
        compiler_params=pltpu.CompilerParams(vmem_limit_bytes=limit * MIB),
        cost_estimate=pl.CostEstimate(flops=flops, bytes_accessed=moved, transcendentals=0),
    )(*[pltpu.with_memory_space_constraint(a, pltpu.HBM) if b is ANY else a for a, b in zip(args, in_specs)])


def shards(grain_ids, jitter, class_table, chosen):
    planes, depth, width = grain_ids.shape
    devices = lax.axis_size("gx")
    total_x = planes * devices
    count = float(total_x * depth * width)
    slots = width // 2
    share = slots // devices
    lanes = 4 * depth
    up = [(i, (i + 1) % devices) for i in range(devices)]
    down = [(j, i) for i, j in up]
    aligned = share % 8 == 0

    def shape(*dims):
        return jax.ShapeDtypeStruct(dims, F32)

    plane = (GRAINS, depth, width)
    table = [jnp.asarray(part) for part in halves(y_table(width))]
    z_forward, z_inverse = z_tables(depth)
    z_parts = [jnp.asarray(part) for matrix in (z_forward, z_inverse) for part in halves(matrix)]
    x_parts = [jnp.asarray(part) for part in halves(np.concatenate(phases(total_x), axis=1))]

    two = (2, *plane)
    six = (GRAINS - 2, depth, width)
    small = [pltpu.SMEM((2,), jnp.int32), pltpu.SMEM((GRAINS, GRAINS), jnp.int32)]
    to_next, to_prev, c0, c2 = call(
        start_kernel,
        (shape(*two), shape(*two), shape(2, depth, width), shape(2, depth, width)),
        [ANY] * 3,
        chosen, jitter, grain_ids,
        scratch=[
            small[0],
            pltpu.VMEM(jitter.shape, jitter.dtype),
            pltpu.VMEM(grain_ids.shape, jnp.int32),
            pltpu.SemaphoreType.DMA((2 * planes + 1,)),
        ],
        flops=2**21, moved=2**22,
    )
    prev = lax.ppermute(to_next, "gx", up)
    nxt = lax.ppermute(to_prev, "gx", down)
    rates, middle, r0, r2 = call(
        inner_kernel,
        (shape(planes, *plane), shape(*plane), shape(*six), shape(*six)),
        [ANY] * 2 + [VMEM] * 2,
        chosen, class_table, to_next, to_prev,
        scratch=[*small, pltpu.SemaphoreType.DMA((2,))],
        flops=2**24, moved=2**22,
    )
    c0, c2, r0, r2, prev, nxt = lax.optimization_barrier((c0, c2, r0, r2, prev, nxt))
    prev3 = lax.ppermute(c0, "gx", up)
    next3 = lax.ppermute(c2, "gx", down)
    edge_rates, eta1, eta2 = call(
        near_kernel,
        (shape(*two), shape(4, *plane), shape(planes, *plane)),
        [ANY] + [VMEM] * 6,
        class_table, to_next, to_prev, prev, nxt, rates, middle,
        scratch=[small[1], pltpu.SemaphoreType.DMA((1,))],
        flops=2**25, moved=2**24,
    )
    prev3_rest = lax.ppermute(r0, "gx", up)
    next3_rest = lax.ppermute(r2, "gx", down)
    packed_shape = (devices, planes * share, lanes) if aligned else (planes, slots, lanes)
    packed, final = call(
        pair_kernel,
        (shape(*packed_shape), shape(2, planes, depth, width)),
        [ANY] * 2 + [VMEM] * 8 + [ANY] * 2,
        chosen, class_table, prev, nxt, prev3, next3, rates, edge_rates, eta1, eta2, *table,
        scratch=[
            *small,
            pltpu.VMEM(table[0].shape, BF16),
            pltpu.VMEM(table[1].shape, BF16),
            pltpu.VMEM((2, 2, depth, width), F32),
            pltpu.VMEM((planes * lanes, width), F32),
            pltpu.SemaphoreType.DMA((4,)),
        ],
        flops=2**28, moved=2**23,
    )
    packed, prev3_rest, next3_rest = lax.optimization_barrier((packed, prev3_rest, next3_rest))
    if aligned:
        lines = lax.all_to_all(packed, "gx", split_axis=0, concat_axis=0, tiled=True)
    else:
        lines = lax.all_to_all(packed, "gx", split_axis=1, concat_axis=0, tiled=True)
    lines = lines.reshape(total_x * share, lanes)
    def lines_body(*refs):
        line_kernel(*refs, scale=1.0 / (count * count))

    back = call(
        lines_body,
        shape(total_x * share, lanes),
        [VMEM] * 7,
        lines, *z_parts, *x_parts,
        scratch=[
            pltpu.VMEM((total_x * share, lanes), F32),
            pltpu.VMEM((total_x * share, lanes), F32),
            pltpu.VMEM((2 * total_x, (share + 2) * lanes), F32),
        ],
        flops=2**28, moved=2**22,
    )
    back = back.reshape(devices, planes * share, lanes)
    returned = lax.all_to_all(back, "gx", split_axis=0, concat_axis=0, tiled=True)
    if not aligned:
        returned = returned.reshape(devices, planes, share, lanes).transpose(1, 0, 2, 3)
        returned = returned.reshape(planes, slots, lanes)
    late = (chosen, class_table, prev, nxt, prev3_rest, next3_rest, rates, edge_rates, eta1, eta2, final)
    late, _ = lax.optimization_barrier((late, back))
    order_params = call(
        rest_kernel,
        shape(GRAINS, planes, depth, width),
        [ANY] * 11,
        *late,
        scratch=[
            *small,
            *[pltpu.VMEM(value.shape, F32) for value in late[2:]],
            pltpu.VMEM((2, *six), F32),
            pltpu.SemaphoreType.DMA((11,)),
        ],
        flops=2**26, moved=2**24, limit=24,
    )
    correlation = call(
        finish_kernel,
        shape(2, planes, depth, width),
        [VMEM] + [ANY] * 2,
        returned, *table,
        scratch=[
            pltpu.VMEM(table[0].shape, BF16),
            pltpu.VMEM(table[1].shape, BF16),
            pltpu.SemaphoreType.DMA((2,)),
        ],
        flops=2**28, moved=2**22,
    )
    return (order_params, correlation)


def solution(mesh):
    in_specs = (P(("grp", "gx"), None, None), P(None, ("grp", "gx"), None, None), P(), P())
    out_specs = (P(None, ("grp", "gx"), None, None), P(None, ("grp", "gx"), None, None))
    return jax.shard_map(shards, mesh=mesh, in_specs=in_specs, out_specs=out_specs, check_vma=False)
```

```python
import math

import jax
import jax.numpy as jnp
import ml_dtypes
import numpy as np
from jax import lax
from jax.experimental import pallas as pl
from jax.experimental.pallas import tpu as pltpu
from jax.sharding import PartitionSpec as P

STEPS = 3
GRAINS = 8
F32 = jnp.float32
BF16 = jnp.bfloat16
VMEM = pl.BlockSpec(memory_space=pltpu.VMEM)
ANY = pl.BlockSpec(memory_space=pltpu.HBM)
MIB = 2**20


def halves(table):
    table = np.asarray(table, np.float32)
    high = table.astype(ml_dtypes.bfloat16)
    low = (table - high.astype(np.float32)).astype(ml_dtypes.bfloat16)
    return high, low


def phases(length, rows=None):
    index = np.arange(length)
    product = np.arange(length if rows is None else rows)[:, None] * index[None, :] % length
    angle = product * (2.0 * math.pi / length)
    return np.cos(angle), np.sin(angle)


def y_table(width):
    cos_y, sin_y = phases(width, width // 2)
    sin_y = -sin_y
    sin_y[0] = 1.0 - 2.0 * (np.arange(width) % 2)
    return np.concatenate([cos_y, sin_y], axis=0)


def z_tables(depth):
    cos_z, sin_z = phases(depth)
    two = np.eye(2)
    cos_z, sin_z = np.kron(two, cos_z), np.kron(two, sin_z)
    forward = np.block([[cos_z, -sin_z], [sin_z, cos_z]])
    half = 2 * depth
    forward_turned = np.concatenate([forward[:, half:], -forward[:, :half]], axis=1)
    inverse = np.block([[cos_z, sin_z], [-sin_z, cos_z]])
    inverse_turned = np.concatenate([-inverse[:, half:], inverse[:, :half]], axis=1)
    return (
        np.concatenate([forward, forward_turned], axis=1),
        np.concatenate([inverse, inverse_turned], axis=0),
    )


def split(value):
    high = value.astype(BF16)
    low = (value - high.astype(F32)).astype(BF16)
    return high, low


def dot3(left, right, contract=((1,), (0,))):
    def one(a, b):
        return lax.dot_general(a, b, (contract, ((), ())), preferred_element_type=F32)

    return one(left[0], right[0]) + (one(left[0], right[1]) + one(left[1], right[0]))


def fetch(pairs, semaphores):
    copies = [pltpu.make_async_copy(src, dst, semaphores.at[k]) for k, (src, dst) in enumerate(pairs)]
    for copy in copies:
        copy.start()
    return copies


def pair_of(chosen):
    first, second = chosen[0], chosen[1]
    second = jnp.where(second == first, lax.rem(first + 1, GRAINS), second)
    return first, second


def others_of(chosen):
    first, second = pair_of(chosen)
    low, high = jnp.minimum(first, second), jnp.maximum(first, second)

    def other(r):
        i = jnp.where(r >= low, r + 1, r)
        return jnp.where(i >= high, i + 1, i)

    return other


def start_kernel(chosen_any, jitter_any, ids_any, p0, p2, up2, down2, chosen, jitter, grain_ids, semaphores):
    planes = grain_ids.shape[0]
    pairs = []
    for k in (2, 0, 1):
        pairs.append((jitter_any.at[:, k], jitter.at[:, k]))
        pairs.append((ids_any.at[k], grain_ids.at[k]))
    pairs.append((chosen_any, chosen))
    copies = fetch(pairs, semaphores)
    for step, (plane, outs) in enumerate(((2, (p2,)), (0, (p0,)), (1, (up2, down2)))):
        copies[2 * step].wait()
        copies[2 * step + 1].wait()
        ids = grain_ids[plane]
        for i in range(GRAINS):
            base = jnp.where(ids == i, jnp.float32(0.6), jnp.float32(0.0))
            value = base + jitter[i, plane].astype(F32)
            for out in outs:
                out[i] = value
    copies[-1].wait()
    for k, i in enumerate(pair_of(chosen)):
        up2[GRAINS + k] = p0[i]
        down2[GRAINS + k] = p2[i]

def grain_of(start):
    ids = jnp.where(start[1] > 0.55, 1, 0)
    for g in range(2, GRAINS):
        ids = jnp.where(start[g] > 0.55, g, ids)
    return ids


def rate(classes, ids, i):
    def level(g):
        return 0.12 * (0.4 + 0.2 * classes[g, i].astype(F32))

    value = jnp.full(ids.shape, level(0), F32)
    for g in range(1, GRAINS):
        value = jnp.where(ids == g, level(g), value)
    return value


def squares(state):
    total = state[0] * state[0]
    for i in range(1, GRAINS):
        total = total + state[i] * state[i]
    return 5.0 + 3.0 * total


def update(e, before, after, total, mobility):
    depth, width = e.shape
    near = before + after
    near = near + (pltpu.roll(e, 1, 0) + pltpu.roll(e, depth - 1, 0))
    near = near + (pltpu.roll(e, 1, 1) + pltpu.roll(e, width - 1, 1))
    return e + mobility * (near - e * (total - 2.0 * (e * e)))


def step_plane(center, before, after, mobility, out):
    total = squares(center)

    def body(i, carry):
        out[i] = update(center[i], before[i], after[i], total, mobility[i])
        return carry

    lax.fori_loop(0, GRAINS, body, 0)


def rates_plane(classes, start, out):
    ids = grain_of(start)

    def body(i, carry):
        out[i] = rate(classes, ids, i)
        return carry

    lax.fori_loop(0, GRAINS, body, 0)


def inner_kernel(chosen_any, classes_any, p0, p2, up2, rates, middle, r0, r2, chosen, classes, semaphores):
    copies = fetch(((chosen_any, chosen), (classes_any, classes)), semaphores)
    row = (p0, up2, p2)
    for copy in copies:
        copy.wait()
    other = others_of(chosen)
    for r in range(GRAINS - 2):
        i = other(r)
        r0[r] = p0[i]
        r2[r] = p2[i]
    for k in range(3):
        rates_plane(classes, row[k], rates.at[k])
    step_plane(up2, p0, p2, rates.at[1], middle)


def near_kernel(
    classes_any, p0, p2, up2, prev1, next1, rates, middle, edge_rates, inner1, middle2, classes, semaphores
):
    copies = fetch(((classes_any, classes),), semaphores)
    step_plane(p0, prev1, up2, rates.at[0], inner1.at[0])
    step_plane(p2, up2, next1, rates.at[2], inner1.at[1])
    copies[0].wait()
    rates_plane(classes, prev1, edge_rates.at[0])
    rates_plane(classes, next1, edge_rates.at[1])
    step_plane(middle, inner1.at[0], inner1.at[1], rates.at[1], middle2)


def pair_kernel(
    chosen_any, classes_any, p0, p2, prev1, next1, prev2, next2, rates, edge_rates, middle, inner1, middle2,
    high_any, low_any, packed, outer1, side2, final_any, chosen, classes, high, low, edge, fields, final, semaphores,
):
    copies = fetch(
        ((chosen_any, chosen), (classes_any, classes), (high_any, high), (low_any, low)), semaphores
    )
    step_plane(prev1, prev2, p0, edge_rates.at[0], outer1.at[0])
    step_plane(next1, p2, next2, edge_rates.at[1], outer1.at[1])
    step_plane(inner1.at[0], outer1.at[0], middle, rates.at[0], side2.at[0])
    step_plane(inner1.at[1], middle, outer1.at[1], rates.at[2], side2.at[1])
    eta2 = (side2.at[0], middle2, side2.at[1])
    depth, width = final.shape[2:]
    totals = [squares(state) for state in eta2]
    copies[0].wait()
    copies[1].wait()
    pair = pair_of(chosen)
    for side, (mid, near) in enumerate(((prev2, prev1), (next2, next1))):
        ids = grain_of(mid)
        total0 = squares(mid)
        total1 = squares(outer1.at[side])
        for k, i in enumerate(pair):
            first = update(mid[i], mid[GRAINS + k], near[i], total0, rate(classes, ids, i))
            edge[side, k] = update(outer1[side, i], first, inner1[side, i], total1, edge_rates[side, i])
    repeated = chosen[1] == chosen[0]
    for k in range(3):
        values = []
        for f, i in enumerate(pair):
            before = edge[0, f] if k == 0 else eta2[k - 1][i]
            after = edge[1, f] if k == 2 else eta2[k + 1][i]
            value = update(eta2[k][i], before, after, totals[k], rates[k, i])
            final[f, k] = value
            values.append(value)
        values[1] = jnp.where(repeated, values[0], values[1])
        for f in range(2):
            base = k * 4 * depth + f * depth
            fields[base : base + depth] = values[f]
            fields[base + 2 * depth : base + 3 * depth] = values[f]
    out_copy = pltpu.make_async_copy(final, final_any, semaphores.at[4])
    out_copy.start()
    copies[2].wait()
    copies[3].wait()
    full = dot3((high[...], low[...]), split(fields[...]), ((1,), (1,)))
    slots = width // 2
    lanes = 4 * depth
    real_lane = lax.broadcasted_iota(jnp.int32, (slots, lanes), 1) < 2 * depth
    for k in range(3):
        part = full[:, k * lanes : (k + 1) * lanes]
        part = jnp.where(real_lane, part[:slots], part[slots:])
        if packed.shape[0] == 3:
            packed[k] = part
        else:
            devices, rows, _ = packed.shape
            rows = rows // 3
            packed[:, k * rows : (k + 1) * rows, :] = part.reshape(devices, rows, lanes)
    out_copy.wait()


def rest_kernel(*refs):
    count = (len(refs) - 3) // 2
    sources, out, targets = refs[:count], refs[count], refs[count + 1 : 2 * count + 1]
    edge, semaphores = refs[-2:]
    copies = fetch(list(zip(sources, targets)), semaphores)
    (
        chosen, classes, prev2, prev1, prev3, next2, next1, next3, outer1, inner1, edge_rates,
        middle2, side2, rates, final,
    ) = targets
    for copy in copies[:11]:
        copy.wait()
    other = others_of(chosen)
    rest = GRAINS - 2
    for side, (far, mid, near) in enumerate(((prev3, prev2, prev1), (next3, next2, next1))):
        ids = grain_of(mid)
        total0 = squares(mid)
        total1 = squares(outer1.at[side])

        def body(r, carry):
            i = other(r)
            first = update(mid[i], far[r], near[i], total0, rate(classes, ids, i))
            edge[side, r] = update(outer1[side, i], first, inner1[side, i], total1, edge_rates[side, i])
            return carry

        lax.fori_loop(0, rest, body, 0)
    for copy in copies[11:]:
        copy.wait()
    eta2 = (side2.at[0], middle2, side2.at[1])
    for k in range(3):
        total = squares(eta2[k])

        def last(r, carry):
            i = other(r)
            before = edge[0, r] if k == 0 else eta2[k - 1][i]
            after = edge[1, r] if k == 2 else eta2[k + 1][i]
            out[i, k] = update(eta2[k][i], before, after, total, rates[k, i])
            return carry

        lax.fori_loop(0, rest, last, 0)
        for f, i in enumerate(pair_of(chosen)):
            out[i, k] = final[f, k]


def line_kernel(
    lines, zf_high, zf_low, zi_high, zi_low, xf_high, xf_low, out, r1, r2, gathered, scale
):
    rows, lanes = lines.shape
    total_x = xf_high.shape[0]
    slots = rows // total_x
    half = lanes // 2
    zf = (zf_high[...], zf_low[...])
    xf = (xf_high[...], xf_low[...])
    turned = dot3(split(lines[...]), zf)
    r1[...] = turned[:, :lanes]
    r2[...] = turned[:, lanes:]
    real_lane = lax.broadcasted_iota(jnp.int32, (total_x, lanes), 1) < half
    mixed = lines[pl.ds(0, total_x, stride=slots), :]
    pair = jnp.concatenate(
        [jnp.where(real_lane, mixed, 0.0), jnp.where(real_lane, pltpu.roll(mixed, half, 1), 0.0)], axis=0
    )
    pair = dot3(split(pair), zf)
    for j in range(slots):
        at = slice(j * lanes, (j + 1) * lanes)
        gathered[:total_x, at] = r1[pl.ds(j, total_x, stride=slots), :]
        gathered[total_x:, at] = r2[pl.ds(j, total_x, stride=slots), :]
    for j in range(2):
        at = slice((slots + j) * lanes, (slots + j + 1) * lanes)
        gathered[:total_x, at] = pair[j * total_x : (j + 1) * total_x, :lanes]
        gathered[total_x:, at] = pair[j * total_x : (j + 1) * total_x, lanes:]
    spectrum = dot3(xf, split(gathered[...]))

    def power(j):
        part = spectrum[:, j * lanes : (j + 1) * lanes]
        part = part * part
        return part + pltpu.roll(part, half, 1)

    first = lax.axis_index("gx") == 0
    lane = lax.broadcasted_iota(jnp.int32, (total_x, lanes), 1)
    line = lax.broadcasted_iota(jnp.int32, (total_x, lanes), 0)
    constant = jnp.logical_and(line == 0, jnp.logical_or(lane == 0, lane == half // 2))
    powers = []
    for j in range(slots):
        value = jnp.where(real_lane, power(j), 0.0) * (2.0 * scale)
        if j == 0:
            special = jnp.where(real_lane, power(slots), power(slots + 1)) * scale
            special = jnp.where(constant, 0.0, special)
            value = jnp.where(first, special, value)
        powers.append(value)
    powers = split(jnp.concatenate(powers, axis=1))
    cos_x = (xf[0][:, :total_x], xf[1][:, :total_x])
    sin_x = (xf[0][:, total_x:], xf[1][:, total_x:])
    for target, matrix in ((r1, cos_x), (r2, sin_x)):
        back = dot3(matrix, powers)
        for j in range(slots):
            target[pl.ds(j, total_x, stride=slots), :] = back[:, j * lanes : (j + 1) * lanes]
    zi = (zi_high[...], zi_low[...])
    out[...] = dot3(split(r1[...]), (zi[0][:lanes], zi[1][:lanes])) + dot3(
        split(r2[...]), (zi[0][lanes:], zi[1][lanes:])
    )


def finish_kernel(returned, high_any, low_any, out, high, low, semaphores):
    copies = fetch(((high_any, high), (low_any, low)), semaphores)
    fields, planes, depth, width = out.shape
    lanes = 2 * fields * depth
    half = lanes // 2
    slots = width // 2
    stacked = []
    for k in range(planes):
        if returned.shape[0] == planes:
            part = returned[k]
        else:
            devices, rows, _ = returned.shape
            rows = rows // planes
            part = returned[:, k * rows : (k + 1) * rows, :].reshape(slots, lanes)
        part = part.T
        stacked.append(jnp.concatenate([part[:half], part[half:]], axis=1))
    stacked = split(jnp.concatenate(stacked, axis=0))
    for copy in copies:
        copy.wait()
    result = dot3(stacked, (high[...], low[...]))
    for k in range(planes):
        for f in range(fields):
            base = k * half + f * depth
            out[f, k] = result[base : base + depth]


def call(kernel, outs, in_specs, *args, scratch=(), flops=0, moved=0, limit=12, out_specs=None):
    return pl.pallas_call(
        kernel,
        out_shape=outs,
        in_specs=in_specs,
        out_specs=out_specs or jax.tree.map(lambda _: VMEM, outs),
        scratch_shapes=scratch,
        compiler_params=pltpu.CompilerParams(vmem_limit_bytes=limit * MIB),
        cost_estimate=pl.CostEstimate(flops=flops, bytes_accessed=moved, transcendentals=0),
    )(*[pltpu.with_memory_space_constraint(a, pltpu.HBM) if b is ANY else a for a, b in zip(args, in_specs)])


def shards(grain_ids, jitter, class_table, chosen):
    planes, depth, width = grain_ids.shape
    devices = lax.axis_size("gx")
    total_x = planes * devices
    count = float(total_x * depth * width)
    slots = width // 2
    share = slots // devices
    lanes = 4 * depth
    up = [(i, (i + 1) % devices) for i in range(devices)]
    down = [(j, i) for i, j in up]
    aligned = share % 8 == 0

    def shape(*dims):
        return jax.ShapeDtypeStruct(dims, F32)

    plane = (GRAINS, depth, width)
    table = [jnp.asarray(part) for part in halves(y_table(width))]
    z_forward, z_inverse = z_tables(depth)
    z_parts = [jnp.asarray(part) for matrix in (z_forward, z_inverse) for part in halves(matrix)]
    x_parts = [jnp.asarray(part) for part in halves(np.concatenate(phases(total_x), axis=1))]

    two = (2, *plane)
    six = (GRAINS - 2, depth, width)
    small = [pltpu.SMEM((2,), jnp.int32), pltpu.SMEM((GRAINS, GRAINS), jnp.int32)]
    ten = (GRAINS + 2, depth, width)
    p0, p2, up2, down2 = call(
        start_kernel,
        (shape(*plane), shape(*plane), shape(*ten), shape(*ten)),
        [ANY] * 3,
        chosen, jitter, grain_ids,
        scratch=[
            small[0],
            pltpu.VMEM(jitter.shape, jitter.dtype),
            pltpu.VMEM(grain_ids.shape, jnp.int32),
            pltpu.SemaphoreType.DMA((2 * planes + 1,)),
        ],
        flops=2**21, moved=2**22,
    )
    prev1 = lax.ppermute(p2, "gx", up)
    next1 = lax.ppermute(p0, "gx", down)
    prev2 = lax.ppermute(up2, "gx", up)
    next2 = lax.ppermute(down2, "gx", down)
    rates, middle, r0, r2 = call(
        inner_kernel,
        (shape(planes, *plane), shape(*plane), shape(*six), shape(*six)),
        [ANY] * 2 + [VMEM] * 3,
        chosen, class_table, p0, p2, up2,
        scratch=[*small, pltpu.SemaphoreType.DMA((2,))],
        flops=2**24, moved=2**22,
    )
    prev3 = lax.ppermute(r0, "gx", up)
    next3 = lax.ppermute(r2, "gx", down)
    edge_rates, inner1, middle2 = call(
        near_kernel,
        (shape(*two), shape(*two), shape(*plane)),
        [ANY] + [VMEM] * 7,
        class_table, p0, p2, up2, prev1, next1, rates, middle,
        scratch=[small[1], pltpu.SemaphoreType.DMA((1,))],
        flops=2**25, moved=2**24,
    )
    packed_shape = (devices, planes * share, lanes) if aligned else (planes, slots, lanes)
    packed, outer1, side2, final = call(
        pair_kernel,
        (shape(*packed_shape), shape(*two), shape(*two), shape(2, planes, depth, width)),
        [ANY] * 2 + [VMEM] * 11 + [ANY] * 2,
        chosen, class_table, p0, p2, prev1, next1, prev2, next2, rates, edge_rates, middle, inner1, middle2, *table,
        scratch=[
            *small,
            pltpu.VMEM(table[0].shape, BF16),
            pltpu.VMEM(table[1].shape, BF16),
            pltpu.VMEM((2, 2, depth, width), F32),
            pltpu.VMEM((planes * lanes, width), F32),
            pltpu.VMEM((2, planes, depth, width), F32),
            pltpu.SemaphoreType.DMA((5,)),
        ],
        out_specs=(VMEM, VMEM, VMEM, ANY),
        flops=2**28, moved=2**23,
    )
    packed, prev3, next3 = lax.optimization_barrier((packed, prev3, next3))
    if aligned:
        lines = lax.all_to_all(packed, "gx", split_axis=0, concat_axis=0, tiled=True)
    else:
        lines = lax.all_to_all(packed, "gx", split_axis=1, concat_axis=0, tiled=True)
    lines = lines.reshape(total_x * share, lanes)
    def lines_body(*refs):
        line_kernel(*refs, scale=1.0 / (count * count))

    back = call(
        lines_body,
        shape(total_x * share, lanes),
        [VMEM] * 7,
        lines, *z_parts, *x_parts,
        scratch=[
            pltpu.VMEM((total_x * share, lanes), F32),
            pltpu.VMEM((total_x * share, lanes), F32),
            pltpu.VMEM((2 * total_x, (share + 2) * lanes), F32),
        ],
        flops=2**28, moved=2**22,
    )
    back = back.reshape(devices, planes * share, lanes)
    returned = lax.all_to_all(back, "gx", split_axis=0, concat_axis=0, tiled=True)
    if not aligned:
        returned = returned.reshape(devices, planes, share, lanes).transpose(1, 0, 2, 3)
        returned = returned.reshape(planes, slots, lanes)
    late = (
        chosen, class_table, prev2, prev1, prev3, next2, next1, next3, outer1, inner1, edge_rates,
        middle2, side2, rates, final,
    )
    late, _ = lax.optimization_barrier((late, back))
    order_params = call(
        rest_kernel,
        shape(GRAINS, planes, depth, width),
        [ANY] * len(late),
        *late,
        scratch=[
            *small,
            *[pltpu.VMEM(value.shape, F32) for value in late[2:]],
            pltpu.VMEM((2, *six), F32),
            pltpu.SemaphoreType.DMA((len(late),)),
        ],
        flops=2**26, moved=2**24, limit=24,
    )
    correlation = call(
        finish_kernel,
        shape(2, planes, depth, width),
        [VMEM] + [ANY] * 2,
        returned, *table,
        scratch=[
            pltpu.VMEM(table[0].shape, BF16),
            pltpu.VMEM(table[1].shape, BF16),
            pltpu.SemaphoreType.DMA((2,)),
        ],
        flops=2**28, moved=2**22,
    )
    return (order_params, correlation)


def solution(mesh):
    in_specs = (P(("grp", "gx"), None, None), P(None, ("grp", "gx"), None, None), P(), P())
    out_specs = (P(None, ("grp", "gx"), None, None), P(None, ("grp", "gx"), None, None))
    return jax.shard_map(shards, mesh=mesh, in_specs=in_specs, out_specs=out_specs, check_vma=False)
```

```python
import math

import jax
import jax.numpy as jnp
import ml_dtypes
import numpy as np
from jax import lax
from jax.experimental import pallas as pl
from jax.experimental.pallas import tpu as pltpu
from jax.sharding import PartitionSpec as P

STEPS = 3
GRAINS = 8
F32 = jnp.float32
BF16 = jnp.bfloat16
VMEM = pl.BlockSpec(memory_space=pltpu.VMEM)
ANY = pl.BlockSpec(memory_space=pltpu.HBM)
MIB = 2**20


def halves(table):
    table = np.asarray(table, np.float32)
    high = table.astype(ml_dtypes.bfloat16)
    low = (table - high.astype(np.float32)).astype(ml_dtypes.bfloat16)
    return high, low


def phases(length, rows=None):
    index = np.arange(length)
    product = np.arange(length if rows is None else rows)[:, None] * index[None, :] % length
    angle = product * (2.0 * math.pi / length)
    return np.cos(angle), np.sin(angle)


def y_table(width):
    cos_y, sin_y = phases(width, width // 2)
    sin_y = -sin_y
    sin_y[0] = 1.0 - 2.0 * (np.arange(width) % 2)
    return np.concatenate([cos_y, sin_y], axis=0)


def z_tables(depth):
    cos_z, sin_z = phases(depth)
    two = np.eye(2)
    cos_z, sin_z = np.kron(two, cos_z), np.kron(two, sin_z)
    forward = np.block([[cos_z, -sin_z], [sin_z, cos_z]])
    half = 2 * depth
    forward_turned = np.concatenate([forward[:, half:], -forward[:, :half]], axis=1)
    inverse = np.block([[cos_z, sin_z], [-sin_z, cos_z]])
    inverse_turned = np.concatenate([-inverse[:, half:], inverse[:, :half]], axis=1)
    return (
        np.concatenate([forward, forward_turned], axis=1),
        np.concatenate([inverse, inverse_turned], axis=0),
    )


def split(value):
    high = value.astype(BF16)
    low = (value - high.astype(F32)).astype(BF16)
    return high, low


def dot3(left, right, contract=((1,), (0,))):
    def one(a, b):
        return lax.dot_general(a, b, (contract, ((), ())), preferred_element_type=F32)

    return one(left[0], right[0]) + (one(left[0], right[1]) + one(left[1], right[0]))


def fetch(pairs, semaphores):
    copies = [pltpu.make_async_copy(src, dst, semaphores.at[k]) for k, (src, dst) in enumerate(pairs)]
    for copy in copies:
        copy.start()
    return copies


def pair_of(chosen):
    first, second = chosen[0], chosen[1]
    second = jnp.where(second == first, lax.rem(first + 1, GRAINS), second)
    return first, second


def others_of(chosen):
    first, second = pair_of(chosen)
    low, high = jnp.minimum(first, second), jnp.maximum(first, second)

    def other(r):
        i = jnp.where(r >= low, r + 1, r)
        return jnp.where(i >= high, i + 1, i)

    return other


def start_kernel(chosen_any, jitter_any, ids_any, p0, p2, up2, down2, chosen, jitter, grain_ids, semaphores):
    planes = grain_ids.shape[0]
    pairs = []
    for k in (2, 0, 1):
        pairs.append((jitter_any.at[:, k], jitter.at[:, k]))
        pairs.append((ids_any.at[k], grain_ids.at[k]))
    pairs.append((chosen_any, chosen))
    copies = fetch(pairs, semaphores)
    for step, (plane, outs) in enumerate(((2, (p2,)), (0, (p0,)), (1, (up2, down2)))):
        copies[2 * step].wait()
        copies[2 * step + 1].wait()
        ids = grain_ids[plane]
        for i in range(GRAINS):
            base = jnp.where(ids == i, jnp.float32(0.6), jnp.float32(0.0))
            value = base + jitter[i, plane].astype(F32)
            for out in outs:
                out[i] = value
    copies[-1].wait()
    for k, i in enumerate(pair_of(chosen)):
        up2[GRAINS + k] = p0[i]
        down2[GRAINS + k] = p2[i]

def grain_of(start):
    ids = jnp.where(start[1] > 0.55, 1, 0)
    for g in range(2, GRAINS):
        ids = jnp.where(start[g] > 0.55, g, ids)
    return ids


def rate(classes, ids, i):
    def level(g):
        return 0.12 * (0.4 + 0.2 * classes[g, i].astype(F32))

    value = jnp.full(ids.shape, level(0), F32)
    for g in range(1, GRAINS):
        value = jnp.where(ids == g, level(g), value)
    return value


def squares(state):
    total = state[0] * state[0]
    for i in range(1, GRAINS):
        total = total + state[i] * state[i]
    return 5.0 + 3.0 * total


def update(e, before, after, total, mobility):
    depth, width = e.shape
    near = before + after
    near = near + (pltpu.roll(e, 1, 0) + pltpu.roll(e, depth - 1, 0))
    near = near + (pltpu.roll(e, 1, 1) + pltpu.roll(e, width - 1, 1))
    return e + mobility * (near - e * (total - 2.0 * (e * e)))


def step_plane(center, before, after, mobility, out):
    total = squares(center)
    for i in range(GRAINS):
        out[i] = update(center[i], before[i], after[i], total, mobility[i])


def rates_plane(classes, start, out):
    ids = grain_of(start)
    for i in range(GRAINS):
        out[i] = rate(classes, ids, i)


def inner_kernel(chosen_any, classes_any, p0, p2, up2, rates, middle, r0, r2, chosen, classes, semaphores):
    copies = fetch(((chosen_any, chosen), (classes_any, classes)), semaphores)
    row = (p0, up2, p2)
    for copy in copies:
        copy.wait()
    other = others_of(chosen)
    for r in range(GRAINS - 2):
        i = other(r)
        r0[r] = p0[i]
        r2[r] = p2[i]
    for k in range(3):
        rates_plane(classes, row[k], rates.at[k])
    step_plane(up2, p0, p2, rates.at[1], middle)


def near_kernel(
    classes_any, p0, p2, up2, prev1, next1, rates, middle, edge_rates, inner1, middle2, classes, semaphores
):
    copies = fetch(((classes_any, classes),), semaphores)
    step_plane(p0, prev1, up2, rates.at[0], inner1.at[0])
    step_plane(p2, up2, next1, rates.at[2], inner1.at[1])
    copies[0].wait()
    rates_plane(classes, prev1, edge_rates.at[0])
    rates_plane(classes, next1, edge_rates.at[1])
    step_plane(middle, inner1.at[0], inner1.at[1], rates.at[1], middle2)


def pair_kernel(
    chosen_any, classes_any, p0, p2, prev1, next1, prev2, next2, rates, edge_rates, middle, inner1, middle2,
    high_any, low_any, packed, outer1, side2, final_any, chosen, classes, high, low, edge, fields, final, semaphores,
):
    copies = fetch(
        ((chosen_any, chosen), (classes_any, classes), (high_any, high), (low_any, low)), semaphores
    )
    step_plane(prev1, prev2, p0, edge_rates.at[0], outer1.at[0])
    step_plane(next1, p2, next2, edge_rates.at[1], outer1.at[1])
    step_plane(inner1.at[0], outer1.at[0], middle, rates.at[0], side2.at[0])
    step_plane(inner1.at[1], middle, outer1.at[1], rates.at[2], side2.at[1])
    eta2 = (side2.at[0], middle2, side2.at[1])
    depth, width = final.shape[2:]
    totals = [squares(state) for state in eta2]
    copies[0].wait()
    copies[1].wait()
    pair = pair_of(chosen)
    for side, (mid, near) in enumerate(((prev2, prev1), (next2, next1))):
        ids = grain_of(mid)
        total0 = squares(mid)
        total1 = squares(outer1.at[side])
        for k, i in enumerate(pair):
            first = update(mid[i], mid[GRAINS + k], near[i], total0, rate(classes, ids, i))
            edge[side, k] = update(outer1[side, i], first, inner1[side, i], total1, edge_rates[side, i])
    repeated = chosen[1] == chosen[0]
    for k in range(3):
        values = []
        for f, i in enumerate(pair):
            before = edge[0, f] if k == 0 else eta2[k - 1][i]
            after = edge[1, f] if k == 2 else eta2[k + 1][i]
            value = update(eta2[k][i], before, after, totals[k], rates[k, i])
            final[f, k] = value
            values.append(value)
        values[1] = jnp.where(repeated, values[0], values[1])
        for f in range(2):
            base = k * 4 * depth + f * depth
            fields[base : base + depth] = values[f]
            fields[base + 2 * depth : base + 3 * depth] = values[f]
    out_copy = pltpu.make_async_copy(final, final_any, semaphores.at[4])
    out_copy.start()
    copies[2].wait()
    copies[3].wait()
    full = dot3((high[...], low[...]), split(fields[...]), ((1,), (1,)))
    slots = width // 2
    lanes = 4 * depth
    real_lane = lax.broadcasted_iota(jnp.int32, (slots, lanes), 1) < 2 * depth
    for k in range(3):
        part = full[:, k * lanes : (k + 1) * lanes]
        part = jnp.where(real_lane, part[:slots], part[slots:])
        if packed.shape[0] == 3:
            packed[k] = part
        else:
            devices, rows, _ = packed.shape
            rows = rows // 3
            packed[:, k * rows : (k + 1) * rows, :] = part.reshape(devices, rows, lanes)
    out_copy.wait()


def rest_kernel(*refs):
    count = (len(refs) - 3) // 2
    sources, out, targets = refs[:count], refs[count], refs[count + 1 : 2 * count + 1]
    edge, semaphores = refs[-2:]
    copies = fetch(list(zip(sources, targets)), semaphores)
    (
        chosen, classes, prev2, prev1, prev3, next2, next1, next3, outer1, inner1, edge_rates,
        middle2, side2, rates, final,
    ) = targets
    for copy in copies[:11]:
        copy.wait()
    other = others_of(chosen)
    rest = GRAINS - 2
    for side, (far, mid, near) in enumerate(((prev3, prev2, prev1), (next3, next2, next1))):
        ids = grain_of(mid)
        total0 = squares(mid)
        total1 = squares(outer1.at[side])
        for r in range(rest):
            i = other(r)
            first = update(mid[i], far[r], near[i], total0, rate(classes, ids, i))
            edge[side, r] = update(outer1[side, i], first, inner1[side, i], total1, edge_rates[side, i])
    for copy in copies[11:]:
        copy.wait()
    eta2 = (side2.at[0], middle2, side2.at[1])
    for k in range(3):
        total = squares(eta2[k])
        for r in range(rest):
            i = other(r)
            before = edge[0, r] if k == 0 else eta2[k - 1][i]
            after = edge[1, r] if k == 2 else eta2[k + 1][i]
            out[i, k] = update(eta2[k][i], before, after, total, rates[k, i])
        for f, i in enumerate(pair_of(chosen)):
            out[i, k] = final[f, k]


def line_kernel(
    lines, zf_high, zf_low, zi_high, zi_low, xf_high, xf_low, out, r1, r2, gathered, scale
):
    rows, lanes = lines.shape
    total_x = xf_high.shape[0]
    slots = rows // total_x
    half = lanes // 2
    zf = (zf_high[...], zf_low[...])
    xf = (xf_high[...], xf_low[...])
    turned = dot3(split(lines[...]), zf)
    r1[...] = turned[:, :lanes]
    r2[...] = turned[:, lanes:]
    real_lane = lax.broadcasted_iota(jnp.int32, (total_x, lanes), 1) < half
    mixed = lines[pl.ds(0, total_x, stride=slots), :]
    pair = jnp.concatenate(
        [jnp.where(real_lane, mixed, 0.0), jnp.where(real_lane, pltpu.roll(mixed, half, 1), 0.0)], axis=0
    )
    pair = dot3(split(pair), zf)
    for j in range(slots):
        at = slice(j * lanes, (j + 1) * lanes)
        gathered[:total_x, at] = r1[pl.ds(j, total_x, stride=slots), :]
        gathered[total_x:, at] = r2[pl.ds(j, total_x, stride=slots), :]
    for j in range(2):
        at = slice((slots + j) * lanes, (slots + j + 1) * lanes)
        gathered[:total_x, at] = pair[j * total_x : (j + 1) * total_x, :lanes]
        gathered[total_x:, at] = pair[j * total_x : (j + 1) * total_x, lanes:]
    spectrum = dot3(xf, split(gathered[...]))

    def power(j):
        part = spectrum[:, j * lanes : (j + 1) * lanes]
        part = part * part
        return part + pltpu.roll(part, half, 1)

    first = lax.axis_index("gx") == 0
    lane = lax.broadcasted_iota(jnp.int32, (total_x, lanes), 1)
    line = lax.broadcasted_iota(jnp.int32, (total_x, lanes), 0)
    constant = jnp.logical_and(line == 0, jnp.logical_or(lane == 0, lane == half // 2))
    powers = []
    for j in range(slots):
        value = jnp.where(real_lane, power(j), 0.0) * (2.0 * scale)
        if j == 0:
            special = jnp.where(real_lane, power(slots), power(slots + 1)) * scale
            special = jnp.where(constant, 0.0, special)
            value = jnp.where(first, special, value)
        powers.append(value)
    powers = split(jnp.concatenate(powers, axis=1))
    cos_x = (xf[0][:, :total_x], xf[1][:, :total_x])
    sin_x = (xf[0][:, total_x:], xf[1][:, total_x:])
    for target, matrix in ((r1, cos_x), (r2, sin_x)):
        back = dot3(matrix, powers)
        for j in range(slots):
            target[pl.ds(j, total_x, stride=slots), :] = back[:, j * lanes : (j + 1) * lanes]
    zi = (zi_high[...], zi_low[...])
    out[...] = dot3(split(r1[...]), (zi[0][:lanes], zi[1][:lanes])) + dot3(
        split(r2[...]), (zi[0][lanes:], zi[1][lanes:])
    )


def finish_kernel(returned, high_any, low_any, out, high, low, semaphores):
    copies = fetch(((high_any, high), (low_any, low)), semaphores)
    fields, planes, depth, width = out.shape
    lanes = 2 * fields * depth
    half = lanes // 2
    slots = width // 2
    stacked = []
    for k in range(planes):
        if returned.shape[0] == planes:
            part = returned[k]
        else:
            devices, rows, _ = returned.shape
            rows = rows // planes
            part = returned[:, k * rows : (k + 1) * rows, :].reshape(slots, lanes)
        part = part.T
        stacked.append(jnp.concatenate([part[:half], part[half:]], axis=1))
    stacked = split(jnp.concatenate(stacked, axis=0))
    for copy in copies:
        copy.wait()
    result = dot3(stacked, (high[...], low[...]))
    for k in range(planes):
        for f in range(fields):
            base = k * half + f * depth
            out[f, k] = result[base : base + depth]


def call(kernel, outs, in_specs, *args, scratch=(), flops=0, moved=0, limit=12, out_specs=None):
    return pl.pallas_call(
        kernel,
        out_shape=outs,
        in_specs=in_specs,
        out_specs=out_specs or jax.tree.map(lambda _: VMEM, outs),
        scratch_shapes=scratch,
        compiler_params=pltpu.CompilerParams(vmem_limit_bytes=limit * MIB),
        cost_estimate=pl.CostEstimate(flops=flops, bytes_accessed=moved, transcendentals=0),
    )(*[pltpu.with_memory_space_constraint(a, pltpu.HBM) if b is ANY else a for a, b in zip(args, in_specs)])


def shards(grain_ids, jitter, class_table, chosen):
    planes, depth, width = grain_ids.shape
    devices = lax.axis_size("gx")
    total_x = planes * devices
    count = float(total_x * depth * width)
    slots = width // 2
    share = slots // devices
    lanes = 4 * depth
    up = [(i, (i + 1) % devices) for i in range(devices)]
    down = [(j, i) for i, j in up]
    aligned = share % 8 == 0

    def shape(*dims):
        return jax.ShapeDtypeStruct(dims, F32)

    plane = (GRAINS, depth, width)
    table = [jnp.asarray(part) for part in halves(y_table(width))]
    z_forward, z_inverse = z_tables(depth)
    z_parts = [jnp.asarray(part) for matrix in (z_forward, z_inverse) for part in halves(matrix)]
    x_parts = [jnp.asarray(part) for part in halves(np.concatenate(phases(total_x), axis=1))]

    two = (2, *plane)
    six = (GRAINS - 2, depth, width)
    small = [pltpu.SMEM((2,), jnp.int32), pltpu.SMEM((GRAINS, GRAINS), jnp.int32)]
    ten = (GRAINS + 2, depth, width)
    p0, p2, up2, down2 = call(
        start_kernel,
        (shape(*plane), shape(*plane), shape(*ten), shape(*ten)),
        [ANY] * 3,
        chosen, jitter, grain_ids,
        scratch=[
            small[0],
            pltpu.VMEM(jitter.shape, jitter.dtype),
            pltpu.VMEM(grain_ids.shape, jnp.int32),
            pltpu.SemaphoreType.DMA((2 * planes + 1,)),
        ],
        flops=2**21, moved=2**22,
    )
    prev1 = lax.ppermute(p2, "gx", up)
    next1 = lax.ppermute(p0, "gx", down)
    prev2 = lax.ppermute(up2, "gx", up)
    next2 = lax.ppermute(down2, "gx", down)
    rates, middle, r0, r2 = call(
        inner_kernel,
        (shape(planes, *plane), shape(*plane), shape(*six), shape(*six)),
        [ANY] * 2 + [VMEM] * 3,
        chosen, class_table, p0, p2, up2,
        scratch=[*small, pltpu.SemaphoreType.DMA((2,))],
        flops=2**24, moved=2**22,
    )
    r0, r2, prev1, next1 = lax.optimization_barrier((r0, r2, prev1, next1))
    prev3 = lax.ppermute(r0, "gx", up)
    next3 = lax.ppermute(r2, "gx", down)
    edge_rates, inner1, middle2 = call(
        near_kernel,
        (shape(*two), shape(*two), shape(*plane)),
        [ANY] + [VMEM] * 7,
        class_table, p0, p2, up2, prev1, next1, rates, middle,
        scratch=[small[1], pltpu.SemaphoreType.DMA((1,))],
        flops=2**25, moved=2**24,
    )
    packed_shape = (devices, planes * share, lanes) if aligned else (planes, slots, lanes)
    packed, outer1, side2, final = call(
        pair_kernel,
        (shape(*packed_shape), shape(*two), shape(*two), shape(2, planes, depth, width)),
        [ANY] * 2 + [VMEM] * 11 + [ANY] * 2,
        chosen, class_table, p0, p2, prev1, next1, prev2, next2, rates, edge_rates, middle, inner1, middle2, *table,
        scratch=[
            *small,
            pltpu.VMEM(table[0].shape, BF16),
            pltpu.VMEM(table[1].shape, BF16),
            pltpu.VMEM((2, 2, depth, width), F32),
            pltpu.VMEM((planes * lanes, width), F32),
            pltpu.VMEM((2, planes, depth, width), F32),
            pltpu.SemaphoreType.DMA((5,)),
        ],
        out_specs=(VMEM, VMEM, VMEM, ANY),
        flops=2**28, moved=2**23,
    )
    packed, prev3, next3 = lax.optimization_barrier((packed, prev3, next3))
    if aligned:
        lines = lax.all_to_all(packed, "gx", split_axis=0, concat_axis=0, tiled=True)
    else:
        lines = lax.all_to_all(packed, "gx", split_axis=1, concat_axis=0, tiled=True)
    lines = lines.reshape(total_x * share, lanes)
    def lines_body(*refs):
        line_kernel(*refs, scale=1.0 / (count * count))

    back = call(
        lines_body,
        shape(total_x * share, lanes),
        [VMEM] * 7,
        lines, *z_parts, *x_parts,
        scratch=[
            pltpu.VMEM((total_x * share, lanes), F32),
            pltpu.VMEM((total_x * share, lanes), F32),
            pltpu.VMEM((2 * total_x, (share + 2) * lanes), F32),
        ],
        flops=2**28, moved=2**22,
    )
    back = back.reshape(devices, planes * share, lanes)
    returned = lax.all_to_all(back, "gx", split_axis=0, concat_axis=0, tiled=True)
    if not aligned:
        returned = returned.reshape(devices, planes, share, lanes).transpose(1, 0, 2, 3)
        returned = returned.reshape(planes, slots, lanes)
    late = (
        chosen, class_table, prev2, prev1, prev3, next2, next1, next3, outer1, inner1, edge_rates,
        middle2, side2, rates, final,
    )
    late, _ = lax.optimization_barrier((late, back))
    order_params = call(
        rest_kernel,
        shape(GRAINS, planes, depth, width),
        [ANY] * len(late),
        *late,
        scratch=[
            *small,
            *[pltpu.VMEM(value.shape, F32) for value in late[2:]],
            pltpu.VMEM((2, *six), F32),
            pltpu.SemaphoreType.DMA((len(late),)),
        ],
        flops=2**26, moved=2**24, limit=24,
    )
    correlation = call(
        finish_kernel,
        shape(2, planes, depth, width),
        [VMEM] + [ANY] * 2,
        returned, *table,
        scratch=[
            pltpu.VMEM(table[0].shape, BF16),
            pltpu.VMEM(table[1].shape, BF16),
            pltpu.SemaphoreType.DMA((2,)),
        ],
        flops=2**28, moved=2**22,
    )
    return (order_params, correlation)


def solution(mesh):
    in_specs = (P(("grp", "gx"), None, None), P(None, ("grp", "gx"), None, None), P(), P())
    out_specs = (P(None, ("grp", "gx"), None, None), P(None, ("grp", "gx"), None, None))
    return jax.shard_map(shards, mesh=mesh, in_specs=in_specs, out_specs=out_specs, check_vma=False)
```

```python
import math

import jax
import jax.numpy as jnp
import ml_dtypes
import numpy as np
from jax import lax
from jax.experimental import pallas as pl
from jax.experimental.pallas import tpu as pltpu
from jax.sharding import PartitionSpec as P

STEPS = 3
GRAINS = 8
F32 = jnp.float32
BF16 = jnp.bfloat16
VMEM = pl.BlockSpec(memory_space=pltpu.VMEM)
ANY = pl.BlockSpec(memory_space=pltpu.HBM)
MIB = 2**20


def halves(table):
    table = np.asarray(table, np.float32)
    high = table.astype(ml_dtypes.bfloat16)
    low = (table - high.astype(np.float32)).astype(ml_dtypes.bfloat16)
    return high, low


def phases(length, rows=None):
    index = np.arange(length)
    product = np.arange(length if rows is None else rows)[:, None] * index[None, :] % length
    angle = product * (2.0 * math.pi / length)
    return np.cos(angle), np.sin(angle)


def y_table(width):
    cos_y, sin_y = phases(width, width // 2)
    sin_y = -sin_y
    sin_y[0] = 1.0 - 2.0 * (np.arange(width) % 2)
    return np.concatenate([cos_y, sin_y], axis=0)


def z_tables(depth):
    cos_z, sin_z = phases(depth)
    two = np.eye(2)
    cos_z, sin_z = np.kron(two, cos_z), np.kron(two, sin_z)
    forward = np.block([[cos_z, -sin_z], [sin_z, cos_z]])
    half = 2 * depth
    forward_turned = np.concatenate([forward[:, half:], -forward[:, :half]], axis=1)
    inverse = np.block([[cos_z, sin_z], [-sin_z, cos_z]])
    inverse_turned = np.concatenate([-inverse[:, half:], inverse[:, :half]], axis=1)
    return (
        np.concatenate([forward, forward_turned], axis=0),
        np.concatenate([inverse, inverse_turned], axis=0),
    )


def split(value):
    high = value.astype(BF16)
    low = (value - high.astype(F32)).astype(BF16)
    return high, low


def dot3(left, right, contract=((1,), (0,))):
    def one(a, b):
        return lax.dot_general(a, b, (contract, ((), ())), preferred_element_type=F32)

    return one(left[0], right[0]) + (one(left[0], right[1]) + one(left[1], right[0]))


def fetch(pairs, semaphores):
    copies = [pltpu.make_async_copy(src, dst, semaphores.at[k]) for k, (src, dst) in enumerate(pairs)]
    for copy in copies:
        copy.start()
    return copies


def pair_of(chosen):
    first, second = chosen[0], chosen[1]
    second = jnp.where(second == first, lax.rem(first + 1, GRAINS), second)
    return first, second


def others_of(chosen):
    first, second = pair_of(chosen)
    low, high = jnp.minimum(first, second), jnp.maximum(first, second)

    def other(r):
        i = jnp.where(r >= low, r + 1, r)
        return jnp.where(i >= high, i + 1, i)

    return other


def start_kernel(chosen_any, jitter_any, ids_any, p0, p2, up2, down2, chosen, jitter, grain_ids, semaphores):
    planes = grain_ids.shape[0]
    pairs = []
    for k in (2, 0, 1):
        pairs.append((jitter_any.at[:, k], jitter.at[:, k]))
        pairs.append((ids_any.at[k], grain_ids.at[k]))
    pairs.append((chosen_any, chosen))
    copies = fetch(pairs, semaphores)
    for step, (plane, outs) in enumerate(((2, (p2,)), (0, (p0,)), (1, (up2, down2)))):
        copies[2 * step].wait()
        copies[2 * step + 1].wait()
        ids = grain_ids[plane]
        for i in range(GRAINS):
            base = jnp.where(ids == i, jnp.float32(0.6), jnp.float32(0.0))
            value = base + jitter[i, plane].astype(F32)
            for out in outs:
                out[i] = value
    copies[-1].wait()
    for k, i in enumerate(pair_of(chosen)):
        up2[GRAINS + k] = p0[i]
        down2[GRAINS + k] = p2[i]

def grain_of(start):
    ids = jnp.where(start[1] > 0.55, 1, 0)
    for g in range(2, GRAINS):
        ids = jnp.where(start[g] > 0.55, g, ids)
    return ids


def rate(classes, ids, i):
    def level(g):
        return 0.12 * (0.4 + 0.2 * classes[g, i].astype(F32))

    value = jnp.full(ids.shape, level(0), F32)
    for g in range(1, GRAINS):
        value = jnp.where(ids == g, level(g), value)
    return value


def squares(state):
    total = state[0] * state[0]
    for i in range(1, GRAINS):
        total = total + state[i] * state[i]
    return 5.0 + 3.0 * total


def update(e, before, after, total, mobility):
    depth, width = e.shape
    near = before + after
    near = near + (pltpu.roll(e, 1, 0) + pltpu.roll(e, depth - 1, 0))
    near = near + (pltpu.roll(e, 1, 1) + pltpu.roll(e, width - 1, 1))
    return e + mobility * (near - e * (total - 2.0 * (e * e)))


def step_plane(center, before, after, mobility, out):
    total = squares(center)
    for i in range(GRAINS):
        out[i] = update(center[i], before[i], after[i], total, mobility[i])


def rates_plane(classes, start, out):
    ids = grain_of(start)
    for i in range(GRAINS):
        out[i] = rate(classes, ids, i)


def inner_kernel(chosen_any, classes_any, p0, p2, up2, rates, middle, r0, r2, chosen, classes, semaphores):
    copies = fetch(((chosen_any, chosen), (classes_any, classes)), semaphores)
    row = (p0, up2, p2)
    for copy in copies:
        copy.wait()
    other = others_of(chosen)
    for r in range(GRAINS - 2):
        i = other(r)
        r0[r] = p0[i]
        r2[r] = p2[i]
    for k in range(3):
        rates_plane(classes, row[k], rates.at[k])
    step_plane(up2, p0, p2, rates.at[1], middle)


def groups(ref, count, base=0):
    return [ref.at[pl.ds(base + k * GRAINS, GRAINS)] for k in range(count)]


def near_kernel(classes_any, p0, p2, up2, prev1, next1, rates, middle, near_out, classes, semaphores):
    edge0, edge1, inner0, inner2, middle2 = groups(near_out, 5)
    copies = fetch(((classes_any, classes),), semaphores)
    step_plane(p0, prev1, up2, rates.at[0], inner0)
    step_plane(p2, up2, next1, rates.at[2], inner2)
    copies[0].wait()
    rates_plane(classes, prev1, edge0)
    rates_plane(classes, next1, edge1)
    step_plane(middle, inner0, inner2, rates.at[1], middle2)


def pair_kernel(
    chosen_any, classes_any, p0, p2, prev1, next1, prev2, next2, rates, middle, near_out, high_any, low_any,
    packed, late, chosen, classes, high, low, edge, fields, semaphores,
):
    copies = fetch(
        ((chosen_any, chosen), (classes_any, classes), (high_any, high), (low_any, low)), semaphores
    )
    near_state = groups(near_out, 5)
    edge_rates, inner1, middle2 = near_state[:2], near_state[2:4], near_state[4]
    late_state = groups(late, 4)
    outer1, side2 = late_state[:2], late_state[2:]
    step_plane(prev1, prev2, p0, edge_rates[0], outer1[0])
    step_plane(next1, p2, next2, edge_rates[1], outer1[1])
    step_plane(inner1[0], outer1[0], middle, rates.at[0], side2[0])
    step_plane(inner1[1], middle, outer1[1], rates.at[2], side2[1])
    eta2 = (side2[0], middle2, side2[1])
    depth, width = late.shape[1:]
    totals = [squares(state) for state in eta2]
    copies[0].wait()
    copies[1].wait()
    pair = pair_of(chosen)
    for side, (mid, near) in enumerate(((prev2, prev1), (next2, next1))):
        ids = grain_of(mid)
        total0 = squares(mid)
        total1 = squares(outer1[side])
        for k, i in enumerate(pair):
            first = update(mid[i], mid[GRAINS + k], near[i], total0, rate(classes, ids, i))
            edge[side, k] = update(outer1[side][i], first, inner1[side][i], total1, edge_rates[side][i])
    repeated = chosen[1] == chosen[0]
    for k in range(3):
        values = []
        for f, i in enumerate(pair):
            before = edge[0, f] if k == 0 else eta2[k - 1][i]
            after = edge[1, f] if k == 2 else eta2[k + 1][i]
            value = update(eta2[k][i], before, after, totals[k], rates[k, i])
            late[4 * GRAINS + 3 * f + k] = value
            values.append(value)
        values[1] = jnp.where(repeated, values[0], values[1])
        for f in range(2):
            base = k * 2 * depth + f * depth
            fields[base : base + depth] = values[f]
    copies[2].wait()
    copies[3].wait()
    full = dot3((high[...], low[...]), split(fields[...]), ((1,), (1,)))
    slots = width // 2
    lanes = 4 * depth
    half = lanes // 2
    real_lane = lax.broadcasted_iota(jnp.int32, (slots, lanes), 1) < half
    for k in range(3):
        at = slice(k // 2 * lanes, k // 2 * lanes + lanes)
        cosine, sine = full[:slots, at], full[slots:, at]
        if k % 2:
            cosine = pltpu.roll(cosine, half, 1)
        else:
            sine = pltpu.roll(sine, half, 1)
        part = jnp.where(real_lane, cosine, sine)
        if packed.shape[0] == 3:
            packed[k] = part
        else:
            devices, rows, _ = packed.shape
            rows = rows // 3
            packed[:, k * rows : (k + 1) * rows, :] = part.reshape(devices, rows, lanes)


def rest_kernel(*refs):
    count = (len(refs) - 3) // 2
    sources, out, targets = refs[:count], refs[count], refs[count + 1 : 2 * count + 1]
    edge, semaphores = refs[-2:]
    copies = fetch(list(zip(sources, targets)), semaphores)
    chosen, classes, prev2, prev1, prev3, next2, next1, next3, near_out, late, rates = targets
    near_state = groups(near_out, 5)
    edge_rates, inner1, middle2 = near_state[:2], near_state[2:4], near_state[4]
    late_state = groups(late, 4)
    outer1, side2 = late_state[:2], late_state[2:]
    for copy in copies[:10]:
        copy.wait()
    other = others_of(chosen)
    rest = GRAINS - 2
    for side, (far, mid, near) in enumerate(((prev3, prev2, prev1), (next3, next2, next1))):
        ids = grain_of(mid)
        total0 = squares(mid)
        total1 = squares(outer1[side])
        for r in range(rest):
            i = other(r)
            first = update(mid[i], far[r], near[i], total0, rate(classes, ids, i))
            edge[side, r] = update(outer1[side][i], first, inner1[side][i], total1, edge_rates[side][i])
    copies[10].wait()
    eta2 = (side2[0], middle2, side2[1])
    for k in range(3):
        total = squares(eta2[k])
        for r in range(rest):
            i = other(r)
            before = edge[0, r] if k == 0 else eta2[k - 1][i]
            after = edge[1, r] if k == 2 else eta2[k + 1][i]
            out[i, k] = update(eta2[k][i], before, after, total, rates[k, i])
        for f, i in enumerate(pair_of(chosen)):
            out[i, k] = late[4 * GRAINS + 3 * f + k]


def line_kernel(lines, z_forward, z_inverse, x_both, out, wide, tall, scale):
    rows, lanes = lines.shape
    total_x = wide.shape[0] // 3
    slots = rows // total_x
    half = lanes // 2

    def over_x(pieces):
        for j, piece in enumerate(pieces):
            at = slice(j * lanes, (j + 1) * lanes)
            high, low = split(piece)
            wide[:total_x, at] = high
            wide[total_x : 2 * total_x, at] = low
            wide[2 * total_x :, at] = high
        both = jnp.dot(x_both[...], wide[...], preferred_element_type=F32)
        return both[:total_x], both[total_x:]

    def put(row, even, odd):
        at = slice(row * total_x, (row + 1) * total_x)
        for base, value in ((0, even), (lanes, odd)):
            high, low = split(value)
            tall[0, at, base : base + lanes] = high
            tall[1, at, base : base + lanes] = low

    real_lane = lax.broadcasted_iota(jnp.int32, (total_x, lanes), 1) < half
    even, odd = over_x([lines[pl.ds(j, total_x, stride=slots), :] for j in range(slots)])
    for j in range(slots):
        at = slice(j * lanes, (j + 1) * lanes)
        put(j, even[:, at], odd[:, at])
    first_even, first_odd = even[:, :lanes], odd[:, :lanes]
    put(slots, jnp.where(real_lane, first_even, 0.0), jnp.where(real_lane, first_odd, 0.0))
    put(
        slots + 1,
        jnp.where(real_lane, pltpu.roll(first_even, half, 1), 0.0),
        jnp.where(real_lane, pltpu.roll(first_odd, half, 1), 0.0),
    )
    spectrum = dot3((tall[0], tall[1]), (z_forward[0], z_forward[1]))
    spectrum = spectrum * spectrum
    spectrum = spectrum + pltpu.roll(spectrum, half, 1)

    def power(j):
        return spectrum[j * total_x : (j + 1) * total_x]

    first = lax.axis_index("gx") == 0
    lane = lax.broadcasted_iota(jnp.int32, (total_x, lanes), 1)
    line = lax.broadcasted_iota(jnp.int32, (total_x, lanes), 0)
    constant = jnp.logical_and(line == 0, jnp.logical_or(lane == 0, lane == half // 2))
    powers = []
    for j in range(slots):
        value = jnp.where(real_lane, power(j), 0.0) * (2.0 * scale)
        if j == 0:
            special = jnp.where(real_lane, power(slots), power(slots + 1)) * scale
            special = jnp.where(constant, 0.0, special)
            value = jnp.where(first, special, value)
        powers.append(value)
    even, odd = over_x(powers)
    for j in range(slots):
        at = slice(j * lanes, (j + 1) * lanes)
        put(j, even[:, at], odd[:, at])
    back = dot3((tall[0, :rows], tall[1, :rows]), (z_inverse[0], z_inverse[1]))
    for j in range(slots):
        out[pl.ds(j, total_x, stride=slots), :] = back[j * total_x : (j + 1) * total_x]


def finish_kernel(returned, high, low, out):
    fields, planes, depth, width = out.shape
    lanes = 2 * fields * depth
    half = lanes // 2
    slots = width // 2
    stacked = []
    for k in range(planes):
        if returned.shape[0] == planes:
            part = returned[k]
        else:
            devices, rows, _ = returned.shape
            rows = rows // planes
            part = returned[:, k * rows : (k + 1) * rows, :].reshape(slots, lanes)
        part = part.T
        stacked.append(jnp.concatenate([part[:half], part[half:]], axis=1))
    stacked = split(jnp.concatenate(stacked, axis=0))
    result = dot3(stacked, (high[...], low[...]))
    for k in range(planes):
        for f in range(fields):
            base = k * half + f * depth
            out[f, k] = result[base : base + depth]


def call(kernel, outs, in_specs, *args, scratch=(), flops=0, moved=0, limit=12):
    args = [pltpu.with_memory_space_constraint(a, pltpu.HBM) if b is ANY else a for a, b in zip(args, in_specs)]
    return pl.pallas_call(
        kernel,
        out_shape=outs,
        in_specs=in_specs,
        out_specs=jax.tree.map(lambda _: VMEM, outs),
        scratch_shapes=scratch,
        compiler_params=pltpu.CompilerParams(vmem_limit_bytes=limit * MIB),
        cost_estimate=pl.CostEstimate(flops=flops, bytes_accessed=moved, transcendentals=0),
    )(*args)


def shards(grain_ids, jitter, class_table, chosen):
    planes, depth, width = grain_ids.shape
    devices = lax.axis_size("gx")
    total_x = planes * devices
    count = float(total_x * depth * width)
    slots = width // 2
    share = slots // devices
    lanes = 4 * depth
    up = [(i, (i + 1) % devices) for i in range(devices)]
    down = [(j, i) for i, j in up]
    aligned = share % 8 == 0

    def shape(*dims):
        return jax.ShapeDtypeStruct(dims, F32)

    plane = (GRAINS, depth, width)
    table = [jnp.asarray(part) for part in halves(y_table(width))]
    z_forward, z_inverse = z_tables(depth)
    z_parts = [jnp.asarray(np.stack(halves(matrix))) for matrix in (z_forward, z_inverse)]
    x_high, x_low = halves(np.concatenate(phases(total_x), axis=0))
    x_both = jnp.asarray(np.concatenate([x_high, x_high, x_low], axis=1))

    two = (2, *plane)
    six = (GRAINS - 2, depth, width)
    small = [pltpu.SMEM((2,), jnp.int32), pltpu.SMEM((GRAINS, GRAINS), jnp.int32)]
    ten = (GRAINS + 2, depth, width)
    p0, p2, up2, down2 = call(
        start_kernel,
        (shape(*plane), shape(*plane), shape(*ten), shape(*ten)),
        [ANY] * 3,
        chosen, jitter, grain_ids,
        scratch=[
            small[0],
            pltpu.VMEM(jitter.shape, jitter.dtype),
            pltpu.VMEM(grain_ids.shape, jnp.int32),
            pltpu.SemaphoreType.DMA((2 * planes + 1,)),
        ],
        flops=2**21, moved=2**22,
    )
    prev1 = lax.ppermute(p2, "gx", up)
    next1 = lax.ppermute(p0, "gx", down)
    prev2 = lax.ppermute(up2, "gx", up)
    next2 = lax.ppermute(down2, "gx", down)
    rates, middle, r0, r2 = call(
        inner_kernel,
        (shape(planes, *plane), shape(*plane), shape(*six), shape(*six)),
        [ANY] * 2 + [VMEM] * 3,
        chosen, class_table, p0, p2, up2,
        scratch=[*small, pltpu.SemaphoreType.DMA((2,))],
        flops=2**24, moved=2**22,
    )
    r0, r2, prev1, next1 = lax.optimization_barrier((r0, r2, prev1, next1))
    prev3 = lax.ppermute(r0, "gx", up)
    next3 = lax.ppermute(r2, "gx", down)
    near_out = call(
        near_kernel,
        shape(5 * GRAINS, depth, width),
        [ANY] + [VMEM] * 7,
        class_table, p0, p2, up2, prev1, next1, rates, middle,
        scratch=[small[1], pltpu.SemaphoreType.DMA((1,))],
        flops=2**25, moved=2**24,
    )
    packed_shape = (devices, planes * share, lanes) if aligned else (planes, slots, lanes)
    packed, late_out = call(
        pair_kernel,
        (shape(*packed_shape), shape(4 * GRAINS + 2 * planes, depth, width)),
        [ANY] * 2 + [VMEM] * 9 + [ANY] * 2,
        chosen, class_table, p0, p2, prev1, next1, prev2, next2, rates, middle, near_out, *table,
        scratch=[
            *small,
            pltpu.VMEM(table[0].shape, BF16),
            pltpu.VMEM(table[1].shape, BF16),
            pltpu.VMEM((2, 2, depth, width), F32),
            pltpu.VMEM(((planes + 1) // 2 * lanes, width), F32),
            pltpu.SemaphoreType.DMA((4,)),
        ],
        flops=2**28, moved=2**23, limit=50,
    )
    if aligned:
        lines = lax.all_to_all(packed, "gx", split_axis=0, concat_axis=0, tiled=True)
    else:
        lines = lax.all_to_all(packed, "gx", split_axis=1, concat_axis=0, tiled=True)
    lines = lines.reshape(total_x * share, lanes)
    lines, prev3, next3 = lax.optimization_barrier((lines, prev3, next3))
    def lines_body(*refs):
        line_kernel(*refs, scale=1.0 / (count * count))

    back = call(
        lines_body,
        shape(total_x * share, lanes),
        [VMEM] * 4,
        lines, *z_parts, x_both,
        scratch=[
            pltpu.VMEM((3 * total_x, share * lanes), BF16),
            pltpu.VMEM((2, total_x * (share + 2), 2 * lanes), BF16),
        ],
        flops=2**28, moved=2**22,
    )
    back = back.reshape(devices, planes * share, lanes)
    returned = lax.all_to_all(back, "gx", split_axis=0, concat_axis=0, tiled=True)
    if not aligned:
        returned = returned.reshape(devices, planes, share, lanes).transpose(1, 0, 2, 3)
        returned = returned.reshape(planes, slots, lanes)
    late = (chosen, class_table, prev2, prev1, prev3, next2, next1, next3, near_out, late_out, rates)
    late, _ = lax.optimization_barrier((late, back))
    order_params = call(
        rest_kernel,
        shape(GRAINS, planes, depth, width),
        [ANY] * len(late),
        *late,
        scratch=[
            *small,
            *[pltpu.VMEM(value.shape, F32) for value in late[2:]],
            pltpu.VMEM((2, *six), F32),
            pltpu.SemaphoreType.DMA((len(late),)),
        ],
        flops=2**26, moved=2**24, limit=24,
    )
    correlation = call(
        finish_kernel,
        shape(2, planes, depth, width),
        [VMEM] * 3,
        returned, *table,
        flops=2**28, moved=2**22,
    )
    return (order_params, correlation)


def solution(mesh):
    in_specs = (P(("grp", "gx"), None, None), P(None, ("grp", "gx"), None, None), P(), P())
    out_specs = (P(None, ("grp", "gx"), None, None), P(None, ("grp", "gx"), None, None))
    return jax.shard_map(shards, mesh=mesh, in_specs=in_specs, out_specs=out_specs, check_vma=False)
```

```python
import math

import jax
import jax.numpy as jnp
import ml_dtypes
import numpy as np
from jax import lax
from jax.experimental import pallas as pl
from jax.experimental.pallas import tpu as pltpu
from jax.sharding import PartitionSpec as P

STEPS = 3
GRAINS = 8
F32 = jnp.float32
BF16 = jnp.bfloat16
VMEM = pl.BlockSpec(memory_space=pltpu.VMEM)
ANY = pl.BlockSpec(memory_space=pltpu.HBM)
MIB = 2**20


def halves(table):
    table = np.asarray(table, np.float32)
    high = table.astype(ml_dtypes.bfloat16)
    low = (table - high.astype(np.float32)).astype(ml_dtypes.bfloat16)
    return high, low


def phases(length, rows=None):
    index = np.arange(length)
    product = np.arange(length if rows is None else rows)[:, None] * index[None, :] % length
    angle = product * (2.0 * math.pi / length)
    return np.cos(angle), np.sin(angle)


def y_table(width):
    cos_y, sin_y = phases(width, width // 2)
    sin_y = -sin_y
    sin_y[0] = 1.0 - 2.0 * (np.arange(width) % 2)
    return np.concatenate([cos_y, sin_y], axis=0)


def z_tables(depth):
    cos_z, sin_z = phases(depth)
    two = np.eye(2)
    cos_z, sin_z = np.kron(two, cos_z), np.kron(two, sin_z)
    forward = np.block([[cos_z, -sin_z], [sin_z, cos_z]])
    half = 2 * depth
    forward_turned = np.concatenate([forward[:, half:], -forward[:, :half]], axis=1)
    inverse = np.block([[cos_z, sin_z], [-sin_z, cos_z]])
    inverse_turned = np.concatenate([-inverse[:, half:], inverse[:, :half]], axis=1)
    return (
        np.concatenate([forward, forward_turned], axis=0),
        np.concatenate([inverse, inverse_turned], axis=0),
    )


def split(value):
    high = value.astype(BF16)
    low = (value - high.astype(F32)).astype(BF16)
    return high, low


def dot3(left, right, contract=((1,), (0,))):
    def one(a, b):
        return lax.dot_general(a, b, (contract, ((), ())), preferred_element_type=F32)

    return one(left[0], right[0]) + (one(left[0], right[1]) + one(left[1], right[0]))


def fetch(pairs, semaphores):
    copies = [pltpu.make_async_copy(src, dst, semaphores.at[k]) for k, (src, dst) in enumerate(pairs)]
    for copy in copies:
        copy.start()
    return copies


def pair_of(chosen):
    first, second = chosen[0], chosen[1]
    second = jnp.where(second == first, lax.rem(first + 1, GRAINS), second)
    return first, second


def others_of(chosen):
    first, second = pair_of(chosen)
    low, high = jnp.minimum(first, second), jnp.maximum(first, second)

    def other(r):
        i = jnp.where(r >= low, r + 1, r)
        return jnp.where(i >= high, i + 1, i)

    return other


def start_kernel(jitter_any, ids_any, p0, p1, p2, jitter, grain_ids, semaphores):
    planes = grain_ids.shape[0]
    pairs = []
    for k in range(planes):
        pairs.append((jitter_any.at[:, k], jitter.at[:, k]))
        pairs.append((ids_any.at[k], grain_ids.at[k]))
    copies = fetch(pairs, semaphores)
    for k, out in enumerate((p0, p1, p2)):
        copies[2 * k].wait()
        copies[2 * k + 1].wait()
        ids = grain_ids[k]
        for i in range(GRAINS):
            base = jnp.where(ids == i, jnp.float32(0.6), jnp.float32(0.0))
            out[i] = base + jitter[i, k].astype(F32)


def grain_of(start):
    ids = jnp.where(start[1] > 0.55, 1, 0)
    for g in range(2, GRAINS):
        ids = jnp.where(start[g] > 0.55, g, ids)
    return ids


def rate(classes, ids, i):
    def level(g):
        return 0.12 * (0.4 + 0.2 * classes[g, i].astype(F32))

    value = jnp.full(ids.shape, level(0), F32)
    for g in range(1, GRAINS):
        value = jnp.where(ids == g, level(g), value)
    return value


def squares(state):
    total = state[0] * state[0]
    for i in range(1, GRAINS):
        total = total + state[i] * state[i]
    return 5.0 + 3.0 * total


def update(e, before, after, total, mobility):
    depth, width = e.shape
    near = before + after
    near = near + (pltpu.roll(e, 1, 0) + pltpu.roll(e, depth - 1, 0))
    near = near + (pltpu.roll(e, 1, 1) + pltpu.roll(e, width - 1, 1))
    return e + mobility * (near - e * (total - 2.0 * (e * e)))


def step_plane(center, before, after, mobility, out):
    total = squares(center)
    for i in range(GRAINS):
        out[i] = update(center[i], before[i], after[i], total, mobility[i])


def rates_plane(classes, start, out):
    ids = grain_of(start)
    for i in range(GRAINS):
        out[i] = rate(classes, ids, i)


def inner_kernel(
    chosen_any, classes_any, p0, p1, p2, up2, down2, r0, r2, rates, middle, chosen, classes, semaphores
):
    copies = fetch(((chosen_any, chosen), (classes_any, classes)), semaphores)
    for i in range(GRAINS):
        up2[i] = p1[i]
        down2[i] = p1[i]
    for copy in copies:
        copy.wait()
    for k, i in enumerate(pair_of(chosen)):
        up2[GRAINS + k] = p0[i]
        down2[GRAINS + k] = p2[i]
    other = others_of(chosen)
    for r in range(GRAINS - 2):
        i = other(r)
        r0[r] = p0[i]
        r2[r] = p2[i]
    for k, start in enumerate((p0, p1, p2)):
        rates_plane(classes, start, rates.at[k])
    step_plane(p1, p0, p2, rates.at[1], middle)


def groups(ref, count, base=0):
    return [ref.at[pl.ds(base + k * GRAINS, GRAINS)] for k in range(count)]


def near_kernel(classes_any, p0, p1, p2, prev1, next1, rates, middle, near_out, classes, semaphores):
    edge0, edge1, inner0, inner2, middle2 = groups(near_out, 5)
    copies = fetch(((classes_any, classes),), semaphores)
    step_plane(p0, prev1, p1, rates.at[0], inner0)
    step_plane(p2, p1, next1, rates.at[2], inner2)
    copies[0].wait()
    rates_plane(classes, prev1, edge0)
    rates_plane(classes, next1, edge1)
    step_plane(middle, inner0, inner2, rates.at[1], middle2)


def second_step(p0, p2, prev1, next1, prev2, next2, rates, middle, near_state, outer1, side2):
    edge_rates, inner1 = near_state[:2], near_state[2:4]
    step_plane(prev1, prev2, p0, edge_rates[0], outer1[0])
    step_plane(next1, p2, next2, edge_rates[1], outer1[1])
    step_plane(inner1[0], outer1[0], middle, rates.at[0], side2[0])
    step_plane(inner1[1], middle, outer1[1], rates.at[2], side2[1])


def pair_kernel(
    chosen_any, classes_any, p0, p2, prev1, next1, prev2, next2, rates, middle, near_out, high_any, low_any,
    packed, chosen, classes, high, low, second, edge, fields, semaphores,
):
    copies = fetch(
        ((chosen_any, chosen), (classes_any, classes), (high_any, high), (low_any, low)), semaphores
    )
    near_state = groups(near_out, 5)
    edge_rates, inner1, middle2 = near_state[:2], near_state[2:4], near_state[4]
    outer1, side2 = groups(second, 2), groups(second, 2, 2 * GRAINS)
    second_step(p0, p2, prev1, next1, prev2, next2, rates, middle, near_state, outer1, side2)
    eta2 = (side2[0], middle2, side2[1])
    depth, width = p0.shape[1:]
    totals = [squares(state) for state in eta2]
    copies[0].wait()
    copies[1].wait()
    pair = pair_of(chosen)
    for side, (mid, near) in enumerate(((prev2, prev1), (next2, next1))):
        ids = grain_of(mid)
        total0 = squares(mid)
        total1 = squares(outer1[side])
        for k, i in enumerate(pair):
            first = update(mid[i], mid[GRAINS + k], near[i], total0, rate(classes, ids, i))
            edge[side, k] = update(outer1[side][i], first, inner1[side][i], total1, edge_rates[side][i])
    repeated = chosen[1] == chosen[0]
    for k in range(3):
        values = []
        for f, i in enumerate(pair):
            before = edge[0, f] if k == 0 else eta2[k - 1][i]
            after = edge[1, f] if k == 2 else eta2[k + 1][i]
            value = update(eta2[k][i], before, after, totals[k], rates[k, i])
            values.append(value)
        values[1] = jnp.where(repeated, values[0], values[1])
        for f in range(2):
            base = k * 2 * depth + f * depth
            fields[base : base + depth] = values[f]
    copies[2].wait()
    copies[3].wait()
    full = dot3((high[...], low[...]), split(fields[...]), ((1,), (1,)))
    slots = width // 2
    lanes = 4 * depth
    half = lanes // 2
    real_lane = lax.broadcasted_iota(jnp.int32, (slots, lanes), 1) < half
    for k in range(3):
        at = slice(k // 2 * lanes, k // 2 * lanes + lanes)
        cosine, sine = full[:slots, at], full[slots:, at]
        if k % 2:
            cosine = pltpu.roll(cosine, half, 1)
        else:
            sine = pltpu.roll(sine, half, 1)
        part = jnp.where(real_lane, cosine, sine)
        if packed.shape[0] == 3:
            packed[k] = part
        else:
            devices, rows, _ = packed.shape
            rows = rows // 3
            packed[:, k * rows : (k + 1) * rows, :] = part.reshape(devices, rows, lanes)


def rest_kernel(*refs):
    count = (len(refs) - 4) // 2
    sources, out, targets = refs[:count], refs[count], refs[count + 1 : 2 * count + 1]
    second, edge, semaphores = refs[-3:]
    copies = fetch(list(zip(sources, targets)), semaphores)
    chosen, classes, p0, p2, prev1, next1, prev2, next2, near_out, middle, rates, prev3, next3 = targets
    near_state = groups(near_out, 5)
    edge_rates, inner1, middle2 = near_state[:2], near_state[2:4], near_state[4]
    outer1, side2 = groups(second, 2), groups(second, 2, 2 * GRAINS)
    for copy in copies:
        copy.wait()
    second_step(p0, p2, prev1, next1, prev2, next2, rates, middle, near_state, outer1, side2)
    other = others_of(chosen)
    pair = pair_of(chosen)
    places = [(pair[k], GRAINS + k, None) for k in range(2)] + [(other(r), None, r) for r in range(GRAINS - 2)]
    for side, (far, mid, near) in enumerate(((prev3, prev2, prev1), (next3, next2, next1))):
        ids = grain_of(mid)
        total0 = squares(mid)
        total1 = squares(outer1[side])
        for k, (i, early, late) in enumerate(places):
            third = far[late] if early is None else mid[early]
            first = update(mid[i], third, near[i], total0, rate(classes, ids, i))
            edge[side, k] = update(outer1[side][i], first, inner1[side][i], total1, edge_rates[side][i])
    eta2 = (side2[0], middle2, side2[1])
    for plane in range(3):
        total = squares(eta2[plane])
        for k, (i, _, _) in enumerate(places):
            before = edge[0, k] if plane == 0 else eta2[plane - 1][i]
            after = edge[1, k] if plane == 2 else eta2[plane + 1][i]
            out[i, plane] = update(eta2[plane][i], before, after, total, rates[plane, i])


def line_kernel(lines, z_forward, z_inverse, x_both, out, wide, tall, scale):
    rows, lanes = lines.shape
    total_x = wide.shape[0] // 3
    slots = rows // total_x
    half = lanes // 2

    def over_x(pieces):
        for j, piece in enumerate(pieces):
            at = slice(j * lanes, (j + 1) * lanes)
            high, low = split(piece)
            wide[:total_x, at] = high
            wide[total_x : 2 * total_x, at] = low
            wide[2 * total_x :, at] = high
        both = jnp.dot(x_both[...], wide[...], preferred_element_type=F32)
        return both[:total_x], both[total_x:]

    def put(row, even, odd):
        at = slice(row * total_x, (row + 1) * total_x)
        for base, value in ((0, even), (lanes, odd)):
            high, low = split(value)
            tall[0, at, base : base + lanes] = high
            tall[1, at, base : base + lanes] = low

    real_lane = lax.broadcasted_iota(jnp.int32, (total_x, lanes), 1) < half
    even, odd = over_x([lines[pl.ds(j, total_x, stride=slots), :] for j in range(slots)])
    for j in range(slots):
        at = slice(j * lanes, (j + 1) * lanes)
        put(j, even[:, at], odd[:, at])
    first_even, first_odd = even[:, :lanes], odd[:, :lanes]
    put(slots, jnp.where(real_lane, first_even, 0.0), jnp.where(real_lane, first_odd, 0.0))
    put(
        slots + 1,
        jnp.where(real_lane, pltpu.roll(first_even, half, 1), 0.0),
        jnp.where(real_lane, pltpu.roll(first_odd, half, 1), 0.0),
    )
    spectrum = dot3((tall[0], tall[1]), (z_forward[0], z_forward[1]))
    spectrum = spectrum * spectrum
    spectrum = spectrum + pltpu.roll(spectrum, half, 1)

    def power(j):
        return spectrum[j * total_x : (j + 1) * total_x]

    first = lax.axis_index("gx") == 0
    lane = lax.broadcasted_iota(jnp.int32, (total_x, lanes), 1)
    line = lax.broadcasted_iota(jnp.int32, (total_x, lanes), 0)
    constant = jnp.logical_and(line == 0, jnp.logical_or(lane == 0, lane == half // 2))
    powers = []
    for j in range(slots):
        value = jnp.where(real_lane, power(j), 0.0) * (2.0 * scale)
        if j == 0:
            special = jnp.where(real_lane, power(slots), power(slots + 1)) * scale
            special = jnp.where(constant, 0.0, special)
            value = jnp.where(first, special, value)
        powers.append(value)
    even, odd = over_x(powers)
    for j in range(slots):
        at = slice(j * lanes, (j + 1) * lanes)
        put(j, even[:, at], odd[:, at])
    back = dot3((tall[0, :rows], tall[1, :rows]), (z_inverse[0], z_inverse[1]))
    for j in range(slots):
        out[pl.ds(j, total_x, stride=slots), :] = back[j * total_x : (j + 1) * total_x]


def finish_kernel(returned, high, low, out):
    fields, planes, depth, width = out.shape
    lanes = 2 * fields * depth
    half = lanes // 2
    slots = width // 2
    stacked = []
    for k in range(planes):
        if returned.shape[0] == planes:
            part = returned[k]
        else:
            devices, rows, _ = returned.shape
            rows = rows // planes
            part = returned[:, k * rows : (k + 1) * rows, :].reshape(slots, lanes)
        part = part.T
        stacked.append(jnp.concatenate([part[:half], part[half:]], axis=1))
    stacked = split(jnp.concatenate(stacked, axis=0))
    result = dot3(stacked, (high[...], low[...]))
    for k in range(planes):
        for f in range(fields):
            base = k * half + f * depth
            out[f, k] = result[base : base + depth]


def call(kernel, outs, in_specs, *args, scratch=(), flops=0, moved=0, limit=12):
    args = [pltpu.with_memory_space_constraint(a, pltpu.HBM) if b is ANY else a for a, b in zip(args, in_specs)]
    return pl.pallas_call(
        kernel,
        out_shape=outs,
        in_specs=in_specs,
        out_specs=jax.tree.map(lambda _: VMEM, outs),
        scratch_shapes=scratch,
        compiler_params=pltpu.CompilerParams(vmem_limit_bytes=limit * MIB),
        cost_estimate=pl.CostEstimate(flops=flops, bytes_accessed=moved, transcendentals=0),
    )(*args)


def shards(grain_ids, jitter, class_table, chosen):
    planes, depth, width = grain_ids.shape
    devices = lax.axis_size("gx")
    total_x = planes * devices
    count = float(total_x * depth * width)
    slots = width // 2
    share = slots // devices
    lanes = 4 * depth
    up = [(i, (i + 1) % devices) for i in range(devices)]
    down = [(j, i) for i, j in up]
    aligned = share % 8 == 0

    def shape(*dims):
        return jax.ShapeDtypeStruct(dims, F32)

    plane = (GRAINS, depth, width)
    table = [jnp.asarray(part) for part in halves(y_table(width))]
    z_forward, z_inverse = z_tables(depth)
    z_parts = [jnp.asarray(np.stack(halves(matrix))) for matrix in (z_forward, z_inverse)]
    x_high, x_low = halves(np.concatenate(phases(total_x), axis=0))
    x_both = jnp.asarray(np.concatenate([x_high, x_high, x_low], axis=1))

    two = (2, *plane)
    six = (GRAINS - 2, depth, width)
    small = [pltpu.SMEM((2,), jnp.int32), pltpu.SMEM((GRAINS, GRAINS), jnp.int32)]
    ten = (GRAINS + 2, depth, width)
    p0, p1, p2 = call(
        start_kernel,
        (shape(*plane), shape(*plane), shape(*plane)),
        [ANY] * 2,
        jitter, grain_ids,
        scratch=[
            pltpu.VMEM(jitter.shape, jitter.dtype),
            pltpu.VMEM(grain_ids.shape, jnp.int32),
            pltpu.SemaphoreType.DMA((2 * planes,)),
        ],
        flops=2**21, moved=2**22,
    )
    prev1 = lax.ppermute(p2, "gx", up)
    next1 = lax.ppermute(p0, "gx", down)
    up2, down2, r0, r2, rates, middle = call(
        inner_kernel,
        (shape(*ten), shape(*ten), shape(*six), shape(*six), shape(planes, *plane), shape(*plane)),
        [ANY] * 2 + [VMEM] * 3,
        chosen, class_table, p0, p1, p2,
        scratch=[*small, pltpu.SemaphoreType.DMA((2,))],
        flops=2**24, moved=2**22,
    )
    prev2 = lax.ppermute(up2, "gx", up)
    next2 = lax.ppermute(down2, "gx", down)
    r0, r2, prev1, next1 = lax.optimization_barrier((r0, r2, prev1, next1))
    prev3 = lax.ppermute(r0, "gx", up)
    next3 = lax.ppermute(r2, "gx", down)
    near_out = call(
        near_kernel,
        shape(5 * GRAINS, depth, width),
        [ANY] + [VMEM] * 7,
        class_table, p0, p1, p2, prev1, next1, rates, middle,
        scratch=[small[1], pltpu.SemaphoreType.DMA((1,))],
        flops=2**25, moved=2**24,
    )
    packed_shape = (devices, planes * share, lanes) if aligned else (planes, slots, lanes)
    packed = call(
        pair_kernel,
        shape(*packed_shape),
        [ANY] * 2 + [VMEM] * 9 + [ANY] * 2,
        chosen, class_table, p0, p2, prev1, next1, prev2, next2, rates, middle, near_out, *table,
        scratch=[
            *small,
            pltpu.VMEM(table[0].shape, BF16),
            pltpu.VMEM(table[1].shape, BF16),
            pltpu.VMEM((4 * GRAINS, depth, width), F32),
            pltpu.VMEM((2, 2, depth, width), F32),
            pltpu.VMEM(((planes + 1) // 2 * lanes, width), F32),
            pltpu.SemaphoreType.DMA((4,)),
        ],
        flops=2**28, moved=2**23,
    )
    packed, prev3, next3 = lax.optimization_barrier((packed, prev3, next3))
    if aligned:
        lines = lax.all_to_all(packed, "gx", split_axis=0, concat_axis=0, tiled=True)
    else:
        lines = lax.all_to_all(packed, "gx", split_axis=1, concat_axis=0, tiled=True)
    lines = lines.reshape(total_x * share, lanes)
    def lines_body(*refs):
        line_kernel(*refs, scale=1.0 / (count * count))

    back = call(
        lines_body,
        shape(total_x * share, lanes),
        [VMEM] * 4,
        lines, *z_parts, x_both,
        scratch=[
            pltpu.VMEM((3 * total_x, share * lanes), BF16),
            pltpu.VMEM((2, total_x * (share + 2), 2 * lanes), BF16),
        ],
        flops=2**28, moved=2**22,
    )
    back = back.reshape(devices, planes * share, lanes)
    returned = lax.all_to_all(back, "gx", split_axis=0, concat_axis=0, tiled=True)
    if not aligned:
        returned = returned.reshape(devices, planes, share, lanes).transpose(1, 0, 2, 3)
        returned = returned.reshape(planes, slots, lanes)
    late = (chosen, class_table, p0, p2, prev1, next1, prev2, next2, near_out, middle, rates, prev3, next3)
    late, _ = lax.optimization_barrier((late, back))
    order_params = call(
        rest_kernel,
        shape(GRAINS, planes, depth, width),
        [ANY] * len(late),
        *late,
        scratch=[
            *small,
            *[pltpu.VMEM(value.shape, F32) for value in late[2:]],
            pltpu.VMEM((4 * GRAINS, depth, width), F32),
            pltpu.VMEM((2, *plane), F32),
            pltpu.SemaphoreType.DMA((len(late),)),
        ],
        flops=2**26, moved=2**24, limit=24,
    )
    correlation = call(
        finish_kernel,
        shape(2, planes, depth, width),
        [VMEM] * 3,
        returned, *table,
        flops=2**28, moved=2**22,
    )
    return (order_params, correlation)


def solution(mesh):
    in_specs = (P(("grp", "gx"), None, None), P(None, ("grp", "gx"), None, None), P(), P())
    out_specs = (P(None, ("grp", "gx"), None, None), P(None, ("grp", "gx"), None, None))
    return jax.shard_map(shards, mesh=mesh, in_specs=in_specs, out_specs=out_specs, check_vma=False)
```

```python
import math

import jax
import jax.numpy as jnp
import ml_dtypes
import numpy as np
from jax import lax
from jax.experimental import pallas as pl
from jax.experimental.pallas import tpu as pltpu
from jax.sharding import PartitionSpec as P

STEPS = 3
SOON = 3
GRAINS = 8
F32 = jnp.float32
BF16 = jnp.bfloat16
VMEM = pl.BlockSpec(memory_space=pltpu.VMEM)
ANY = pl.BlockSpec(memory_space=pltpu.HBM)
MIB = 2**20


def halves(table):
    table = np.asarray(table, np.float32)
    high = table.astype(ml_dtypes.bfloat16)
    low = (table - high.astype(np.float32)).astype(ml_dtypes.bfloat16)
    return high, low


def phases(length, rows=None):
    index = np.arange(length)
    product = np.arange(length if rows is None else rows)[:, None] * index[None, :] % length
    angle = product * (2.0 * math.pi / length)
    return np.cos(angle), np.sin(angle)


def y_table(width):
    cos_y, sin_y = phases(width, width // 2)
    sin_y = -sin_y
    sin_y[0] = 1.0 - 2.0 * (np.arange(width) % 2)
    return np.concatenate([cos_y, sin_y], axis=0)


def z_tables(depth):
    cos_z, sin_z = phases(depth)
    two = np.eye(2)
    cos_z, sin_z = np.kron(two, cos_z), np.kron(two, sin_z)
    forward = np.block([[cos_z, -sin_z], [sin_z, cos_z]])
    half = 2 * depth
    forward_turned = np.concatenate([forward[:, half:], -forward[:, :half]], axis=1)
    inverse = np.block([[cos_z, sin_z], [-sin_z, cos_z]])
    inverse_turned = np.concatenate([-inverse[:, half:], inverse[:, :half]], axis=1)
    return (
        np.concatenate([forward, forward_turned], axis=0),
        np.concatenate([inverse, inverse_turned], axis=0),
    )


def split(value):
    high = value.astype(BF16)
    low = (value - high.astype(F32)).astype(BF16)
    return high, low


def dot3(left, right, contract=((1,), (0,))):
    def one(a, b):
        return lax.dot_general(a, b, (contract, ((), ())), preferred_element_type=F32)

    return one(left[0], right[0]) + (one(left[0], right[1]) + one(left[1], right[0]))


def fetch(pairs, semaphores):
    copies = [pltpu.make_async_copy(src, dst, semaphores.at[k]) for k, (src, dst) in enumerate(pairs)]
    for copy in copies:
        copy.start()
    return copies


def pair_of(chosen):
    first, second = chosen[0], chosen[1]
    second = jnp.where(second == first, lax.rem(first + 1, GRAINS), second)
    return first, second


def others_of(chosen):
    first, second = pair_of(chosen)
    low, high = jnp.minimum(first, second), jnp.maximum(first, second)

    def other(r):
        i = jnp.where(r >= low, r + 1, r)
        return jnp.where(i >= high, i + 1, i)

    return other


def start_kernel(jitter_any, ids_any, p0, p1, p2, jitter, grain_ids, semaphores):
    planes = grain_ids.shape[0]
    pairs = []
    for k in range(planes):
        pairs.append((jitter_any.at[:, k], jitter.at[:, k]))
        pairs.append((ids_any.at[k], grain_ids.at[k]))
    copies = fetch(pairs, semaphores)
    for k, out in enumerate((p0, p1, p2)):
        copies[2 * k].wait()
        copies[2 * k + 1].wait()
        ids = grain_ids[k]
        for i in range(GRAINS):
            base = jnp.where(ids == i, jnp.float32(0.6), jnp.float32(0.0))
            out[i] = base + jitter[i, k].astype(F32)


def grain_of(start):
    ids = jnp.where(start[1] > 0.55, 1, 0)
    for g in range(2, GRAINS):
        ids = jnp.where(start[g] > 0.55, g, ids)
    return ids


def rate(classes, ids, i):
    def level(g):
        return 0.12 * (0.4 + 0.2 * classes[g, i].astype(F32))

    value = jnp.full(ids.shape, level(0), F32)
    for g in range(1, GRAINS):
        value = jnp.where(ids == g, level(g), value)
    return value


def squares(state):
    total = state[0] * state[0]
    for i in range(1, GRAINS):
        total = total + state[i] * state[i]
    return 5.0 + 3.0 * total


def update(e, before, after, total, mobility):
    depth, width = e.shape
    near = before + after
    near = near + (pltpu.roll(e, 1, 0) + pltpu.roll(e, depth - 1, 0))
    near = near + (pltpu.roll(e, 1, 1) + pltpu.roll(e, width - 1, 1))
    return e + mobility * (near - e * (total - 2.0 * (e * e)))


def step_plane(center, before, after, mobility, out):
    total = squares(center)
    for i in range(GRAINS):
        out[i] = update(center[i], before[i], after[i], total, mobility[i])


def rates_plane(classes, start, out):
    ids = grain_of(start)
    for i in range(GRAINS):
        out[i] = rate(classes, ids, i)


def inner_kernel(
    chosen_any, classes_any, p0, p1, p2, up2, down2, r0, r2, l0, l2, rates, middle, chosen, classes, semaphores
):
    copies = fetch(((chosen_any, chosen), (classes_any, classes)), semaphores)
    for i in range(GRAINS):
        up2[i] = p1[i]
        down2[i] = p1[i]
    for copy in copies:
        copy.wait()
    for k, i in enumerate(pair_of(chosen)):
        up2[GRAINS + k] = p0[i]
        down2[GRAINS + k] = p2[i]
    other = others_of(chosen)
    for r in range(GRAINS - 2):
        i = other(r)
        for soon, late, start in ((r0, l0, p0), (r2, l2, p2)):
            if r < SOON:
                soon[r] = start[i]
            else:
                late[r - SOON] = start[i]
    for k, start in enumerate((p0, p1, p2)):
        rates_plane(classes, start, rates.at[k])
    step_plane(p1, p0, p2, rates.at[1], middle)


def groups(ref, count, base=0):
    return [ref.at[pl.ds(base + k * GRAINS, GRAINS)] for k in range(count)]


def near_kernel(classes_any, p0, p1, p2, prev1, next1, rates, middle, near_out, classes, semaphores):
    edge0, edge1, inner0, inner2, middle2 = groups(near_out, 5)
    copies = fetch(((classes_any, classes),), semaphores)
    step_plane(p0, prev1, p1, rates.at[0], inner0)
    step_plane(p2, p1, next1, rates.at[2], inner2)
    copies[0].wait()
    rates_plane(classes, prev1, edge0)
    rates_plane(classes, next1, edge1)
    step_plane(middle, inner0, inner2, rates.at[1], middle2)


def second_step(p0, p2, prev1, next1, prev2, next2, rates, middle, near_state, outer1, side2):
    edge_rates, inner1 = near_state[:2], near_state[2:4]
    step_plane(prev1, prev2, p0, edge_rates[0], outer1[0])
    step_plane(next1, p2, next2, edge_rates[1], outer1[1])
    step_plane(inner1[0], outer1[0], middle, rates.at[0], side2[0])
    step_plane(inner1[1], middle, outer1[1], rates.at[2], side2[1])


def pair_kernel(
    chosen_any, classes_any, p0, p2, prev1, next1, prev2, next2, rates, middle, near_out, high_any, low_any,
    packed, chosen, classes, high, low, second, edge, fields, semaphores,
):
    copies = fetch(
        ((chosen_any, chosen), (classes_any, classes), (high_any, high), (low_any, low)), semaphores
    )
    near_state = groups(near_out, 5)
    edge_rates, inner1, middle2 = near_state[:2], near_state[2:4], near_state[4]
    outer1, side2 = groups(second, 2), groups(second, 2, 2 * GRAINS)
    second_step(p0, p2, prev1, next1, prev2, next2, rates, middle, near_state, outer1, side2)
    eta2 = (side2[0], middle2, side2[1])
    depth, width = p0.shape[1:]
    totals = [squares(state) for state in eta2]
    copies[0].wait()
    copies[1].wait()
    pair = pair_of(chosen)
    for side, (mid, near) in enumerate(((prev2, prev1), (next2, next1))):
        ids = grain_of(mid)
        total0 = squares(mid)
        total1 = squares(outer1[side])
        for k, i in enumerate(pair):
            first = update(mid[i], mid[GRAINS + k], near[i], total0, rate(classes, ids, i))
            edge[side, k] = update(outer1[side][i], first, inner1[side][i], total1, edge_rates[side][i])
    repeated = chosen[1] == chosen[0]
    for k in range(3):
        values = []
        for f, i in enumerate(pair):
            before = edge[0, f] if k == 0 else eta2[k - 1][i]
            after = edge[1, f] if k == 2 else eta2[k + 1][i]
            value = update(eta2[k][i], before, after, totals[k], rates[k, i])
            values.append(value)
        values[1] = jnp.where(repeated, values[0], values[1])
        for f in range(2):
            base = k * 2 * depth + f * depth
            fields[base : base + depth] = values[f]
    copies[2].wait()
    copies[3].wait()
    full = dot3((high[...], low[...]), split(fields[...]), ((1,), (1,)))
    slots = width // 2
    lanes = 4 * depth
    half = lanes // 2
    real_lane = lax.broadcasted_iota(jnp.int32, (slots, lanes), 1) < half
    for k in range(3):
        at = slice(k // 2 * lanes, k // 2 * lanes + lanes)
        cosine, sine = full[:slots, at], full[slots:, at]
        if k % 2:
            cosine = pltpu.roll(cosine, half, 1)
        else:
            sine = pltpu.roll(sine, half, 1)
        part = jnp.where(real_lane, cosine, sine)
        if packed.shape[0] == 3:
            packed[k] = part
        else:
            devices, rows, _ = packed.shape
            rows = rows // 3
            packed[:, k * rows : (k + 1) * rows, :] = part.reshape(devices, rows, lanes)


def rest_kernel(*refs):
    count = (len(refs) - 4) // 2
    sources, out, targets = refs[:count], refs[count], refs[count + 1 : 2 * count + 1]
    second, edge, semaphores = refs[-3:]
    copies = fetch(list(zip(sources, targets)), semaphores)
    chosen, classes, p0, p2, prev1, next1, prev2, next2, near_out, middle, rates, prev3, next3, prev4, next4 = targets
    near_state = groups(near_out, 5)
    edge_rates, inner1, middle2 = near_state[:2], near_state[2:4], near_state[4]
    outer1, side2 = groups(second, 2), groups(second, 2, 2 * GRAINS)
    for copy in copies:
        copy.wait()
    second_step(p0, p2, prev1, next1, prev2, next2, rates, middle, near_state, outer1, side2)
    other = others_of(chosen)
    pair = pair_of(chosen)
    places = [(pair[k], GRAINS + k, None) for k in range(2)] + [(other(r), None, r) for r in range(GRAINS - 2)]
    for side, (soon, far, mid, near) in enumerate(((prev3, prev4, prev2, prev1), (next3, next4, next2, next1))):
        ids = grain_of(mid)
        total0 = squares(mid)
        total1 = squares(outer1[side])
        for k, (i, early, late) in enumerate(places):
            if early is not None:
                third = mid[early]
            else:
                third = soon[late] if late < SOON else far[late - SOON]
            first = update(mid[i], third, near[i], total0, rate(classes, ids, i))
            edge[side, k] = update(outer1[side][i], first, inner1[side][i], total1, edge_rates[side][i])
    eta2 = (side2[0], middle2, side2[1])
    for plane in range(3):
        total = squares(eta2[plane])
        for k, (i, _, _) in enumerate(places):
            before = edge[0, k] if plane == 0 else eta2[plane - 1][i]
            after = edge[1, k] if plane == 2 else eta2[plane + 1][i]
            out[i, plane] = update(eta2[plane][i], before, after, total, rates[plane, i])


def line_kernel(lines, z_forward, z_inverse, x_both, out, wide, tall, scale):
    rows, lanes = lines.shape
    total_x = wide.shape[0] // 3
    slots = rows // total_x
    half = lanes // 2

    def over_x(pieces):
        for j, piece in enumerate(pieces):
            at = slice(j * lanes, (j + 1) * lanes)
            high, low = split(piece)
            wide[:total_x, at] = high
            wide[total_x : 2 * total_x, at] = low
            wide[2 * total_x :, at] = high
        both = jnp.dot(x_both[...], wide[...], preferred_element_type=F32)
        return both[:total_x], both[total_x:]

    def put(row, even, odd):
        at = slice(row * total_x, (row + 1) * total_x)
        for base, value in ((0, even), (lanes, odd)):
            high, low = split(value)
            tall[0, at, base : base + lanes] = high
            tall[1, at, base : base + lanes] = low

    real_lane = lax.broadcasted_iota(jnp.int32, (total_x, lanes), 1) < half
    even, odd = over_x([lines[pl.ds(j, total_x, stride=slots), :] for j in range(slots)])
    for j in range(slots):
        at = slice(j * lanes, (j + 1) * lanes)
        put(j, even[:, at], odd[:, at])
    first_even, first_odd = even[:, :lanes], odd[:, :lanes]
    put(slots, jnp.where(real_lane, first_even, 0.0), jnp.where(real_lane, first_odd, 0.0))
    put(
        slots + 1,
        jnp.where(real_lane, pltpu.roll(first_even, half, 1), 0.0),
        jnp.where(real_lane, pltpu.roll(first_odd, half, 1), 0.0),
    )
    spectrum = dot3((tall[0], tall[1]), (z_forward[0], z_forward[1]))
    spectrum = spectrum * spectrum
    spectrum = spectrum + pltpu.roll(spectrum, half, 1)

    def power(j):
        return spectrum[j * total_x : (j + 1) * total_x]

    first = lax.axis_index("gx") == 0
    lane = lax.broadcasted_iota(jnp.int32, (total_x, lanes), 1)
    line = lax.broadcasted_iota(jnp.int32, (total_x, lanes), 0)
    constant = jnp.logical_and(line == 0, jnp.logical_or(lane == 0, lane == half // 2))
    powers = []
    for j in range(slots):
        value = jnp.where(real_lane, power(j), 0.0) * (2.0 * scale)
        if j == 0:
            special = jnp.where(real_lane, power(slots), power(slots + 1)) * scale
            special = jnp.where(constant, 0.0, special)
            value = jnp.where(first, special, value)
        powers.append(value)
    even, odd = over_x(powers)
    for j in range(slots):
        at = slice(j * lanes, (j + 1) * lanes)
        put(j, even[:, at], odd[:, at])
    back = dot3((tall[0, :rows], tall[1, :rows]), (z_inverse[0], z_inverse[1]))
    for j in range(slots):
        out[pl.ds(j, total_x, stride=slots), :] = back[j * total_x : (j + 1) * total_x]


def finish_kernel(returned, high, low, out):
    fields, planes, depth, width = out.shape
    lanes = 2 * fields * depth
    half = lanes // 2
    slots = width // 2
    stacked = []
    for k in range(planes):
        if returned.shape[0] == planes:
            part = returned[k]
        else:
            devices, rows, _ = returned.shape
            rows = rows // planes
            part = returned[:, k * rows : (k + 1) * rows, :].reshape(slots, lanes)
        part = part.T
        stacked.append(jnp.concatenate([part[:half], part[half:]], axis=1))
    stacked = split(jnp.concatenate(stacked, axis=0))
    result = dot3(stacked, (high[...], low[...]))
    for k in range(planes):
        for f in range(fields):
            base = k * half + f * depth
            out[f, k] = result[base : base + depth]


def call(kernel, outs, in_specs, *args, scratch=(), flops=0, moved=0, limit=12):
    args = [pltpu.with_memory_space_constraint(a, pltpu.HBM) if b is ANY else a for a, b in zip(args, in_specs)]
    return pl.pallas_call(
        kernel,
        out_shape=outs,
        in_specs=in_specs,
        out_specs=jax.tree.map(lambda _: VMEM, outs),
        scratch_shapes=scratch,
        compiler_params=pltpu.CompilerParams(vmem_limit_bytes=limit * MIB),
        cost_estimate=pl.CostEstimate(flops=flops, bytes_accessed=moved, transcendentals=0),
    )(*args)


def shards(grain_ids, jitter, class_table, chosen):
    planes, depth, width = grain_ids.shape
    devices = lax.axis_size("gx")
    total_x = planes * devices
    count = float(total_x * depth * width)
    slots = width // 2
    share = slots // devices
    lanes = 4 * depth
    up = [(i, (i + 1) % devices) for i in range(devices)]
    down = [(j, i) for i, j in up]
    aligned = share % 8 == 0

    def shape(*dims):
        return jax.ShapeDtypeStruct(dims, F32)

    plane = (GRAINS, depth, width)
    table = [jnp.asarray(part) for part in halves(y_table(width))]
    z_forward, z_inverse = z_tables(depth)
    z_parts = [jnp.asarray(np.stack(halves(matrix))) for matrix in (z_forward, z_inverse)]
    x_high, x_low = halves(np.concatenate(phases(total_x), axis=0))
    x_both = jnp.asarray(np.concatenate([x_high, x_high, x_low], axis=1))

    two = (2, *plane)
    soon, last = (SOON, depth, width), (GRAINS - 2 - SOON, depth, width)
    small = [pltpu.SMEM((2,), jnp.int32), pltpu.SMEM((GRAINS, GRAINS), jnp.int32)]
    ten = (GRAINS + 2, depth, width)
    p0, p1, p2 = call(
        start_kernel,
        (shape(*plane), shape(*plane), shape(*plane)),
        [ANY] * 2,
        jitter, grain_ids,
        scratch=[
            pltpu.VMEM(jitter.shape, jitter.dtype),
            pltpu.VMEM(grain_ids.shape, jnp.int32),
            pltpu.SemaphoreType.DMA((2 * planes,)),
        ],
        flops=2**21, moved=2**22,
    )
    prev1 = lax.ppermute(p2, "gx", up)
    next1 = lax.ppermute(p0, "gx", down)
    up2, down2, r0, r2, l0, l2, rates, middle = call(
        inner_kernel,
        (
            shape(*ten), shape(*ten), shape(*soon), shape(*soon), shape(*last), shape(*last),
            shape(planes, *plane), shape(*plane),
        ),
        [ANY] * 2 + [VMEM] * 3,
        chosen, class_table, p0, p1, p2,
        scratch=[*small, pltpu.SemaphoreType.DMA((2,))],
        flops=2**24, moved=2**22,
    )
    prev2 = lax.ppermute(up2, "gx", up)
    next2 = lax.ppermute(down2, "gx", down)
    r0, r2, l0, l2, prev1, next1 = lax.optimization_barrier((r0, r2, l0, l2, prev1, next1))
    prev3 = lax.ppermute(r0, "gx", up)
    next3 = lax.ppermute(r2, "gx", down)
    prev4 = lax.ppermute(l0, "gx", up)
    next4 = lax.ppermute(l2, "gx", down)
    near_out = call(
        near_kernel,
        shape(5 * GRAINS, depth, width),
        [ANY] + [VMEM] * 7,
        class_table, p0, p1, p2, prev1, next1, rates, middle,
        scratch=[small[1], pltpu.SemaphoreType.DMA((1,))],
        flops=2**25, moved=2**24,
    )
    packed_shape = (devices, planes * share, lanes) if aligned else (planes, slots, lanes)
    packed = call(
        pair_kernel,
        shape(*packed_shape),
        [ANY] * 2 + [VMEM] * 9 + [ANY] * 2,
        chosen, class_table, p0, p2, prev1, next1, prev2, next2, rates, middle, near_out, *table,
        scratch=[
            *small,
            pltpu.VMEM(table[0].shape, BF16),
            pltpu.VMEM(table[1].shape, BF16),
            pltpu.VMEM((4 * GRAINS, depth, width), F32),
            pltpu.VMEM((2, 2, depth, width), F32),
            pltpu.VMEM(((planes + 1) // 2 * lanes, width), F32),
            pltpu.SemaphoreType.DMA((4,)),
        ],
        flops=2**28, moved=2**23,
    )
    packed, prev3, next3 = lax.optimization_barrier((packed, prev3, next3))
    if aligned:
        lines = lax.all_to_all(packed, "gx", split_axis=0, concat_axis=0, tiled=True)
    else:
        lines = lax.all_to_all(packed, "gx", split_axis=1, concat_axis=0, tiled=True)
    lines = lines.reshape(total_x * share, lanes)
    lines, prev4, next4 = lax.optimization_barrier((lines, prev4, next4))
    def lines_body(*refs):
        line_kernel(*refs, scale=1.0 / (count * count))

    back = call(
        lines_body,
        shape(total_x * share, lanes),
        [VMEM] * 4,
        lines, *z_parts, x_both,
        scratch=[
            pltpu.VMEM((3 * total_x, share * lanes), BF16),
            pltpu.VMEM((2, total_x * (share + 2), 2 * lanes), BF16),
        ],
        flops=2**28, moved=2**22,
    )
    back = back.reshape(devices, planes * share, lanes)
    returned = lax.all_to_all(back, "gx", split_axis=0, concat_axis=0, tiled=True)
    if not aligned:
        returned = returned.reshape(devices, planes, share, lanes).transpose(1, 0, 2, 3)
        returned = returned.reshape(planes, slots, lanes)
    late = (chosen, class_table, p0, p2, prev1, next1, prev2, next2, near_out, middle, rates, prev3, next3, prev4, next4)
    late, _ = lax.optimization_barrier((late, back))
    order_params = call(
        rest_kernel,
        shape(GRAINS, planes, depth, width),
        [ANY] * len(late),
        *late,
        scratch=[
            *small,
            *[pltpu.VMEM(value.shape, F32) for value in late[2:]],
            pltpu.VMEM((4 * GRAINS, depth, width), F32),
            pltpu.VMEM((2, *plane), F32),
            pltpu.SemaphoreType.DMA((len(late),)),
        ],
        flops=2**26, moved=2**24, limit=24,
    )
    correlation = call(
        finish_kernel,
        shape(2, planes, depth, width),
        [VMEM] * 3,
        returned, *table,
        flops=2**28, moved=2**22,
    )
    return (order_params, correlation)


def solution(mesh):
    in_specs = (P(("grp", "gx"), None, None), P(None, ("grp", "gx"), None, None), P(), P())
    out_specs = (P(None, ("grp", "gx"), None, None), P(None, ("grp", "gx"), None, None))
    return jax.shard_map(shards, mesh=mesh, in_specs=in_specs, out_specs=out_specs, check_vma=False)
```

```python
import math

import jax
import jax.numpy as jnp
import ml_dtypes
import numpy as np
from jax import lax
from jax.experimental import pallas as pl
from jax.experimental.pallas import tpu as pltpu
from jax.sharding import PartitionSpec as P

STEPS = 3
SOON = 3
GRAINS = 8
F32 = jnp.float32
BF16 = jnp.bfloat16
VMEM = pl.BlockSpec(memory_space=pltpu.VMEM)
ANY = pl.BlockSpec(memory_space=pltpu.HBM)
MIB = 2**20


def halves(table):
    table = np.asarray(table, np.float32)
    high = table.astype(ml_dtypes.bfloat16)
    low = (table - high.astype(np.float32)).astype(ml_dtypes.bfloat16)
    return high, low


def phases(length, rows=None):
    index = np.arange(length)
    product = np.arange(length if rows is None else rows)[:, None] * index[None, :] % length
    angle = product * (2.0 * math.pi / length)
    return np.cos(angle), np.sin(angle)


def y_table(width):
    cos_y, sin_y = phases(width, width // 2)
    sin_y = -sin_y
    sin_y[0] = 1.0 - 2.0 * (np.arange(width) % 2)
    return np.concatenate([cos_y, sin_y], axis=0)


def z_tables(depth):
    cos_z, sin_z = phases(depth)
    two = np.eye(2)
    cos_z, sin_z = np.kron(two, cos_z), np.kron(two, sin_z)
    forward = np.block([[cos_z, -sin_z], [sin_z, cos_z]])
    half = 2 * depth
    forward_turned = np.concatenate([forward[:, half:], -forward[:, :half]], axis=1)
    inverse = np.block([[cos_z, sin_z], [-sin_z, cos_z]])
    inverse_turned = np.concatenate([-inverse[:, half:], inverse[:, :half]], axis=1)
    return (
        np.concatenate([forward, forward_turned], axis=0),
        np.concatenate([inverse, inverse_turned], axis=0),
    )


def split(value):
    high = value.astype(BF16)
    low = (value - high.astype(F32)).astype(BF16)
    return high, low


def dot3(left, right, contract=((1,), (0,))):
    def one(a, b):
        return lax.dot_general(a, b, (contract, ((), ())), preferred_element_type=F32)

    return one(left[0], right[0]) + (one(left[0], right[1]) + one(left[1], right[0]))


def fetch(pairs, semaphores):
    copies = [pltpu.make_async_copy(src, dst, semaphores.at[k]) for k, (src, dst) in enumerate(pairs)]
    for copy in copies:
        copy.start()
    return copies


def pair_of(chosen):
    first, second = chosen[0], chosen[1]
    second = jnp.where(second == first, lax.rem(first + 1, GRAINS), second)
    return first, second


def others_of(chosen):
    first, second = pair_of(chosen)
    low, high = jnp.minimum(first, second), jnp.maximum(first, second)

    def other(r):
        i = jnp.where(r >= low, r + 1, r)
        return jnp.where(i >= high, i + 1, i)

    return other


def start_kernel(jitter_any, ids_any, p0, p1, p2, jitter, grain_ids, semaphores):
    planes = grain_ids.shape[0]
    pairs = []
    for k in range(planes):
        pairs.append((jitter_any.at[:, k], jitter.at[:, k]))
        pairs.append((ids_any.at[k], grain_ids.at[k]))
    copies = fetch(pairs, semaphores)
    for k, out in enumerate((p0, p1, p2)):
        copies[2 * k].wait()
        copies[2 * k + 1].wait()
        ids = grain_ids[k]
        for i in range(GRAINS):
            base = jnp.where(ids == i, jnp.float32(0.6), jnp.float32(0.0))
            out[i] = base + jitter[i, k].astype(F32)


def grain_of(start):
    ids = jnp.where(start[1] > 0.55, 1, 0)
    for g in range(2, GRAINS):
        ids = jnp.where(start[g] > 0.55, g, ids)
    return ids


def rate(classes, ids, i):
    def level(g):
        return 0.12 * (0.4 + 0.2 * classes[g, i].astype(F32))

    value = jnp.full(ids.shape, level(0), F32)
    for g in range(1, GRAINS):
        value = jnp.where(ids == g, level(g), value)
    return value


def squares(state):
    total = state[0] * state[0]
    for i in range(1, GRAINS):
        total = total + state[i] * state[i]
    return 5.0 + 3.0 * total


def update(e, before, after, total, mobility):
    depth, width = e.shape
    near = before + after
    near = near + (pltpu.roll(e, 1, 0) + pltpu.roll(e, depth - 1, 0))
    near = near + (pltpu.roll(e, 1, 1) + pltpu.roll(e, width - 1, 1))
    return e + mobility * (near - e * (total - 2.0 * (e * e)))


def step_plane(center, before, after, mobility, out):
    total = squares(center)
    for i in range(GRAINS):
        out[i] = update(center[i], before[i], after[i], total, mobility[i])


def rates_plane(classes, start, out):
    ids = grain_of(start)
    for i in range(GRAINS):
        out[i] = rate(classes, ids, i)


def inner_kernel(
    chosen_any, classes_any, p0, p1, p2, up2, down2, r0, r2, l0, l2, rates, middle, chosen, classes, semaphores
):
    copies = fetch(((chosen_any, chosen), (classes_any, classes)), semaphores)
    for i in range(GRAINS):
        up2[i] = p1[i]
        down2[i] = p1[i]
    for copy in copies:
        copy.wait()
    for k, i in enumerate(pair_of(chosen)):
        up2[GRAINS + k] = p0[i]
        down2[GRAINS + k] = p2[i]
    other = others_of(chosen)
    for r in range(GRAINS - 2):
        i = other(r)
        for soon, late, start in ((r0, l0, p0), (r2, l2, p2)):
            if r < SOON:
                soon[r] = start[i]
            else:
                late[r - SOON] = start[i]
    for k, start in enumerate((p0, p1, p2)):
        rates_plane(classes, start, rates.at[k])
    step_plane(p1, p0, p2, rates.at[1], middle)


def groups(ref, count, base=0):
    return [ref.at[pl.ds(base + k * GRAINS, GRAINS)] for k in range(count)]


def near_kernel(classes_any, p0, p1, p2, prev1, next1, rates, middle, near_out, classes, semaphores):
    edge0, edge1, inner0, inner2, middle2 = groups(near_out, 5)
    copies = fetch(((classes_any, classes),), semaphores)
    step_plane(p0, prev1, p1, rates.at[0], inner0)
    step_plane(p2, p1, next1, rates.at[2], inner2)
    copies[0].wait()
    rates_plane(classes, prev1, edge0)
    rates_plane(classes, next1, edge1)
    step_plane(middle, inner0, inner2, rates.at[1], middle2)


def second_step(p0, p2, prev1, next1, prev2, next2, rates, middle, near_state, outer1, side2):
    edge_rates, inner1 = near_state[:2], near_state[2:4]
    step_plane(prev1, prev2, p0, edge_rates[0], outer1[0])
    step_plane(next1, p2, next2, edge_rates[1], outer1[1])
    step_plane(inner1[0], outer1[0], middle, rates.at[0], side2[0])
    step_plane(inner1[1], middle, outer1[1], rates.at[2], side2[1])


def pair_kernel(
    chosen_any, classes_any, p0, p2, prev1, next1, prev2, next2, rates, middle, near_out, high_any, low_any,
    packed, chosen, classes, high, low, second, edge, fields, semaphores,
):
    copies = fetch(
        ((chosen_any, chosen), (classes_any, classes), (high_any, high), (low_any, low)), semaphores
    )
    near_state = groups(near_out, 5)
    edge_rates, inner1, middle2 = near_state[:2], near_state[2:4], near_state[4]
    outer1, side2 = groups(second, 2), groups(second, 2, 2 * GRAINS)
    second_step(p0, p2, prev1, next1, prev2, next2, rates, middle, near_state, outer1, side2)
    eta2 = (side2[0], middle2, side2[1])
    depth, width = p0.shape[1:]
    totals = [squares(state) for state in eta2]
    copies[0].wait()
    copies[1].wait()
    pair = pair_of(chosen)
    for side, (mid, near) in enumerate(((prev2, prev1), (next2, next1))):
        ids = grain_of(mid)
        total0 = squares(mid)
        total1 = squares(outer1[side])
        for k, i in enumerate(pair):
            first = update(mid[i], mid[GRAINS + k], near[i], total0, rate(classes, ids, i))
            edge[side, k] = update(outer1[side][i], first, inner1[side][i], total1, edge_rates[side][i])
    repeated = chosen[1] == chosen[0]
    for k in range(3):
        values = []
        for f, i in enumerate(pair):
            before = edge[0, f] if k == 0 else eta2[k - 1][i]
            after = edge[1, f] if k == 2 else eta2[k + 1][i]
            value = update(eta2[k][i], before, after, totals[k], rates[k, i])
            values.append(value)
        values[1] = jnp.where(repeated, values[0], values[1])
        for f in range(2):
            base = k * 2 * depth + f * depth
            fields[base : base + depth] = values[f]
    copies[2].wait()
    copies[3].wait()
    full = dot3((high[...], low[...]), split(fields[...]), ((1,), (1,)))
    slots = width // 2
    lanes = 4 * depth
    half = lanes // 2
    real_lane = lax.broadcasted_iota(jnp.int32, (slots, lanes), 1) < half
    for k in range(3):
        at = slice(k // 2 * lanes, k // 2 * lanes + lanes)
        cosine, sine = full[:slots, at], full[slots:, at]
        if k % 2:
            cosine = pltpu.roll(cosine, half, 1)
        else:
            sine = pltpu.roll(sine, half, 1)
        part = jnp.where(real_lane, cosine, sine)
        if packed.shape[0] == 3:
            packed[k] = part
        else:
            devices, rows, _ = packed.shape
            rows = rows // 3
            packed[:, k * rows : (k + 1) * rows, :] = part.reshape(devices, rows, lanes)


def rest_kernel(*refs):
    count = (len(refs) - 4) // 2
    sources, out, targets = refs[:count], refs[count], refs[count + 1 : 2 * count + 1]
    second, edge, semaphores = refs[-3:]
    copies = fetch(list(zip(sources, targets)), semaphores)
    chosen, classes, p0, p2, prev1, next1, prev2, next2, near_out, middle, rates, prev3, next3, prev4, next4 = targets
    near_state = groups(near_out, 5)
    edge_rates, inner1, middle2 = near_state[:2], near_state[2:4], near_state[4]
    outer1, side2 = groups(second, 2), groups(second, 2, 2 * GRAINS)
    for copy in copies:
        copy.wait()
    second_step(p0, p2, prev1, next1, prev2, next2, rates, middle, near_state, outer1, side2)
    other = others_of(chosen)
    pair = pair_of(chosen)
    places = [(pair[k], GRAINS + k, None) for k in range(2)] + [(other(r), None, r) for r in range(GRAINS - 2)]
    for side, (soon, far, mid, near) in enumerate(((prev3, prev4, prev2, prev1), (next3, next4, next2, next1))):
        ids = grain_of(mid)
        total0 = squares(mid)
        total1 = squares(outer1[side])
        for k, (i, early, late) in enumerate(places):
            if early is not None:
                third = mid[early]
            else:
                third = soon[late] if late < SOON else far[late - SOON]
            first = update(mid[i], third, near[i], total0, rate(classes, ids, i))
            edge[side, k] = update(outer1[side][i], first, inner1[side][i], total1, edge_rates[side][i])
    eta2 = (side2[0], middle2, side2[1])
    for plane in range(3):
        total = squares(eta2[plane])
        for k, (i, _, _) in enumerate(places):
            before = edge[0, k] if plane == 0 else eta2[plane - 1][i]
            after = edge[1, k] if plane == 2 else eta2[plane + 1][i]
            out[i, plane] = update(eta2[plane][i], before, after, total, rates[plane, i])


def line_kernel(lines, z_forward, z_inverse, x_both, out, wide, tall, scale):
    rows, lanes = lines.shape
    total_x = wide.shape[0] // 3
    slots = rows // total_x
    half = lanes // 2

    def over_x(pieces):
        for j, piece in enumerate(pieces):
            at = slice(j * lanes, (j + 1) * lanes)
            high, low = split(piece)
            wide[:total_x, at] = high
            wide[total_x : 2 * total_x, at] = low
            wide[2 * total_x :, at] = high
        both = jnp.dot(x_both[...], wide[...], preferred_element_type=F32)
        return both[:total_x], both[total_x:]

    def put(row, even, odd):
        at = slice(row * total_x, (row + 1) * total_x)
        for base, value in ((0, even), (lanes, odd)):
            high, low = split(value)
            tall[0, at, base : base + lanes] = high
            tall[1, at, base : base + lanes] = low

    real_lane = lax.broadcasted_iota(jnp.int32, (total_x, lanes), 1) < half
    even, odd = over_x([lines[pl.ds(j, total_x, stride=slots), :] for j in range(slots)])
    for j in range(slots):
        at = slice(j * lanes, (j + 1) * lanes)
        put(j, even[:, at], odd[:, at])
    first_even, first_odd = even[:, :lanes], odd[:, :lanes]
    put(slots, jnp.where(real_lane, first_even, 0.0), jnp.where(real_lane, first_odd, 0.0))
    put(
        slots + 1,
        jnp.where(real_lane, pltpu.roll(first_even, half, 1), 0.0),
        jnp.where(real_lane, pltpu.roll(first_odd, half, 1), 0.0),
    )
    spectrum = dot3((tall[0], tall[1]), (z_forward[0], z_forward[1]))
    spectrum = spectrum * spectrum
    spectrum = spectrum + pltpu.roll(spectrum, half, 1)

    def power(j):
        return spectrum[j * total_x : (j + 1) * total_x]

    first = lax.axis_index("gx") == 0
    lane = lax.broadcasted_iota(jnp.int32, (total_x, lanes), 1)
    line = lax.broadcasted_iota(jnp.int32, (total_x, lanes), 0)
    constant = jnp.logical_and(line == 0, jnp.logical_or(lane == 0, lane == half // 2))
    powers = []
    for j in range(slots):
        value = jnp.where(real_lane, power(j), 0.0) * (2.0 * scale)
        if j == 0:
            special = jnp.where(real_lane, power(slots), power(slots + 1)) * scale
            special = jnp.where(constant, 0.0, special)
            value = jnp.where(first, special, value)
        powers.append(value)
    even, odd = over_x(powers)
    for j in range(slots):
        at = slice(j * lanes, (j + 1) * lanes)
        put(j, even[:, at], odd[:, at])
    back = dot3((tall[0, :rows], tall[1, :rows]), (z_inverse[0], z_inverse[1]))
    for j in range(slots):
        out[pl.ds(j, total_x, stride=slots), :] = back[j * total_x : (j + 1) * total_x]


def finish_kernel(returned, high, low, out):
    fields, planes, depth, width = out.shape
    lanes = 2 * fields * depth
    half = lanes // 2
    slots = width // 2
    stacked = []
    for k in range(planes):
        if returned.shape[0] == planes:
            part = returned[k]
        else:
            devices, rows, _ = returned.shape
            rows = rows // planes
            part = returned[:, k * rows : (k + 1) * rows, :].reshape(slots, lanes)
        part = part.T
        stacked.append(jnp.concatenate([part[:half], part[half:]], axis=1))
    stacked = split(jnp.concatenate(stacked, axis=0))
    result = dot3(stacked, (high[...], low[...]))
    for k in range(planes):
        for f in range(fields):
            base = k * half + f * depth
            out[f, k] = result[base : base + depth]


def call(kernel, outs, in_specs, *args, scratch=(), flops=0, moved=0, limit=12):
    args = [pltpu.with_memory_space_constraint(a, pltpu.HBM) if b is ANY else a for a, b in zip(args, in_specs)]
    return pl.pallas_call(
        kernel,
        out_shape=outs,
        in_specs=in_specs,
        out_specs=jax.tree.map(lambda _: VMEM, outs),
        scratch_shapes=scratch,
        compiler_params=pltpu.CompilerParams(vmem_limit_bytes=limit * MIB),
        cost_estimate=pl.CostEstimate(flops=flops, bytes_accessed=moved, transcendentals=0),
    )(*args)


def shards(grain_ids, jitter, class_table, chosen):
    planes, depth, width = grain_ids.shape
    devices = lax.axis_size("gx")
    total_x = planes * devices
    count = float(total_x * depth * width)
    slots = width // 2
    share = slots // devices
    lanes = 4 * depth
    up = [(i, (i + 1) % devices) for i in range(devices)]
    down = [(j, i) for i, j in up]
    aligned = share % 8 == 0

    def shape(*dims):
        return jax.ShapeDtypeStruct(dims, F32)

    plane = (GRAINS, depth, width)
    table = [jnp.asarray(part) for part in halves(y_table(width))]
    z_forward, z_inverse = z_tables(depth)
    z_parts = [jnp.asarray(np.stack(halves(matrix))) for matrix in (z_forward, z_inverse)]
    x_high, x_low = halves(np.concatenate(phases(total_x), axis=0))
    x_both = jnp.asarray(np.concatenate([x_high, x_high, x_low], axis=1))

    two = (2, *plane)
    soon, last = (SOON, depth, width), (GRAINS - 2 - SOON, depth, width)
    small = [pltpu.SMEM((2,), jnp.int32), pltpu.SMEM((GRAINS, GRAINS), jnp.int32)]
    ten = (GRAINS + 2, depth, width)
    p0, p1, p2 = call(
        start_kernel,
        (shape(*plane), shape(*plane), shape(*plane)),
        [ANY] * 2,
        jitter, grain_ids,
        scratch=[
            pltpu.VMEM(jitter.shape, jitter.dtype),
            pltpu.VMEM(grain_ids.shape, jnp.int32),
            pltpu.SemaphoreType.DMA((2 * planes,)),
        ],
        flops=2**21, moved=2**22,
    )
    prev1 = lax.ppermute(p2, "gx", up)
    next1 = lax.ppermute(p0, "gx", down)
    up2, down2, r0, r2, l0, l2, rates, middle = call(
        inner_kernel,
        (
            shape(*ten), shape(*ten), shape(*soon), shape(*soon), shape(*last), shape(*last),
            shape(planes, *plane), shape(*plane),
        ),
        [ANY] * 2 + [VMEM] * 3,
        chosen, class_table, p0, p1, p2,
        scratch=[*small, pltpu.SemaphoreType.DMA((2,))],
        flops=2**24, moved=2**22,
    )
    prev2 = lax.ppermute(up2, "gx", up)
    next2 = lax.ppermute(down2, "gx", down)
    r0, r2, l0, l2, prev1, next1 = lax.optimization_barrier((r0, r2, l0, l2, prev1, next1))
    prev3 = lax.ppermute(r0, "gx", up)
    next3 = lax.ppermute(r2, "gx", down)
    near_out = call(
        near_kernel,
        shape(5 * GRAINS, depth, width),
        [ANY] + [VMEM] * 7,
        class_table, p0, p1, p2, prev1, next1, rates, middle,
        scratch=[small[1], pltpu.SemaphoreType.DMA((1,))],
        flops=2**25, moved=2**24,
    )
    packed_shape = (devices, planes * share, lanes) if aligned else (planes, slots, lanes)
    packed = call(
        pair_kernel,
        shape(*packed_shape),
        [ANY] * 2 + [VMEM] * 9 + [ANY] * 2,
        chosen, class_table, p0, p2, prev1, next1, prev2, next2, rates, middle, near_out, *table,
        scratch=[
            *small,
            pltpu.VMEM(table[0].shape, BF16),
            pltpu.VMEM(table[1].shape, BF16),
            pltpu.VMEM((4 * GRAINS, depth, width), F32),
            pltpu.VMEM((2, 2, depth, width), F32),
            pltpu.VMEM(((planes + 1) // 2 * lanes, width), F32),
            pltpu.SemaphoreType.DMA((4,)),
        ],
        flops=2**28, moved=2**23,
    )
    packed, prev3, next3 = lax.optimization_barrier((packed, prev3, next3))
    if aligned:
        lines = lax.all_to_all(packed, "gx", split_axis=0, concat_axis=0, tiled=True)
    else:
        lines = lax.all_to_all(packed, "gx", split_axis=1, concat_axis=0, tiled=True)
    lines = lines.reshape(total_x * share, lanes)
    lines, l0, l2 = lax.optimization_barrier((lines, l0, l2))
    prev4 = lax.ppermute(l0, "gx", up)
    next4 = lax.ppermute(l2, "gx", down)
    def lines_body(*refs):
        line_kernel(*refs, scale=1.0 / (count * count))

    back = call(
        lines_body,
        shape(total_x * share, lanes),
        [VMEM] * 4,
        lines, *z_parts, x_both,
        scratch=[
            pltpu.VMEM((3 * total_x, share * lanes), BF16),
            pltpu.VMEM((2, total_x * (share + 2), 2 * lanes), BF16),
        ],
        flops=2**28, moved=2**22,
    )
    back = back.reshape(devices, planes * share, lanes)
    returned = lax.all_to_all(back, "gx", split_axis=0, concat_axis=0, tiled=True)
    if not aligned:
        returned = returned.reshape(devices, planes, share, lanes).transpose(1, 0, 2, 3)
        returned = returned.reshape(planes, slots, lanes)
    late = (chosen, class_table, p0, p2, prev1, next1, prev2, next2, near_out, middle, rates, prev3, next3, prev4, next4)
    late, _ = lax.optimization_barrier((late, back))
    order_params = call(
        rest_kernel,
        shape(GRAINS, planes, depth, width),
        [ANY] * len(late),
        *late,
        scratch=[
            *small,
            *[pltpu.VMEM(value.shape, F32) for value in late[2:]],
            pltpu.VMEM((4 * GRAINS, depth, width), F32),
            pltpu.VMEM((2, *plane), F32),
            pltpu.SemaphoreType.DMA((len(late),)),
        ],
        flops=2**37, moved=2**24, limit=24,
    )
    correlation = call(
        finish_kernel,
        shape(2, planes, depth, width),
        [VMEM] * 3,
        returned, *table,
        flops=2**28, moved=2**22,
    )
    return (order_params, correlation)


def solution(mesh):
    in_specs = (P(("grp", "gx"), None, None), P(None, ("grp", "gx"), None, None), P(), P())
    out_specs = (P(None, ("grp", "gx"), None, None), P(None, ("grp", "gx"), None, None))
    return jax.shard_map(shards, mesh=mesh, in_specs=in_specs, out_specs=out_specs, check_vma=False)
```

```python
import math

import jax
import jax.numpy as jnp
import ml_dtypes
import numpy as np
from jax import lax
from jax.experimental import pallas as pl
from jax.experimental.pallas import tpu as pltpu
from jax.sharding import PartitionSpec as P

STEPS = 3
SOON = 3
GRAINS = 8
F32 = jnp.float32
BF16 = jnp.bfloat16
VMEM = pl.BlockSpec(memory_space=pltpu.VMEM)
ANY = pl.BlockSpec(memory_space=pltpu.HBM)
MIB = 2**20


def halves(table):
    table = np.asarray(table, np.float32)
    high = table.astype(ml_dtypes.bfloat16)
    low = (table - high.astype(np.float32)).astype(ml_dtypes.bfloat16)
    return high, low


def phases(length, rows=None):
    index = np.arange(length)
    product = np.arange(length if rows is None else rows)[:, None] * index[None, :] % length
    angle = product * (2.0 * math.pi / length)
    return np.cos(angle), np.sin(angle)


def y_table(width):
    cos_y, sin_y = phases(width, width // 2)
    sin_y = -sin_y
    sin_y[0] = 1.0 - 2.0 * (np.arange(width) % 2)
    return np.concatenate([cos_y, sin_y], axis=0)


def z_tables(depth):
    cos_z, sin_z = phases(depth)
    two = np.eye(2)
    cos_z, sin_z = np.kron(two, cos_z), np.kron(two, sin_z)
    forward = np.block([[cos_z, -sin_z], [sin_z, cos_z]])
    half = 2 * depth
    forward_turned = np.concatenate([forward[:, half:], -forward[:, :half]], axis=1)
    inverse = np.block([[cos_z, sin_z], [-sin_z, cos_z]])
    inverse_turned = np.concatenate([-inverse[:, half:], inverse[:, :half]], axis=1)
    return (
        np.concatenate([forward, forward_turned], axis=0),
        np.concatenate([inverse, inverse_turned], axis=0),
    )


def split(value):
    high = value.astype(BF16)
    low = (value - high.astype(F32)).astype(BF16)
    return high, low


def dot3(left, right, contract=((1,), (0,))):
    def one(a, b):
        return lax.dot_general(a, b, (contract, ((), ())), preferred_element_type=F32)

    return one(left[0], right[0]) + (one(left[0], right[1]) + one(left[1], right[0]))


def fetch(pairs, semaphores):
    copies = [pltpu.make_async_copy(src, dst, semaphores.at[k]) for k, (src, dst) in enumerate(pairs)]
    for copy in copies:
        copy.start()
    return copies


def pair_of(chosen):
    first, second = chosen[0], chosen[1]
    second = jnp.where(second == first, lax.rem(first + 1, GRAINS), second)
    return first, second


def others_of(chosen):
    first, second = pair_of(chosen)
    low, high = jnp.minimum(first, second), jnp.maximum(first, second)

    def other(r):
        i = jnp.where(r >= low, r + 1, r)
        return jnp.where(i >= high, i + 1, i)

    return other


def start_kernel(jitter_any, ids_any, p0, p1, p2, jitter, grain_ids, semaphores):
    planes = grain_ids.shape[0]
    pairs = []
    for k in range(planes):
        pairs.append((jitter_any.at[:, k], jitter.at[:, k]))
        pairs.append((ids_any.at[k], grain_ids.at[k]))
    copies = fetch(pairs, semaphores)
    for k, out in enumerate((p0, p1, p2)):
        copies[2 * k].wait()
        copies[2 * k + 1].wait()
        ids = grain_ids[k]
        for i in range(GRAINS):
            base = jnp.where(ids == i, jnp.float32(0.6), jnp.float32(0.0))
            out[i] = base + jitter[i, k].astype(F32)


def grain_of(start):
    ids = jnp.where(start[1] > 0.55, 1, 0)
    for g in range(2, GRAINS):
        ids = jnp.where(start[g] > 0.55, g, ids)
    return ids


def rate(classes, ids, i):
    def level(g):
        return 0.12 * (0.4 + 0.2 * classes[g, i].astype(F32))

    value = jnp.full(ids.shape, level(0), F32)
    for g in range(1, GRAINS):
        value = jnp.where(ids == g, level(g), value)
    return value


def squares(state):
    total = state[0] * state[0]
    for i in range(1, GRAINS):
        total = total + state[i] * state[i]
    return 5.0 + 3.0 * total


def update(e, before, after, total, mobility):
    depth, width = e.shape
    near = before + after
    near = near + (pltpu.roll(e, 1, 0) + pltpu.roll(e, depth - 1, 0))
    near = near + (pltpu.roll(e, 1, 1) + pltpu.roll(e, width - 1, 1))
    return e + mobility * (near - e * (total - 2.0 * (e * e)))


def step_plane(center, before, after, mobility, out):
    total = squares(center)
    for i in range(GRAINS):
        out[i] = update(center[i], before[i], after[i], total, mobility[i])


def rates_plane(classes, start, out):
    ids = grain_of(start)
    for i in range(GRAINS):
        out[i] = rate(classes, ids, i)


def inner_kernel(
    chosen_any, classes_any, p0, p1, p2, up2, down2, r0, r2, l0, l2, rates, middle, chosen, classes, semaphores
):
    copies = fetch(((chosen_any, chosen), (classes_any, classes)), semaphores)
    for i in range(GRAINS):
        up2[i] = p1[i]
        down2[i] = p1[i]
    for copy in copies:
        copy.wait()
    for k, i in enumerate(pair_of(chosen)):
        up2[GRAINS + k] = p0[i]
        down2[GRAINS + k] = p2[i]
    other = others_of(chosen)
    for r in range(GRAINS - 2):
        i = other(r)
        for soon, late, start in ((r0, l0, p0), (r2, l2, p2)):
            if r < SOON:
                soon[r] = start[i]
            else:
                late[r - SOON] = start[i]
    for k, start in enumerate((p0, p1, p2)):
        rates_plane(classes, start, rates.at[k])
    step_plane(p1, p0, p2, rates.at[1], middle)


def groups(ref, count, base=0):
    return [ref.at[pl.ds(base + k * GRAINS, GRAINS)] for k in range(count)]


def near_kernel(classes_any, p0, p1, p2, prev1, next1, rates, middle, near_out, classes, semaphores):
    edge0, edge1, inner0, inner2, middle2 = groups(near_out, 5)
    copies = fetch(((classes_any, classes),), semaphores)
    step_plane(p0, prev1, p1, rates.at[0], inner0)
    step_plane(p2, p1, next1, rates.at[2], inner2)
    copies[0].wait()
    rates_plane(classes, prev1, edge0)
    rates_plane(classes, next1, edge1)
    step_plane(middle, inner0, inner2, rates.at[1], middle2)


def second_step(p0, p2, prev1, next1, prev2, next2, rates, middle, near_state, outer1, side2):
    edge_rates, inner1 = near_state[:2], near_state[2:4]
    step_plane(prev1, prev2, p0, edge_rates[0], outer1[0])
    step_plane(next1, p2, next2, edge_rates[1], outer1[1])
    step_plane(inner1[0], outer1[0], middle, rates.at[0], side2[0])
    step_plane(inner1[1], middle, outer1[1], rates.at[2], side2[1])


def pair_kernel(
    chosen_any, classes_any, p0, p2, prev1, next1, prev2, next2, rates, middle, near_out, high_any, low_any,
    packed_any, chosen, classes, high, low, second, edge, fields, packed, semaphores,
):
    copies = fetch(
        ((chosen_any, chosen), (classes_any, classes), (high_any, high), (low_any, low)), semaphores
    )
    near_state = groups(near_out, 5)
    edge_rates, inner1, middle2 = near_state[:2], near_state[2:4], near_state[4]
    outer1, side2 = groups(second, 2), groups(second, 2, 2 * GRAINS)
    second_step(p0, p2, prev1, next1, prev2, next2, rates, middle, near_state, outer1, side2)
    eta2 = (side2[0], middle2, side2[1])
    depth, width = p0.shape[1:]
    totals = [squares(state) for state in eta2]
    copies[0].wait()
    copies[1].wait()
    pair = pair_of(chosen)
    for side, (mid, near) in enumerate(((prev2, prev1), (next2, next1))):
        ids = grain_of(mid)
        total0 = squares(mid)
        total1 = squares(outer1[side])
        for k, i in enumerate(pair):
            first = update(mid[i], mid[GRAINS + k], near[i], total0, rate(classes, ids, i))
            edge[side, k] = update(outer1[side][i], first, inner1[side][i], total1, edge_rates[side][i])
    repeated = chosen[1] == chosen[0]
    for k in range(3):
        values = []
        for f, i in enumerate(pair):
            before = edge[0, f] if k == 0 else eta2[k - 1][i]
            after = edge[1, f] if k == 2 else eta2[k + 1][i]
            value = update(eta2[k][i], before, after, totals[k], rates[k, i])
            values.append(value)
        values[1] = jnp.where(repeated, values[0], values[1])
        for f in range(2):
            base = k * 2 * depth + f * depth
            fields[base : base + depth] = values[f]
    copies[2].wait()
    copies[3].wait()
    full = dot3((high[...], low[...]), split(fields[...]), ((1,), (1,)))
    slots = width // 2
    lanes = 4 * depth
    half = lanes // 2
    real_lane = lax.broadcasted_iota(jnp.int32, (slots, lanes), 1) < half
    out_copies = []
    for k in range(3):
        at = slice(k // 2 * lanes, k // 2 * lanes + lanes)
        cosine, sine = full[:slots, at], full[slots:, at]
        if k % 2:
            cosine = pltpu.roll(cosine, half, 1)
        else:
            sine = pltpu.roll(sine, half, 1)
        part = jnp.where(real_lane, cosine, sine)
        if packed.shape[0] == 3:
            packed[k] = part
            piece = (packed.at[k], packed_any.at[k])
        else:
            devices, rows, _ = packed.shape
            rows = rows // 3
            at = slice(k * rows, (k + 1) * rows)
            packed[:, at, :] = part.reshape(devices, rows, lanes)
            piece = (packed.at[:, at], packed_any.at[:, at])
        out_copies += fetch((piece,), semaphores.at[pl.ds(4 + k, 1)])
    for copy in out_copies:
        copy.wait()


def rest_kernel(*refs):
    count = (len(refs) - 4) // 2
    sources, out, targets = refs[:count], refs[count], refs[count + 1 : 2 * count + 1]
    second, edge, semaphores = refs[-3:]
    copies = fetch(list(zip(sources, targets)), semaphores)
    chosen, classes, p0, p2, prev1, next1, prev2, next2, near_out, middle, rates, prev3, next3, prev4, next4 = targets
    near_state = groups(near_out, 5)
    edge_rates, inner1, middle2 = near_state[:2], near_state[2:4], near_state[4]
    outer1, side2 = groups(second, 2), groups(second, 2, 2 * GRAINS)
    for copy in copies:
        copy.wait()
    second_step(p0, p2, prev1, next1, prev2, next2, rates, middle, near_state, outer1, side2)
    other = others_of(chosen)
    pair = pair_of(chosen)
    places = [(pair[k], GRAINS + k, None) for k in range(2)] + [(other(r), None, r) for r in range(GRAINS - 2)]
    for side, (soon, far, mid, near) in enumerate(((prev3, prev4, prev2, prev1), (next3, next4, next2, next1))):
        ids = grain_of(mid)
        total0 = squares(mid)
        total1 = squares(outer1[side])
        for k, (i, early, late) in enumerate(places):
            if early is not None:
                third = mid[early]
            else:
                third = soon[late] if late < SOON else far[late - SOON]
            first = update(mid[i], third, near[i], total0, rate(classes, ids, i))
            edge[side, k] = update(outer1[side][i], first, inner1[side][i], total1, edge_rates[side][i])
    eta2 = (side2[0], middle2, side2[1])
    for plane in range(3):
        total = squares(eta2[plane])
        for k, (i, _, _) in enumerate(places):
            before = edge[0, k] if plane == 0 else eta2[plane - 1][i]
            after = edge[1, k] if plane == 2 else eta2[plane + 1][i]
            out[i, plane] = update(eta2[plane][i], before, after, total, rates[plane, i])


def line_kernel(lines, z_forward, z_inverse, x_both, out, wide, tall, scale):
    rows, lanes = lines.shape
    total_x = wide.shape[0] // 3
    slots = rows // total_x
    half = lanes // 2

    def over_x(pieces, chunk=2):
        results = []
        for j in range(0, slots, chunk):
            group = pieces[j : j + chunk]
            high, low = split(jnp.concatenate(group, axis=1))
            stacked = jnp.concatenate([high, low, high], axis=0)
            both = jnp.dot(x_both[...], stacked, preferred_element_type=F32)
            for k in range(len(group)):
                at = slice(k * lanes, (k + 1) * lanes)
                results.append((both[:total_x, at], both[total_x:, at]))
        return results

    def put(row, even, odd):
        at = slice(row * total_x, (row + 1) * total_x)
        for base, value in ((0, even), (lanes, odd)):
            high, low = split(value)
            tall[0, at, base : base + lanes] = high
            tall[1, at, base : base + lanes] = low

    real_lane = lax.broadcasted_iota(jnp.int32, (total_x, lanes), 1) < half
    turned = over_x([lines[pl.ds(j, total_x, stride=slots), :] for j in range(slots)])
    for j, (even, odd) in enumerate(turned):
        put(j, even, odd)
    first_even, first_odd = turned[0]
    put(slots, jnp.where(real_lane, first_even, 0.0), jnp.where(real_lane, first_odd, 0.0))
    put(
        slots + 1,
        jnp.where(real_lane, pltpu.roll(first_even, half, 1), 0.0),
        jnp.where(real_lane, pltpu.roll(first_odd, half, 1), 0.0),
    )
    step = 2 * total_x
    parts = []
    for row in range(0, (slots + 2) * total_x, step):
        at = slice(row, row + step)
        part = dot3((tall[0, at], tall[1, at]), (z_forward[0], z_forward[1]))
        part = part * part
        part = part + pltpu.roll(part, half, 1)
        parts += [part[:total_x], part[total_x:]]

    def power(j):
        return parts[j]

    first = lax.axis_index("gx") == 0
    lane = lax.broadcasted_iota(jnp.int32, (total_x, lanes), 1)
    line = lax.broadcasted_iota(jnp.int32, (total_x, lanes), 0)
    constant = jnp.logical_and(line == 0, jnp.logical_or(lane == 0, lane == half // 2))
    powers = []
    for j in range(slots):
        value = jnp.where(real_lane, power(j), 0.0) * (2.0 * scale)
        if j == 0:
            special = jnp.where(real_lane, power(slots), power(slots + 1)) * scale
            special = jnp.where(constant, 0.0, special)
            value = jnp.where(first, special, value)
        powers.append(value)
    for j, (even, odd) in enumerate(over_x(powers)):
        put(j, even, odd)
    for j in range(0, slots, 2):
        at = slice(j * total_x, (j + 2) * total_x)
        back = dot3((tall[0, at], tall[1, at]), (z_inverse[0], z_inverse[1]))
        out[pl.ds(j, total_x, stride=slots), :] = back[:total_x]
        out[pl.ds(j + 1, total_x, stride=slots), :] = back[total_x:]


def finish_kernel(returned, high, low, out_any, out, semaphores):
    fields, planes, depth, width = out.shape
    lanes = 2 * fields * depth
    half = lanes // 2
    slots = width // 2
    stacked = []
    for k in range(planes):
        if returned.shape[0] == planes:
            part = returned[k]
        else:
            devices, rows, _ = returned.shape
            rows = rows // planes
            part = returned[:, k * rows : (k + 1) * rows, :].reshape(slots, lanes)
        part = part.T
        stacked.append(jnp.concatenate([part[:half], part[half:]], axis=1))
    stacked = split(jnp.concatenate(stacked, axis=0))
    copies = []
    for piece in range(2):
        at = slice(piece * slots, (piece + 1) * slots)
        result = dot3(stacked, (high[:, at], low[:, at]))
        for k in range(planes):
            for f in range(fields):
                base = k * half + f * depth
                out[f, k, :, at] = result[base : base + depth]
        copies += fetch(((out.at[:, :, :, at], out_any.at[:, :, :, at]),), semaphores.at[pl.ds(piece, 1)])
    for copy in copies:
        copy.wait()


def call(kernel, outs, in_specs, *args, scratch=(), flops=0, moved=0, limit=12, out_specs=None):
    args = [pltpu.with_memory_space_constraint(a, pltpu.HBM) if b is ANY else a for a, b in zip(args, in_specs)]
    return pl.pallas_call(
        kernel,
        out_shape=outs,
        in_specs=in_specs,
        out_specs=out_specs or jax.tree.map(lambda _: VMEM, outs),
        scratch_shapes=scratch,
        compiler_params=pltpu.CompilerParams(vmem_limit_bytes=limit * MIB),
        cost_estimate=pl.CostEstimate(flops=flops, bytes_accessed=moved, transcendentals=0),
    )(*args)


def shards(grain_ids, jitter, class_table, chosen):
    planes, depth, width = grain_ids.shape
    devices = lax.axis_size("gx")
    total_x = planes * devices
    count = float(total_x * depth * width)
    slots = width // 2
    share = slots // devices
    lanes = 4 * depth
    up = [(i, (i + 1) % devices) for i in range(devices)]
    down = [(j, i) for i, j in up]
    aligned = share % 8 == 0

    def shape(*dims):
        return jax.ShapeDtypeStruct(dims, F32)

    plane = (GRAINS, depth, width)
    table = [jnp.asarray(part) for part in halves(y_table(width))]
    z_forward, z_inverse = z_tables(depth)
    z_parts = [jnp.asarray(np.stack(halves(matrix))) for matrix in (z_forward, z_inverse)]
    x_high, x_low = halves(np.concatenate(phases(total_x), axis=0))
    x_both = jnp.asarray(np.concatenate([x_high, x_high, x_low], axis=1))

    two = (2, *plane)
    soon, last = (SOON, depth, width), (GRAINS - 2 - SOON, depth, width)
    small = [pltpu.SMEM((2,), jnp.int32), pltpu.SMEM((GRAINS, GRAINS), jnp.int32)]
    ten = (GRAINS + 2, depth, width)
    p0, p1, p2 = call(
        start_kernel,
        (shape(*plane), shape(*plane), shape(*plane)),
        [ANY] * 2,
        jitter, grain_ids,
        scratch=[
            pltpu.VMEM(jitter.shape, jitter.dtype),
            pltpu.VMEM(grain_ids.shape, jnp.int32),
            pltpu.SemaphoreType.DMA((2 * planes,)),
        ],
        flops=2**21, moved=2**22,
    )
    prev1 = lax.ppermute(p2, "gx", up)
    next1 = lax.ppermute(p0, "gx", down)
    up2, down2, r0, r2, l0, l2, rates, middle = call(
        inner_kernel,
        (
            shape(*ten), shape(*ten), shape(*soon), shape(*soon), shape(*last), shape(*last),
            shape(planes, *plane), shape(*plane),
        ),
        [ANY] * 2 + [VMEM] * 3,
        chosen, class_table, p0, p1, p2,
        scratch=[*small, pltpu.SemaphoreType.DMA((2,))],
        flops=2**24, moved=2**22,
    )
    prev2 = lax.ppermute(up2, "gx", up)
    next2 = lax.ppermute(down2, "gx", down)
    near_out = call(
        near_kernel,
        shape(5 * GRAINS, depth, width),
        [ANY] + [VMEM] * 7,
        class_table, p0, p1, p2, prev1, next1, rates, middle,
        scratch=[small[1], pltpu.SemaphoreType.DMA((1,))],
        flops=2**25, moved=2**24,
    )
    r0, r2, l0, l2, near_out = lax.optimization_barrier((r0, r2, l0, l2, near_out))
    prev3 = lax.ppermute(r0, "gx", up)
    next3 = lax.ppermute(r2, "gx", down)
    prev4 = lax.ppermute(l0, "gx", up)
    next4 = lax.ppermute(l2, "gx", down)
    packed_shape = (devices, planes * share, lanes) if aligned else (planes, slots, lanes)
    packed = call(
        pair_kernel,
        shape(*packed_shape),
        [ANY] * 2 + [VMEM] * 9 + [ANY] * 2,
        chosen, class_table, p0, p2, prev1, next1, prev2, next2, rates, middle, near_out, *table,
        scratch=[
            *small,
            pltpu.VMEM(table[0].shape, BF16),
            pltpu.VMEM(table[1].shape, BF16),
            pltpu.VMEM((4 * GRAINS, depth, width), F32),
            pltpu.VMEM((2, 2, depth, width), F32),
            pltpu.VMEM(((planes + 1) // 2 * lanes, width), F32),
            pltpu.VMEM(packed_shape, F32),
            pltpu.SemaphoreType.DMA((4 + planes,)),
        ],
        out_specs=ANY, flops=2**28, moved=2**23,
    )
    packed, prev3, next3 = lax.optimization_barrier((packed, prev3, next3))
    if aligned:
        lines = lax.all_to_all(packed, "gx", split_axis=0, concat_axis=0, tiled=True)
    else:
        lines = lax.all_to_all(packed, "gx", split_axis=1, concat_axis=0, tiled=True)
    lines = lines.reshape(total_x * share, lanes)
    lines, prev4, next4 = lax.optimization_barrier((lines, prev4, next4))
    def lines_body(*refs):
        line_kernel(*refs, scale=1.0 / (count * count))

    back = call(
        lines_body,
        shape(total_x * share, lanes),
        [VMEM] * 4,
        lines, *z_parts, x_both,
        scratch=[
            pltpu.VMEM((3 * total_x, share * lanes), BF16),
            pltpu.VMEM((2, total_x * (share + 2), 2 * lanes), BF16),
        ],
        flops=2**28, moved=2**22,
    )
    back = back.reshape(devices, planes * share, lanes)
    returned = lax.all_to_all(back, "gx", split_axis=0, concat_axis=0, tiled=True)
    if not aligned:
        returned = returned.reshape(devices, planes, share, lanes).transpose(1, 0, 2, 3)
        returned = returned.reshape(planes, slots, lanes)
    late = (chosen, class_table, p0, p2, prev1, next1, prev2, next2, near_out, middle, rates, prev3, next3, prev4, next4)
    late, _ = lax.optimization_barrier((late, back))
    order_params = call(
        rest_kernel,
        shape(GRAINS, planes, depth, width),
        [ANY] * len(late),
        *late,
        scratch=[
            *small,
            *[pltpu.VMEM(value.shape, F32) for value in late[2:]],
            pltpu.VMEM((4 * GRAINS, depth, width), F32),
            pltpu.VMEM((2, *plane), F32),
            pltpu.SemaphoreType.DMA((len(late),)),
        ],
        flops=2**26, moved=2**24, limit=24,
    )
    correlation = call(
        finish_kernel,
        shape(2, planes, depth, width),
        [VMEM] * 3,
        returned, *table,
        scratch=[pltpu.VMEM((2, planes, depth, width), F32), pltpu.SemaphoreType.DMA((2,))],
        out_specs=ANY,
        flops=2**28, moved=2**22,
    )
    return (order_params, correlation)


def solution(mesh):
    in_specs = (P(("grp", "gx"), None, None), P(None, ("grp", "gx"), None, None), P(), P())
    out_specs = (P(None, ("grp", "gx"), None, None), P(None, ("grp", "gx"), None, None))
    return jax.shard_map(shards, mesh=mesh, in_specs=in_specs, out_specs=out_specs, check_vma=False)
```

```python
import math

import jax
import jax.numpy as jnp
import ml_dtypes
import numpy as np
from jax import lax
from jax.experimental import pallas as pl
from jax.experimental.pallas import tpu as pltpu
from jax.sharding import PartitionSpec as P

STEPS = 3
SOON = 3
GRAINS = 8
F32 = jnp.float32
BF16 = jnp.bfloat16
VMEM = pl.BlockSpec(memory_space=pltpu.VMEM)
ANY = pl.BlockSpec(memory_space=pltpu.HBM)
MIB = 2**20


def halves(table):
    table = np.asarray(table, np.float32)
    high = table.astype(ml_dtypes.bfloat16)
    low = (table - high.astype(np.float32)).astype(ml_dtypes.bfloat16)
    return high, low


def phases(length, rows=None):
    index = np.arange(length)
    product = np.arange(length if rows is None else rows)[:, None] * index[None, :] % length
    angle = product * (2.0 * math.pi / length)
    return np.cos(angle), np.sin(angle)


def y_table(width):
    cos_y, sin_y = phases(width, width // 2)
    sin_y = -sin_y
    sin_y[0] = 1.0 - 2.0 * (np.arange(width) % 2)
    return np.concatenate([cos_y, sin_y], axis=0)


def z_tables(depth):
    cos_z, sin_z = phases(depth)
    two = np.eye(2)
    cos_z, sin_z = np.kron(two, cos_z), np.kron(two, sin_z)
    forward = np.block([[cos_z, -sin_z], [sin_z, cos_z]])
    half = 2 * depth
    forward_turned = np.concatenate([forward[:, half:], -forward[:, :half]], axis=1)
    inverse = np.block([[cos_z, sin_z], [-sin_z, cos_z]])
    inverse_turned = np.concatenate([-inverse[:, half:], inverse[:, :half]], axis=1)
    return (
        np.concatenate([forward, forward_turned], axis=0),
        np.concatenate([inverse, inverse_turned], axis=0),
    )


def split(value):
    high = value.astype(BF16)
    low = (value - high.astype(F32)).astype(BF16)
    return high, low


def dot3(left, right, contract=((1,), (0,))):
    def one(a, b):
        return lax.dot_general(a, b, (contract, ((), ())), preferred_element_type=F32)

    return one(left[0], right[0]) + (one(left[0], right[1]) + one(left[1], right[0]))


def fetch(pairs, semaphores):
    copies = [pltpu.make_async_copy(src, dst, semaphores.at[k]) for k, (src, dst) in enumerate(pairs)]
    for copy in copies:
        copy.start()
    return copies


def pair_of(chosen):
    first, second = chosen[0], chosen[1]
    second = jnp.where(second == first, lax.rem(first + 1, GRAINS), second)
    return first, second


def others_of(chosen):
    first, second = pair_of(chosen)
    low, high = jnp.minimum(first, second), jnp.maximum(first, second)

    def other(r):
        i = jnp.where(r >= low, r + 1, r)
        return jnp.where(i >= high, i + 1, i)

    return other


def start_kernel(jitter_any, ids_any, p0, p1, p2, jitter, grain_ids, semaphores):
    planes = grain_ids.shape[0]
    pairs = []
    for k in range(planes):
        pairs.append((jitter_any.at[:, k], jitter.at[:, k]))
        pairs.append((ids_any.at[k], grain_ids.at[k]))
    copies = fetch(pairs, semaphores)
    for k, out in enumerate((p0, p1, p2)):
        copies[2 * k].wait()
        copies[2 * k + 1].wait()
        ids = grain_ids[k]
        for i in range(GRAINS):
            base = jnp.where(ids == i, jnp.float32(0.6), jnp.float32(0.0))
            out[i] = base + jitter[i, k].astype(F32)


def grain_of(start):
    ids = jnp.where(start[1] > 0.55, 1, 0)
    for g in range(2, GRAINS):
        ids = jnp.where(start[g] > 0.55, g, ids)
    return ids


def rate(classes, ids, i):
    def level(g):
        return 0.12 * (0.4 + 0.2 * classes[g, i].astype(F32))

    value = jnp.full(ids.shape, level(0), F32)
    for g in range(1, GRAINS):
        value = jnp.where(ids == g, level(g), value)
    return value


def squares(state):
    total = state[0] * state[0]
    for i in range(1, GRAINS):
        total = total + state[i] * state[i]
    return 5.0 + 3.0 * total


def update(e, before, after, total, mobility):
    depth, width = e.shape
    near = before + after
    near = near + (pltpu.roll(e, 1, 0) + pltpu.roll(e, depth - 1, 0))
    near = near + (pltpu.roll(e, 1, 1) + pltpu.roll(e, width - 1, 1))
    return e + mobility * (near - e * (total - 2.0 * (e * e)))


def step_plane(center, before, after, mobility, out):
    total = squares(center)
    for i in range(GRAINS):
        out[i] = update(center[i], before[i], after[i], total, mobility[i])


def rates_plane(classes, start, out):
    ids = grain_of(start)
    for i in range(GRAINS):
        out[i] = rate(classes, ids, i)


def inner_kernel(
    chosen_any, classes_any, p0, p1, p2, up2, down2, r0, r2, l0, l2, rates, middle, chosen, classes, semaphores
):
    copies = fetch(((chosen_any, chosen), (classes_any, classes)), semaphores)
    for i in range(GRAINS):
        up2[i] = p1[i]
        down2[i] = p1[i]
    for copy in copies:
        copy.wait()
    for k, i in enumerate(pair_of(chosen)):
        up2[GRAINS + k] = p0[i]
        down2[GRAINS + k] = p2[i]
    other = others_of(chosen)
    for r in range(GRAINS - 2):
        i = other(r)
        for soon, late, start in ((r0, l0, p0), (r2, l2, p2)):
            if r < SOON:
                soon[r] = start[i]
            else:
                late[r - SOON] = start[i]
    for k, start in enumerate((p0, p1, p2)):
        rates_plane(classes, start, rates.at[k])
    step_plane(p1, p0, p2, rates.at[1], middle)


def groups(ref, count, base=0):
    return [ref.at[pl.ds(base + k * GRAINS, GRAINS)] for k in range(count)]


def near_kernel(classes_any, p0, p1, p2, prev1, next1, rates, middle, near_out, classes, semaphores):
    edge0, edge1, inner0, inner2, middle2 = groups(near_out, 5)
    copies = fetch(((classes_any, classes),), semaphores)
    step_plane(p0, prev1, p1, rates.at[0], inner0)
    step_plane(p2, p1, next1, rates.at[2], inner2)
    copies[0].wait()
    rates_plane(classes, prev1, edge0)
    rates_plane(classes, next1, edge1)
    step_plane(middle, inner0, inner2, rates.at[1], middle2)


def second_step(p0, p2, prev1, next1, prev2, next2, rates, middle, near_state, outer1, side2):
    edge_rates, inner1 = near_state[:2], near_state[2:4]
    step_plane(prev1, prev2, p0, edge_rates[0], outer1[0])
    step_plane(next1, p2, next2, edge_rates[1], outer1[1])
    step_plane(inner1[0], outer1[0], middle, rates.at[0], side2[0])
    step_plane(inner1[1], middle, outer1[1], rates.at[2], side2[1])


def pair_kernel(
    chosen_any, classes_any, p0, p2, prev1, next1, prev2, next2, rates, middle, near_out, high_any, low_any,
    packed, chosen, classes, high, low, second, edge, fields, semaphores,
):
    copies = fetch(
        ((chosen_any, chosen), (classes_any, classes), (high_any, high), (low_any, low)), semaphores
    )
    near_state = groups(near_out, 5)
    edge_rates, inner1, middle2 = near_state[:2], near_state[2:4], near_state[4]
    outer1, side2 = groups(second, 2), groups(second, 2, 2 * GRAINS)
    second_step(p0, p2, prev1, next1, prev2, next2, rates, middle, near_state, outer1, side2)
    eta2 = (side2[0], middle2, side2[1])
    depth, width = p0.shape[1:]
    totals = [squares(state) for state in eta2]
    copies[0].wait()
    copies[1].wait()
    pair = pair_of(chosen)
    for side, (mid, near) in enumerate(((prev2, prev1), (next2, next1))):
        ids = grain_of(mid)
        total0 = squares(mid)
        total1 = squares(outer1[side])
        for k, i in enumerate(pair):
            first = update(mid[i], mid[GRAINS + k], near[i], total0, rate(classes, ids, i))
            edge[side, k] = update(outer1[side][i], first, inner1[side][i], total1, edge_rates[side][i])
    repeated = chosen[1] == chosen[0]
    for k in range(3):
        values = []
        for f, i in enumerate(pair):
            before = edge[0, f] if k == 0 else eta2[k - 1][i]
            after = edge[1, f] if k == 2 else eta2[k + 1][i]
            value = update(eta2[k][i], before, after, totals[k], rates[k, i])
            values.append(value)
        values[1] = jnp.where(repeated, values[0], values[1])
        for f in range(2):
            base = k * 2 * depth + f * depth
            fields[base : base + depth] = values[f]
    copies[2].wait()
    copies[3].wait()
    full = dot3((high[...], low[...]), split(fields[...]), ((1,), (1,)))
    slots = width // 2
    lanes = 4 * depth
    half = lanes // 2
    real_lane = lax.broadcasted_iota(jnp.int32, (slots, lanes), 1) < half
    for k in range(3):
        at = slice(k // 2 * lanes, k // 2 * lanes + lanes)
        cosine, sine = full[:slots, at], full[slots:, at]
        if k % 2:
            cosine = pltpu.roll(cosine, half, 1)
        else:
            sine = pltpu.roll(sine, half, 1)
        part = jnp.where(real_lane, cosine, sine)
        if packed.shape[0] == 3:
            packed[k] = part
        else:
            devices, rows, _ = packed.shape
            rows = rows // 3
            packed[:, k * rows : (k + 1) * rows, :] = part.reshape(devices, rows, lanes)


def rest_kernel(
    prev3, next3, prev4, next4,
    chosen_any, classes_any, p0_any, p2_any, prev1_any, next1_any, prev2_any, next2_any, near_any, middle_any,
    rates_any, out_any,
    chosen, classes, p0, p2, prev1, next1, prev2, next2, near_out, middle, rates, second, edge, out, semaphores,
):
    near_state, near_source = groups(near_out, 5), groups(near_any, 5)
    edge_rates, inner1, middle2 = near_state[:2], near_state[2:4], near_state[4]
    outer1, side2 = groups(second, 2), groups(second, 2, 2 * GRAINS)
    copies = fetch(
        (
            (prev1_any, prev1), (prev2_any, prev2), (p0_any, p0), (near_source[0], near_state[0]),
            (next1_any, next1), (next2_any, next2), (p2_any, p2), (near_source[1], near_state[1]),
            (near_source[2], near_state[2]), (middle_any, middle), (rates_any.at[0], rates.at[0]),
            (near_source[3], near_state[3]), (rates_any.at[2], rates.at[2]),
            (chosen_any, chosen), (classes_any, classes),
            (near_source[4], near_state[4]), (rates_any.at[1], rates.at[1]),
        ),
        semaphores,
    )

    def wait(first, last):
        for copy in copies[first:last]:
            copy.wait()

    wait(0, 4)
    step_plane(prev1, prev2, p0, edge_rates[0], outer1[0])
    wait(4, 8)
    step_plane(next1, p2, next2, edge_rates[1], outer1[1])
    wait(8, 11)
    step_plane(inner1[0], outer1[0], middle, rates.at[0], side2[0])
    wait(11, 13)
    step_plane(inner1[1], middle, outer1[1], rates.at[2], side2[1])
    wait(13, 17)
    other = others_of(chosen)
    pair = pair_of(chosen)
    places = [(pair[k], GRAINS + k, None) for k in range(2)] + [(other(r), None, r) for r in range(GRAINS - 2)]
    eta2 = (side2[0], middle2, side2[1])
    outs = []

    def finish(plane):
        total = squares(eta2[plane])
        for k, (i, _, _) in enumerate(places):
            before = edge[0, k] if plane == 0 else eta2[plane - 1][i]
            after = edge[1, k] if plane == 2 else eta2[plane + 1][i]
            out[i, plane] = update(eta2[plane][i], before, after, total, rates[plane, i])
        outs.extend(fetch(((out.at[:, plane], out_any.at[:, plane]),), semaphores.at[pl.ds(17 + plane, 1)]))

    finish(1)
    for side, (soon, far, mid, near) in enumerate(((prev3, prev4, prev2, prev1), (next3, next4, next2, next1))):
        ids = grain_of(mid)
        total0 = squares(mid)
        total1 = squares(outer1[side])
        for k, (i, early, late) in enumerate(places):
            if early is not None:
                third = mid[early]
            else:
                third = soon[late] if late < SOON else far[late - SOON]
            first = update(mid[i], third, near[i], total0, rate(classes, ids, i))
            edge[side, k] = update(outer1[side][i], first, inner1[side][i], total1, edge_rates[side][i])
        finish(2 * side)
    for copy in outs:
        copy.wait()


def line_kernel(lines, z_forward, z_inverse, x_both, out, wide, tall, scale):
    rows, lanes = lines.shape
    total_x = wide.shape[0] // 3
    slots = rows // total_x
    half = lanes // 2

    def over_x(pieces, chunk=2):
        results = []
        for j in range(0, slots, chunk):
            group = pieces[j : j + chunk]
            high, low = split(jnp.concatenate(group, axis=1))
            stacked = jnp.concatenate([high, low, high], axis=0)
            both = jnp.dot(x_both[...], stacked, preferred_element_type=F32)
            for k in range(len(group)):
                at = slice(k * lanes, (k + 1) * lanes)
                results.append((both[:total_x, at], both[total_x:, at]))
        return results

    def put(row, even, odd):
        at = slice(row * total_x, (row + 1) * total_x)
        for base, value in ((0, even), (lanes, odd)):
            high, low = split(value)
            tall[0, at, base : base + lanes] = high
            tall[1, at, base : base + lanes] = low

    real_lane = lax.broadcasted_iota(jnp.int32, (total_x, lanes), 1) < half
    turned = over_x([lines[pl.ds(j, total_x, stride=slots), :] for j in range(slots)])
    for j, (even, odd) in enumerate(turned):
        put(j, even, odd)
    first_even, first_odd = turned[0]
    put(slots, jnp.where(real_lane, first_even, 0.0), jnp.where(real_lane, first_odd, 0.0))
    put(
        slots + 1,
        jnp.where(real_lane, pltpu.roll(first_even, half, 1), 0.0),
        jnp.where(real_lane, pltpu.roll(first_odd, half, 1), 0.0),
    )
    step = 2 * total_x
    parts = []
    for row in range(0, (slots + 2) * total_x, step):
        at = slice(row, row + step)
        part = dot3((tall[0, at], tall[1, at]), (z_forward[0], z_forward[1]))
        part = part * part
        part = part + pltpu.roll(part, half, 1)
        parts += [part[:total_x], part[total_x:]]

    def power(j):
        return parts[j]

    first = lax.axis_index("gx") == 0
    lane = lax.broadcasted_iota(jnp.int32, (total_x, lanes), 1)
    line = lax.broadcasted_iota(jnp.int32, (total_x, lanes), 0)
    constant = jnp.logical_and(line == 0, jnp.logical_or(lane == 0, lane == half // 2))
    powers = []
    for j in range(slots):
        value = jnp.where(real_lane, power(j), 0.0) * (2.0 * scale)
        if j == 0:
            special = jnp.where(real_lane, power(slots), power(slots + 1)) * scale
            special = jnp.where(constant, 0.0, special)
            value = jnp.where(first, special, value)
        powers.append(value)
    for j, (even, odd) in enumerate(over_x(powers)):
        put(j, even, odd)
    for j in range(0, slots, 2):
        at = slice(j * total_x, (j + 2) * total_x)
        back = dot3((tall[0, at], tall[1, at]), (z_inverse[0], z_inverse[1]))
        out[pl.ds(j, total_x, stride=slots), :] = back[:total_x]
        out[pl.ds(j + 1, total_x, stride=slots), :] = back[total_x:]


def finish_kernel(returned, high, low, out_any, out, semaphores):
    fields, planes, depth, width = out.shape
    lanes = 2 * fields * depth
    half = lanes // 2
    slots = width // 2
    stacked = []
    for k in range(planes):
        if returned.shape[0] == planes:
            part = returned[k]
        else:
            devices, rows, _ = returned.shape
            rows = rows // planes
            part = returned[:, k * rows : (k + 1) * rows, :].reshape(slots, lanes)
        part = part.T
        stacked.append(jnp.concatenate([part[:half], part[half:]], axis=1))
    stacked = split(jnp.concatenate(stacked, axis=0))
    copies = []
    for piece in range(2):
        at = slice(piece * slots, (piece + 1) * slots)
        result = dot3(stacked, (high[:, at], low[:, at]))
        for k in range(planes):
            for f in range(fields):
                base = k * half + f * depth
                out[f, k, :, at] = result[base : base + depth]
        copies += fetch(((out.at[:, :, :, at], out_any.at[:, :, :, at]),), semaphores.at[pl.ds(piece, 1)])
    for copy in copies:
        copy.wait()


def call(kernel, outs, in_specs, *args, scratch=(), flops=0, moved=0, limit=12, out_specs=None):
    args = [pltpu.with_memory_space_constraint(a, pltpu.HBM) if b is ANY else a for a, b in zip(args, in_specs)]
    return pl.pallas_call(
        kernel,
        out_shape=outs,
        in_specs=in_specs,
        out_specs=out_specs or jax.tree.map(lambda _: VMEM, outs),
        scratch_shapes=scratch,
        compiler_params=pltpu.CompilerParams(vmem_limit_bytes=limit * MIB),
        cost_estimate=pl.CostEstimate(flops=flops, bytes_accessed=moved, transcendentals=0),
    )(*args)


def shards(grain_ids, jitter, class_table, chosen):
    planes, depth, width = grain_ids.shape
    devices = lax.axis_size("gx")
    total_x = planes * devices
    count = float(total_x * depth * width)
    slots = width // 2
    share = slots // devices
    lanes = 4 * depth
    up = [(i, (i + 1) % devices) for i in range(devices)]
    down = [(j, i) for i, j in up]
    aligned = share % 8 == 0

    def shape(*dims):
        return jax.ShapeDtypeStruct(dims, F32)

    plane = (GRAINS, depth, width)
    table = [jnp.asarray(part) for part in halves(y_table(width))]
    z_forward, z_inverse = z_tables(depth)
    z_parts = [jnp.asarray(np.stack(halves(matrix))) for matrix in (z_forward, z_inverse)]
    x_high, x_low = halves(np.concatenate(phases(total_x), axis=0))
    x_both = jnp.asarray(np.concatenate([x_high, x_high, x_low], axis=1))

    two = (2, *plane)
    soon, last = (SOON, depth, width), (GRAINS - 2 - SOON, depth, width)
    small = [pltpu.SMEM((2,), jnp.int32), pltpu.SMEM((GRAINS, GRAINS), jnp.int32)]
    ten = (GRAINS + 2, depth, width)
    p0, p1, p2 = call(
        start_kernel,
        (shape(*plane), shape(*plane), shape(*plane)),
        [ANY] * 2,
        jitter, grain_ids,
        scratch=[
            pltpu.VMEM(jitter.shape, jitter.dtype),
            pltpu.VMEM(grain_ids.shape, jnp.int32),
            pltpu.SemaphoreType.DMA((2 * planes,)),
        ],
        flops=2**21, moved=2**22,
    )
    prev1 = lax.ppermute(p2, "gx", up)
    next1 = lax.ppermute(p0, "gx", down)
    up2, down2, r0, r2, l0, l2, rates, middle = call(
        inner_kernel,
        (
            shape(*ten), shape(*ten), shape(*soon), shape(*soon), shape(*last), shape(*last),
            shape(planes, *plane), shape(*plane),
        ),
        [ANY] * 2 + [VMEM] * 3,
        chosen, class_table, p0, p1, p2,
        scratch=[*small, pltpu.SemaphoreType.DMA((2,))],
        flops=2**24, moved=2**22,
    )
    prev2 = lax.ppermute(up2, "gx", up)
    next2 = lax.ppermute(down2, "gx", down)
    near_out = call(
        near_kernel,
        shape(5 * GRAINS, depth, width),
        [ANY] + [VMEM] * 7,
        class_table, p0, p1, p2, prev1, next1, rates, middle,
        scratch=[small[1], pltpu.SemaphoreType.DMA((1,))],
        flops=2**25, moved=2**24,
    )
    r0, r2, near_out = lax.optimization_barrier((r0, r2, near_out))
    prev3 = lax.ppermute(r0, "gx", up)
    next3 = lax.ppermute(r2, "gx", down)
    packed_shape = (devices, planes * share, lanes) if aligned else (planes, slots, lanes)
    packed = call(
        pair_kernel,
        shape(*packed_shape),
        [ANY] * 2 + [VMEM] * 9 + [ANY] * 2,
        chosen, class_table, p0, p2, prev1, next1, prev2, next2, rates, middle, near_out, *table,
        scratch=[
            *small,
            pltpu.VMEM(table[0].shape, BF16),
            pltpu.VMEM(table[1].shape, BF16),
            pltpu.VMEM((4 * GRAINS, depth, width), F32),
            pltpu.VMEM((2, 2, depth, width), F32),
            pltpu.VMEM(((planes + 1) // 2 * lanes, width), F32),
            pltpu.SemaphoreType.DMA((4,)),
        ],
        flops=2**28, moved=2**23,
    )
    packed, prev3, next3 = lax.optimization_barrier((packed, prev3, next3))
    if aligned:
        lines = lax.all_to_all(packed, "gx", split_axis=0, concat_axis=0, tiled=True)
    else:
        lines = lax.all_to_all(packed, "gx", split_axis=1, concat_axis=0, tiled=True)
    lines = lines.reshape(total_x * share, lanes)
    lines, l0, l2 = lax.optimization_barrier((lines, l0, l2))
    prev4 = lax.ppermute(l0, "gx", up)
    next4 = lax.ppermute(l2, "gx", down)
    def lines_body(*refs):
        line_kernel(*refs, scale=1.0 / (count * count))

    back = call(
        lines_body,
        shape(total_x * share, lanes),
        [VMEM] * 4,
        lines, *z_parts, x_both,
        scratch=[
            pltpu.VMEM((3 * total_x, share * lanes), BF16),
            pltpu.VMEM((2, total_x * (share + 2), 2 * lanes), BF16),
        ],
        flops=2**28, moved=2**22,
    )
    back = back.reshape(devices, planes * share, lanes)
    returned = lax.all_to_all(back, "gx", split_axis=0, concat_axis=0, tiled=True)
    if not aligned:
        returned = returned.reshape(devices, planes, share, lanes).transpose(1, 0, 2, 3)
        returned = returned.reshape(planes, slots, lanes)
    late = (
        prev3, next3, prev4, next4,
        chosen, class_table, p0, p2, prev1, next1, prev2, next2, near_out, middle, rates,
    )
    late, _ = lax.optimization_barrier((late, back))
    order_params = call(
        rest_kernel,
        shape(GRAINS, planes, depth, width),
        [VMEM] * 4 + [ANY] * (len(late) - 4),
        *late,
        scratch=[
            *small,
            *[pltpu.VMEM(value.shape, F32) for value in late[6:]],
            pltpu.VMEM((4 * GRAINS, depth, width), F32),
            pltpu.VMEM((2, *plane), F32),
            pltpu.VMEM((GRAINS, planes, depth, width), F32),
            pltpu.SemaphoreType.DMA((17 + planes,)),
        ],
        out_specs=ANY, flops=2**37, moved=2**24, limit=24,
    )
    correlation = call(
        finish_kernel,
        shape(2, planes, depth, width),
        [VMEM] * 3,
        returned, *table,
        scratch=[pltpu.VMEM((2, planes, depth, width), F32), pltpu.SemaphoreType.DMA((2,))],
        out_specs=ANY,
        flops=2**28, moved=2**22,
    )
    return (order_params, correlation)


def solution(mesh):
    in_specs = (P(("grp", "gx"), None, None), P(None, ("grp", "gx"), None, None), P(), P())
    out_specs = (P(None, ("grp", "gx"), None, None), P(None, ("grp", "gx"), None, None))
    return jax.shard_map(shards, mesh=mesh, in_specs=in_specs, out_specs=out_specs, check_vma=False)
```

```python
import math

import jax
import jax.numpy as jnp
import ml_dtypes
import numpy as np
from jax import lax
from jax.experimental import pallas as pl
from jax.experimental.pallas import tpu as pltpu
from jax.sharding import PartitionSpec as P

STEPS = 3
SOON = 3
GRAINS = 8
F32 = jnp.float32
BF16 = jnp.bfloat16
VMEM = pl.BlockSpec(memory_space=pltpu.VMEM)
ANY = pl.BlockSpec(memory_space=pltpu.HBM)
MIB = 2**20


def halves(table):
    table = np.asarray(table, np.float32)
    high = table.astype(ml_dtypes.bfloat16)
    low = (table - high.astype(np.float32)).astype(ml_dtypes.bfloat16)
    return high, low


def phases(length, rows=None):
    index = np.arange(length)
    product = np.arange(length if rows is None else rows)[:, None] * index[None, :] % length
    angle = product * (2.0 * math.pi / length)
    return np.cos(angle), np.sin(angle)


def y_table(width):
    cos_y, sin_y = phases(width, width // 2)
    sin_y = -sin_y
    sin_y[0] = 1.0 - 2.0 * (np.arange(width) % 2)
    return np.concatenate([cos_y, sin_y], axis=0)


def z_tables(depth):
    cos_z, sin_z = phases(depth)
    two = np.eye(2)
    cos_z, sin_z = np.kron(two, cos_z), np.kron(two, sin_z)
    forward = np.block([[cos_z, -sin_z], [sin_z, cos_z]])
    half = 2 * depth
    forward_turned = np.concatenate([forward[:, half:], -forward[:, :half]], axis=1)
    inverse = np.block([[cos_z, sin_z], [-sin_z, cos_z]])
    inverse_turned = np.concatenate([-inverse[:, half:], inverse[:, :half]], axis=1)
    return (
        np.concatenate([forward, forward_turned], axis=0),
        np.concatenate([inverse, inverse_turned], axis=0),
    )


def split(value):
    high = value.astype(BF16)
    low = (value - high.astype(F32)).astype(BF16)
    return high, low


def dot3(left, right, contract=((1,), (0,))):
    def one(a, b):
        return lax.dot_general(a, b, (contract, ((), ())), preferred_element_type=F32)

    return one(left[0], right[0]) + (one(left[0], right[1]) + one(left[1], right[0]))


def fetch(pairs, semaphores):
    copies = [pltpu.make_async_copy(src, dst, semaphores.at[k]) for k, (src, dst) in enumerate(pairs)]
    for copy in copies:
        copy.start()
    return copies


def pair_of(chosen):
    first, second = chosen[0], chosen[1]
    second = jnp.where(second == first, lax.rem(first + 1, GRAINS), second)
    return first, second


def others_of(chosen):
    first, second = pair_of(chosen)
    low, high = jnp.minimum(first, second), jnp.maximum(first, second)

    def other(r):
        i = jnp.where(r >= low, r + 1, r)
        return jnp.where(i >= high, i + 1, i)

    return other


def start_kernel(jitter_any, ids_any, p0, p1, p2, jitter, grain_ids, semaphores):
    planes = grain_ids.shape[0]
    pairs = []
    for k in range(planes):
        pairs.append((jitter_any.at[:, k], jitter.at[:, k]))
        pairs.append((ids_any.at[k], grain_ids.at[k]))
    copies = fetch(pairs, semaphores)
    for k, out in enumerate((p0, p1, p2)):
        copies[2 * k].wait()
        copies[2 * k + 1].wait()
        ids = grain_ids[k]
        for i in range(GRAINS):
            base = jnp.where(ids == i, jnp.float32(0.6), jnp.float32(0.0))
            out[i] = base + jitter[i, k].astype(F32)


def grain_of(start):
    ids = jnp.where(start[1] > 0.55, 1, 0)
    for g in range(2, GRAINS):
        ids = jnp.where(start[g] > 0.55, g, ids)
    return ids


def rate(classes, ids, i):
    def level(g):
        return 0.12 * (0.4 + 0.2 * classes[g, i].astype(F32))

    value = jnp.full(ids.shape, level(0), F32)
    for g in range(1, GRAINS):
        value = jnp.where(ids == g, level(g), value)
    return value


def squares(state):
    total = state[0] * state[0]
    for i in range(1, GRAINS):
        total = total + state[i] * state[i]
    return 5.0 + 3.0 * total


def update(e, before, after, total, mobility):
    depth, width = e.shape
    near = before + after
    near = near + (pltpu.roll(e, 1, 0) + pltpu.roll(e, depth - 1, 0))
    near = near + (pltpu.roll(e, 1, 1) + pltpu.roll(e, width - 1, 1))
    return e + mobility * (near - e * (total - 2.0 * (e * e)))


def step_plane(center, before, after, mobility, out):
    total = squares(center)
    for i in range(GRAINS):
        out[i] = update(center[i], before[i], after[i], total, mobility[i])


def rates_plane(classes, start, out):
    ids = grain_of(start)
    for i in range(GRAINS):
        out[i] = rate(classes, ids, i)


def inner_kernel(
    chosen_any, classes_any, p0, p1, p2, up2, down2, r0, r2, l0, l2, rates, middle, chosen, classes, semaphores
):
    copies = fetch(((chosen_any, chosen), (classes_any, classes)), semaphores)
    for i in range(GRAINS):
        up2[i] = p1[i]
        down2[i] = p1[i]
    for copy in copies:
        copy.wait()
    for k, i in enumerate(pair_of(chosen)):
        up2[GRAINS + k] = p0[i]
        down2[GRAINS + k] = p2[i]
    other = others_of(chosen)
    for r in range(GRAINS - 2):
        i = other(r)
        for soon, late, start in ((r0, l0, p0), (r2, l2, p2)):
            if r < SOON:
                soon[r] = start[i]
            else:
                late[r - SOON] = start[i]
    for k, start in enumerate((p0, p1, p2)):
        rates_plane(classes, start, rates.at[k])
    step_plane(p1, p0, p2, rates.at[1], middle)


def groups(ref, count, base=0):
    return [ref.at[pl.ds(base + k * GRAINS, GRAINS)] for k in range(count)]


def near_kernel(classes_any, p0, p1, p2, prev1, next1, rates, middle, near_out, classes, semaphores):
    edge0, edge1, inner0, inner2, middle2 = groups(near_out, 5)
    copies = fetch(((classes_any, classes),), semaphores)
    step_plane(p0, prev1, p1, rates.at[0], inner0)
    step_plane(p2, p1, next1, rates.at[2], inner2)
    copies[0].wait()
    rates_plane(classes, prev1, edge0)
    rates_plane(classes, next1, edge1)
    step_plane(middle, inner0, inner2, rates.at[1], middle2)


def second_step(p0, p2, prev1, next1, prev2, next2, rates, middle, near_state, outer1, side2):
    edge_rates, inner1 = near_state[:2], near_state[2:4]
    step_plane(prev1, prev2, p0, edge_rates[0], outer1[0])
    step_plane(next1, p2, next2, edge_rates[1], outer1[1])
    step_plane(inner1[0], outer1[0], middle, rates.at[0], side2[0])
    step_plane(inner1[1], middle, outer1[1], rates.at[2], side2[1])


def pair_kernel(
    chosen_any, classes_any, p0, p2, prev1, next1, prev2, next2, rates, middle, near_out, high_any, low_any,
    packed, chosen, classes, high, low, second, edge, fields, semaphores,
):
    copies = fetch(
        ((chosen_any, chosen), (classes_any, classes), (high_any, high), (low_any, low)), semaphores
    )
    near_state = groups(near_out, 5)
    edge_rates, inner1, middle2 = near_state[:2], near_state[2:4], near_state[4]
    outer1, side2 = groups(second, 2), groups(second, 2, 2 * GRAINS)
    second_step(p0, p2, prev1, next1, prev2, next2, rates, middle, near_state, outer1, side2)
    eta2 = (side2[0], middle2, side2[1])
    depth, width = p0.shape[1:]
    totals = [squares(state) for state in eta2]
    copies[0].wait()
    copies[1].wait()
    pair = pair_of(chosen)
    for side, (mid, near) in enumerate(((prev2, prev1), (next2, next1))):
        ids = grain_of(mid)
        total0 = squares(mid)
        total1 = squares(outer1[side])
        for k, i in enumerate(pair):
            first = update(mid[i], mid[GRAINS + k], near[i], total0, rate(classes, ids, i))
            edge[side, k] = update(outer1[side][i], first, inner1[side][i], total1, edge_rates[side][i])
    repeated = chosen[1] == chosen[0]
    for k in range(3):
        values = []
        for f, i in enumerate(pair):
            before = edge[0, f] if k == 0 else eta2[k - 1][i]
            after = edge[1, f] if k == 2 else eta2[k + 1][i]
            value = update(eta2[k][i], before, after, totals[k], rates[k, i])
            values.append(value)
        values[1] = jnp.where(repeated, values[0], values[1])
        for f in range(2):
            base = k * 2 * depth + f * depth
            fields[base : base + depth] = values[f]
    copies[2].wait()
    copies[3].wait()
    full = dot3((high[...], low[...]), split(fields[...]), ((1,), (1,)))
    slots = width // 2
    lanes = 4 * depth
    half = lanes // 2
    real_lane = lax.broadcasted_iota(jnp.int32, (slots, lanes), 1) < half
    for k in range(3):
        at = slice(k // 2 * lanes, k // 2 * lanes + lanes)
        cosine, sine = full[:slots, at], full[slots:, at]
        if k % 2:
            cosine = pltpu.roll(cosine, half, 1)
        else:
            sine = pltpu.roll(sine, half, 1)
        part = jnp.where(real_lane, cosine, sine)
        if packed.shape[0] == 3:
            packed[k] = part
        else:
            devices, rows, _ = packed.shape
            rows = rows // 3
            packed[:, k * rows : (k + 1) * rows, :] = part.reshape(devices, rows, lanes)


def rest_kernel(
    prev3, next3,
    chosen_any, classes_any, p0_any, p2_any, prev1_any, next1_any, prev2_any, next2_any, near_any, middle_any,
    rates_any, out_any, linear,
    chosen, classes, p0, p2, prev1, next1, prev2, next2, near_out, middle, rates, second, edge, out, semaphores,
):
    near_state, near_source = groups(near_out, 5), groups(near_any, 5)
    edge_rates, inner1, middle2 = near_state[:2], near_state[2:4], near_state[4]
    outer1, side2 = groups(second, 2), groups(second, 2, 2 * GRAINS)
    copies = fetch(
        (
            (prev1_any, prev1), (prev2_any, prev2), (p0_any, p0), (near_source[0], near_state[0]),
            (next1_any, next1), (next2_any, next2), (p2_any, p2), (near_source[1], near_state[1]),
            (near_source[2], near_state[2]), (middle_any, middle), (rates_any.at[0], rates.at[0]),
            (near_source[3], near_state[3]), (rates_any.at[2], rates.at[2]),
            (chosen_any, chosen), (classes_any, classes),
            (near_source[4], near_state[4]), (rates_any.at[1], rates.at[1]),
        ),
        semaphores,
    )

    def wait(first, last):
        for copy in copies[first:last]:
            copy.wait()

    wait(0, 4)
    step_plane(prev1, prev2, p0, edge_rates[0], outer1[0])
    wait(4, 8)
    step_plane(next1, p2, next2, edge_rates[1], outer1[1])
    wait(8, 11)
    step_plane(inner1[0], outer1[0], middle, rates.at[0], side2[0])
    wait(11, 13)
    step_plane(inner1[1], middle, outer1[1], rates.at[2], side2[1])
    wait(13, 17)
    other = others_of(chosen)
    pair = pair_of(chosen)
    places = [(pair[k], GRAINS + k, None) for k in range(2)] + [(other(r), None, r) for r in range(GRAINS - 2)]
    eta2 = (side2[0], middle2, side2[1])
    outs = []

    def finish(plane, entries):
        total = squares(eta2[plane])
        for k, i in entries:
            before = edge[0, k] if plane == 0 else eta2[plane - 1][i]
            after = edge[1, k] if plane == 2 else eta2[plane + 1][i]
            out[i, plane] = update(eta2[plane][i], before, after, total, rates[plane, i])
        outs.extend(fetch(((out.at[:, plane], out_any.at[:, plane]),), semaphores.at[pl.ds(17 + plane, 1)]))

    everyone = list(enumerate(place[0] for place in places))
    finish(1, everyone)
    none = jnp.zeros(p0.shape[1:], F32)
    for side, (soon, mid, near) in enumerate(((prev3, prev2, prev1), (next3, next2, next1))):
        ids = grain_of(mid)
        total0 = squares(mid)
        total1 = squares(outer1[side])
        total2 = squares(eta2[2 * side])
        for k, (i, early, late) in enumerate(places):
            known = early is not None or late < SOON
            third = none if not known else soon[late] if early is None else mid[early]
            slope = rate(classes, ids, i)
            first = update(mid[i], third, near[i], total0, slope)
            second_value = update(outer1[side][i], first, inner1[side][i], total1, edge_rates[side][i])
            edge[side, k] = second_value
            if not known:
                linear[side, 0, late - SOON] = update(
                    eta2[2 * side][i], second_value, eta2[1][i], total2, rates[2 * side, i]
                )
                linear[side, 1, late - SOON] = slope * edge_rates[side][i] * rates[2 * side, i]
        finish(2 * side, everyone[: 2 + SOON])
    for copy in outs:
        copy.wait()


def last_kernel(prev4, next4, linear, chosen_any, partial_any, out_any, chosen, values, semaphores):
    copies = fetch(((chosen_any, chosen),), semaphores.at[pl.ds(0, 1)])
    count = prev4.shape[0]
    for side, far in enumerate((prev4, next4)):
        for r in range(count):
            values[side, r] = linear[side, 0, r] + linear[side, 1, r] * far[r]
    copies[0].wait()
    other = others_of(chosen)
    pieces = [
        (values.at[side, r], out_any.at[other(SOON + r), 2 * side]) for side in range(2) for r in range(count)
    ]
    for copy in fetch(pieces, semaphores.at[pl.ds(1, 2 * count)]):
        copy.wait()


def line_kernel(lines, z_forward, z_inverse, x_both, out, wide, tall, scale):
    rows, lanes = lines.shape
    total_x = wide.shape[0] // 3
    slots = rows // total_x
    half = lanes // 2

    def over_x(pieces, chunk=2):
        results = []
        for j in range(0, slots, chunk):
            group = pieces[j : j + chunk]
            high, low = split(jnp.concatenate(group, axis=1))
            stacked = jnp.concatenate([high, low, high], axis=0)
            both = jnp.dot(x_both[...], stacked, preferred_element_type=F32)
            for k in range(len(group)):
                at = slice(k * lanes, (k + 1) * lanes)
                results.append((both[:total_x, at], both[total_x:, at]))
        return results

    def put(row, even, odd):
        at = slice(row * total_x, (row + 1) * total_x)
        for base, value in ((0, even), (lanes, odd)):
            high, low = split(value)
            tall[0, at, base : base + lanes] = high
            tall[1, at, base : base + lanes] = low

    real_lane = lax.broadcasted_iota(jnp.int32, (total_x, lanes), 1) < half
    turned = over_x([lines[pl.ds(j, total_x, stride=slots), :] for j in range(slots)])
    for j, (even, odd) in enumerate(turned):
        put(j, even, odd)
    first_even, first_odd = turned[0]
    put(slots, jnp.where(real_lane, first_even, 0.0), jnp.where(real_lane, first_odd, 0.0))
    put(
        slots + 1,
        jnp.where(real_lane, pltpu.roll(first_even, half, 1), 0.0),
        jnp.where(real_lane, pltpu.roll(first_odd, half, 1), 0.0),
    )
    step = 2 * total_x
    parts = []
    for row in range(0, (slots + 2) * total_x, step):
        at = slice(row, row + step)
        part = dot3((tall[0, at], tall[1, at]), (z_forward[0], z_forward[1]))
        part = part * part
        part = part + pltpu.roll(part, half, 1)
        parts += [part[:total_x], part[total_x:]]

    def power(j):
        return parts[j]

    first = lax.axis_index("gx") == 0
    lane = lax.broadcasted_iota(jnp.int32, (total_x, lanes), 1)
    line = lax.broadcasted_iota(jnp.int32, (total_x, lanes), 0)
    constant = jnp.logical_and(line == 0, jnp.logical_or(lane == 0, lane == half // 2))
    powers = []
    for j in range(slots):
        value = jnp.where(real_lane, power(j), 0.0) * (2.0 * scale)
        if j == 0:
            special = jnp.where(real_lane, power(slots), power(slots + 1)) * scale
            special = jnp.where(constant, 0.0, special)
            value = jnp.where(first, special, value)
        powers.append(value)
    for j, (even, odd) in enumerate(over_x(powers)):
        put(j, even, odd)
    for j in range(0, slots, 2):
        at = slice(j * total_x, (j + 2) * total_x)
        back = dot3((tall[0, at], tall[1, at]), (z_inverse[0], z_inverse[1]))
        out[pl.ds(j, total_x, stride=slots), :] = back[:total_x]
        out[pl.ds(j + 1, total_x, stride=slots), :] = back[total_x:]


def finish_kernel(returned, high, low, out_any, out, semaphores):
    fields, planes, depth, width = out.shape
    lanes = 2 * fields * depth
    half = lanes // 2
    slots = width // 2
    stacked = []
    for k in range(planes):
        if returned.shape[0] == planes:
            part = returned[k]
        else:
            devices, rows, _ = returned.shape
            rows = rows // planes
            part = returned[:, k * rows : (k + 1) * rows, :].reshape(slots, lanes)
        part = part.T
        stacked.append(jnp.concatenate([part[:half], part[half:]], axis=1))
    stacked = split(jnp.concatenate(stacked, axis=0))
    copies = []
    for piece in range(2):
        at = slice(piece * slots, (piece + 1) * slots)
        result = dot3(stacked, (high[:, at], low[:, at]))
        for k in range(planes):
            for f in range(fields):
                base = k * half + f * depth
                out[f, k, :, at] = result[base : base + depth]
        copies += fetch(((out.at[:, :, :, at], out_any.at[:, :, :, at]),), semaphores.at[pl.ds(piece, 1)])
    for copy in copies:
        copy.wait()


def call(kernel, outs, in_specs, *args, scratch=(), flops=0, moved=0, limit=12, out_specs=None):
    args = [pltpu.with_memory_space_constraint(a, pltpu.HBM) if b is ANY else a for a, b in zip(args, in_specs)]
    return pl.pallas_call(
        kernel,
        out_shape=outs,
        in_specs=in_specs,
        out_specs=out_specs or jax.tree.map(lambda _: VMEM, outs),
        scratch_shapes=scratch,
        compiler_params=pltpu.CompilerParams(vmem_limit_bytes=limit * MIB),
        cost_estimate=pl.CostEstimate(flops=flops, bytes_accessed=moved, transcendentals=0),
    )(*args)


def shards(grain_ids, jitter, class_table, chosen):
    planes, depth, width = grain_ids.shape
    devices = lax.axis_size("gx")
    total_x = planes * devices
    count = float(total_x * depth * width)
    slots = width // 2
    share = slots // devices
    lanes = 4 * depth
    up = [(i, (i + 1) % devices) for i in range(devices)]
    down = [(j, i) for i, j in up]
    aligned = share % 8 == 0

    def shape(*dims):
        return jax.ShapeDtypeStruct(dims, F32)

    plane = (GRAINS, depth, width)
    table = [jnp.asarray(part) for part in halves(y_table(width))]
    z_forward, z_inverse = z_tables(depth)
    z_parts = [jnp.asarray(np.stack(halves(matrix))) for matrix in (z_forward, z_inverse)]
    x_high, x_low = halves(np.concatenate(phases(total_x), axis=0))
    x_both = jnp.asarray(np.concatenate([x_high, x_high, x_low], axis=1))

    two = (2, *plane)
    soon, last = (SOON, depth, width), (GRAINS - 2 - SOON, depth, width)
    small = [pltpu.SMEM((2,), jnp.int32), pltpu.SMEM((GRAINS, GRAINS), jnp.int32)]
    ten = (GRAINS + 2, depth, width)
    p0, p1, p2 = call(
        start_kernel,
        (shape(*plane), shape(*plane), shape(*plane)),
        [ANY] * 2,
        jitter, grain_ids,
        scratch=[
            pltpu.VMEM(jitter.shape, jitter.dtype),
            pltpu.VMEM(grain_ids.shape, jnp.int32),
            pltpu.SemaphoreType.DMA((2 * planes,)),
        ],
        flops=2**21, moved=2**22,
    )
    prev1 = lax.ppermute(p2, "gx", up)
    next1 = lax.ppermute(p0, "gx", down)
    up2, down2, r0, r2, l0, l2, rates, middle = call(
        inner_kernel,
        (
            shape(*ten), shape(*ten), shape(*soon), shape(*soon), shape(*last), shape(*last),
            shape(planes, *plane), shape(*plane),
        ),
        [ANY] * 2 + [VMEM] * 3,
        chosen, class_table, p0, p1, p2,
        scratch=[*small, pltpu.SemaphoreType.DMA((2,))],
        flops=2**24, moved=2**22,
    )
    prev2 = lax.ppermute(up2, "gx", up)
    next2 = lax.ppermute(down2, "gx", down)
    near_out = call(
        near_kernel,
        shape(5 * GRAINS, depth, width),
        [ANY] + [VMEM] * 7,
        class_table, p0, p1, p2, prev1, next1, rates, middle,
        scratch=[small[1], pltpu.SemaphoreType.DMA((1,))],
        flops=2**25, moved=2**24,
    )
    r0, r2, near_out = lax.optimization_barrier((r0, r2, near_out))
    prev3 = lax.ppermute(r0, "gx", up)
    next3 = lax.ppermute(r2, "gx", down)
    packed_shape = (devices, planes * share, lanes) if aligned else (planes, slots, lanes)
    packed = call(
        pair_kernel,
        shape(*packed_shape),
        [ANY] * 2 + [VMEM] * 9 + [ANY] * 2,
        chosen, class_table, p0, p2, prev1, next1, prev2, next2, rates, middle, near_out, *table,
        scratch=[
            *small,
            pltpu.VMEM(table[0].shape, BF16),
            pltpu.VMEM(table[1].shape, BF16),
            pltpu.VMEM((4 * GRAINS, depth, width), F32),
            pltpu.VMEM((2, 2, depth, width), F32),
            pltpu.VMEM(((planes + 1) // 2 * lanes, width), F32),
            pltpu.SemaphoreType.DMA((4,)),
        ],
        flops=2**28, moved=2**23,
    )
    packed, prev3, next3 = lax.optimization_barrier((packed, prev3, next3))
    if aligned:
        lines = lax.all_to_all(packed, "gx", split_axis=0, concat_axis=0, tiled=True)
    else:
        lines = lax.all_to_all(packed, "gx", split_axis=1, concat_axis=0, tiled=True)
    lines = lines.reshape(total_x * share, lanes)

    def lines_body(*refs):
        line_kernel(*refs, scale=1.0 / (count * count))

    back = call(
        lines_body,
        shape(total_x * share, lanes),
        [VMEM] * 4,
        lines, *z_parts, x_both,
        scratch=[
            pltpu.VMEM((3 * total_x, share * lanes), BF16),
            pltpu.VMEM((2, total_x * (share + 2), 2 * lanes), BF16),
        ],
        flops=2**28, moved=2**22,
    )
    back = back.reshape(devices, planes * share, lanes)
    returned = lax.all_to_all(back, "gx", split_axis=0, concat_axis=0, tiled=True)
    if not aligned:
        returned = returned.reshape(devices, planes, share, lanes).transpose(1, 0, 2, 3)
        returned = returned.reshape(planes, slots, lanes)
    l0, l2, back = lax.optimization_barrier((l0, l2, back))
    prev4 = lax.ppermute(l0, "gx", up)
    next4 = lax.ppermute(l2, "gx", down)
    late = (prev3, next3, chosen, class_table, p0, p2, prev1, next1, prev2, next2, near_out, middle, rates)
    late, _ = lax.optimization_barrier((late, back))
    partial, linear = call(
        rest_kernel,
        (shape(GRAINS, planes, depth, width), shape(2, 2, *last)),
        [VMEM] * 2 + [ANY] * (len(late) - 2),
        *late,
        scratch=[
            *small,
            *[pltpu.VMEM(value.shape, F32) for value in late[4:]],
            pltpu.VMEM((4 * GRAINS, depth, width), F32),
            pltpu.VMEM((2, *plane), F32),
            pltpu.VMEM((GRAINS, planes, depth, width), F32),
            pltpu.SemaphoreType.DMA((17 + planes,)),
        ],
        out_specs=(ANY, VMEM), flops=2**26, moved=2**24, limit=24,
    )
    order_params = pl.pallas_call(
        last_kernel,
        out_shape=shape(GRAINS, planes, depth, width),
        in_specs=[VMEM] * 3 + [ANY] * 2,
        out_specs=ANY,
        scratch_shapes=[
            small[0],
            pltpu.VMEM((2, *last), F32),
            pltpu.SemaphoreType.DMA((1 + 2 * last[0],)),
        ],
        input_output_aliases={4: 0},
        compiler_params=pltpu.CompilerParams(vmem_limit_bytes=12 * MIB),
        cost_estimate=pl.CostEstimate(flops=2**20, bytes_accessed=2**21, transcendentals=0),
    )(prev4, next4, linear, pltpu.with_memory_space_constraint(chosen, pltpu.HBM), partial)
    correlation = call(
        finish_kernel,
        shape(2, planes, depth, width),
        [VMEM] * 3,
        returned, *table,
        scratch=[pltpu.VMEM((2, planes, depth, width), F32), pltpu.SemaphoreType.DMA((2,))],
        out_specs=ANY,
        flops=2**28, moved=2**22,
    )
    return (order_params, correlation)


def solution(mesh):
    in_specs = (P(("grp", "gx"), None, None), P(None, ("grp", "gx"), None, None), P(), P())
    out_specs = (P(None, ("grp", "gx"), None, None), P(None, ("grp", "gx"), None, None))
    return jax.shard_map(shards, mesh=mesh, in_specs=in_specs, out_specs=out_specs, check_vma=False)
```

```python
import math

import jax
import jax.numpy as jnp
import ml_dtypes
import numpy as np
from jax import lax
from jax.experimental import pallas as pl
from jax.experimental.pallas import tpu as pltpu
from jax.sharding import PartitionSpec as P

STEPS = 3
SOON = 4
GRAINS = 8
F32 = jnp.float32
BF16 = jnp.bfloat16
VMEM = pl.BlockSpec(memory_space=pltpu.VMEM)
ANY = pl.BlockSpec(memory_space=pltpu.HBM)
MIB = 2**20


def halves(table):
    table = np.asarray(table, np.float32)
    high = table.astype(ml_dtypes.bfloat16)
    low = (table - high.astype(np.float32)).astype(ml_dtypes.bfloat16)
    return high, low


def phases(length, rows=None):
    index = np.arange(length)
    product = np.arange(length if rows is None else rows)[:, None] * index[None, :] % length
    angle = product * (2.0 * math.pi / length)
    return np.cos(angle), np.sin(angle)


def y_table(width):
    cos_y, sin_y = phases(width, width // 2)
    sin_y = -sin_y
    sin_y[0] = 1.0 - 2.0 * (np.arange(width) % 2)
    return np.concatenate([cos_y, sin_y], axis=0)


def z_tables(depth):
    cos_z, sin_z = phases(depth)
    two = np.eye(2)
    cos_z, sin_z = np.kron(two, cos_z), np.kron(two, sin_z)
    forward = np.block([[cos_z, -sin_z], [sin_z, cos_z]])
    half = 2 * depth
    forward_turned = np.concatenate([forward[:, half:], -forward[:, :half]], axis=1)
    inverse = np.block([[cos_z, sin_z], [-sin_z, cos_z]])
    inverse_turned = np.concatenate([-inverse[:, half:], inverse[:, :half]], axis=1)
    return (
        np.concatenate([forward, forward_turned], axis=0),
        np.concatenate([inverse, inverse_turned], axis=0),
    )


def split(value):
    high = value.astype(BF16)
    low = (value - high.astype(F32)).astype(BF16)
    return high, low


def dot3(left, right, contract=((1,), (0,))):
    def one(a, b):
        return lax.dot_general(a, b, (contract, ((), ())), preferred_element_type=F32)

    return one(left[0], right[0]) + (one(left[0], right[1]) + one(left[1], right[0]))


def fetch(pairs, semaphores):
    copies = [pltpu.make_async_copy(src, dst, semaphores.at[k]) for k, (src, dst) in enumerate(pairs)]
    for copy in copies:
        copy.start()
    return copies


def pair_of(chosen):
    first, second = chosen[0], chosen[1]
    second = jnp.where(second == first, lax.rem(first + 1, GRAINS), second)
    return first, second


def others_of(chosen):
    first, second = pair_of(chosen)
    low, high = jnp.minimum(first, second), jnp.maximum(first, second)

    def other(r):
        i = jnp.where(r >= low, r + 1, r)
        return jnp.where(i >= high, i + 1, i)

    return other


def start_kernel(jitter_any, ids_any, p0, p1, p2, jitter, grain_ids, semaphores):
    planes = grain_ids.shape[0]
    pairs = []
    for k in range(planes):
        pairs.append((jitter_any.at[:, k], jitter.at[:, k]))
        pairs.append((ids_any.at[k], grain_ids.at[k]))
    copies = fetch(pairs, semaphores)
    for k, out in enumerate((p0, p1, p2)):
        copies[2 * k].wait()
        copies[2 * k + 1].wait()
        ids = grain_ids[k]
        for i in range(GRAINS):
            base = jnp.where(ids == i, jnp.float32(0.6), jnp.float32(0.0))
            out[i] = base + jitter[i, k].astype(F32)


def grain_of(start):
    ids = jnp.where(start[1] > 0.55, 1, 0)
    for g in range(2, GRAINS):
        ids = jnp.where(start[g] > 0.55, g, ids)
    return ids


def rate(classes, ids, i):
    def level(g):
        return 0.12 * (0.4 + 0.2 * classes[g, i].astype(F32))

    value = jnp.full(ids.shape, level(0), F32)
    for g in range(1, GRAINS):
        value = jnp.where(ids == g, level(g), value)
    return value


def squares(state):
    total = state[0] * state[0]
    for i in range(1, GRAINS):
        total = total + state[i] * state[i]
    return 5.0 + 3.0 * total


def update(e, before, after, total, mobility):
    depth, width = e.shape
    near = before + after
    near = near + (pltpu.roll(e, 1, 0) + pltpu.roll(e, depth - 1, 0))
    near = near + (pltpu.roll(e, 1, 1) + pltpu.roll(e, width - 1, 1))
    return e + mobility * (near - e * (total - 2.0 * (e * e)))


def step_plane(center, before, after, mobility, out):
    total = squares(center)
    for i in range(GRAINS):
        out[i] = update(center[i], before[i], after[i], total, mobility[i])


def rates_plane(classes, start, out):
    ids = grain_of(start)
    for i in range(GRAINS):
        out[i] = rate(classes, ids, i)


def inner_kernel(
    chosen_any, classes_any, p0, p1, p2, up2, down2, r0, r2, l0, l2, rates, middle, chosen, classes, semaphores
):
    copies = fetch(((chosen_any, chosen), (classes_any, classes)), semaphores)
    for i in range(GRAINS):
        up2[i] = p1[i]
        down2[i] = p1[i]
    for copy in copies:
        copy.wait()
    for k, i in enumerate(pair_of(chosen)):
        up2[GRAINS + k] = p0[i]
        down2[GRAINS + k] = p2[i]
    other = others_of(chosen)
    for r in range(GRAINS - 2):
        i = other(r)
        for soon, late, start in ((r0, l0, p0), (r2, l2, p2)):
            if r < SOON:
                soon[r] = start[i]
            else:
                late[r - SOON] = start[i]
    for k, start in enumerate((p0, p1, p2)):
        rates_plane(classes, start, rates.at[k])
    step_plane(p1, p0, p2, rates.at[1], middle)


def groups(ref, count, base=0):
    return [ref.at[pl.ds(base + k * GRAINS, GRAINS)] for k in range(count)]


def near_kernel(classes_any, p0, p1, p2, prev1, next1, rates, middle, near_out, classes, semaphores):
    edge0, edge1, inner0, inner2, middle2 = groups(near_out, 5)
    copies = fetch(((classes_any, classes),), semaphores)
    step_plane(p0, prev1, p1, rates.at[0], inner0)
    step_plane(p2, p1, next1, rates.at[2], inner2)
    copies[0].wait()
    rates_plane(classes, prev1, edge0)
    rates_plane(classes, next1, edge1)
    step_plane(middle, inner0, inner2, rates.at[1], middle2)


def second_step(p0, p2, prev1, next1, prev2, next2, rates, middle, near_state, outer1, side2):
    edge_rates, inner1 = near_state[:2], near_state[2:4]
    step_plane(prev1, prev2, p0, edge_rates[0], outer1[0])
    step_plane(next1, p2, next2, edge_rates[1], outer1[1])
    step_plane(inner1[0], outer1[0], middle, rates.at[0], side2[0])
    step_plane(inner1[1], middle, outer1[1], rates.at[2], side2[1])


def pair_kernel(
    chosen_any, classes_any, p0, p2, prev1, next1, prev2, next2, rates, middle, near_out, high_any, low_any,
    packed, chosen, classes, high, low, second, edge, fields, semaphores,
):
    copies = fetch(
        ((chosen_any, chosen), (classes_any, classes), (high_any, high), (low_any, low)), semaphores
    )
    near_state = groups(near_out, 5)
    edge_rates, inner1, middle2 = near_state[:2], near_state[2:4], near_state[4]
    outer1, side2 = groups(second, 2), groups(second, 2, 2 * GRAINS)
    second_step(p0, p2, prev1, next1, prev2, next2, rates, middle, near_state, outer1, side2)
    eta2 = (side2[0], middle2, side2[1])
    depth, width = p0.shape[1:]
    totals = [squares(state) for state in eta2]
    copies[0].wait()
    copies[1].wait()
    pair = pair_of(chosen)
    for side, (mid, near) in enumerate(((prev2, prev1), (next2, next1))):
        ids = grain_of(mid)
        total0 = squares(mid)
        total1 = squares(outer1[side])
        for k, i in enumerate(pair):
            first = update(mid[i], mid[GRAINS + k], near[i], total0, rate(classes, ids, i))
            edge[side, k] = update(outer1[side][i], first, inner1[side][i], total1, edge_rates[side][i])
    repeated = chosen[1] == chosen[0]
    for k in range(3):
        values = []
        for f, i in enumerate(pair):
            before = edge[0, f] if k == 0 else eta2[k - 1][i]
            after = edge[1, f] if k == 2 else eta2[k + 1][i]
            value = update(eta2[k][i], before, after, totals[k], rates[k, i])
            values.append(value)
        values[1] = jnp.where(repeated, values[0], values[1])
        for f in range(2):
            base = k * 2 * depth + f * depth
            fields[base : base + depth] = values[f]
    copies[2].wait()
    copies[3].wait()
    full = dot3((high[...], low[...]), split(fields[...]), ((1,), (1,)))
    slots = width // 2
    lanes = 4 * depth
    half = lanes // 2
    real_lane = lax.broadcasted_iota(jnp.int32, (slots, lanes), 1) < half
    for k in range(3):
        at = slice(k // 2 * lanes, k // 2 * lanes + lanes)
        cosine, sine = full[:slots, at], full[slots:, at]
        if k % 2:
            cosine = pltpu.roll(cosine, half, 1)
        else:
            sine = pltpu.roll(sine, half, 1)
        part = jnp.where(real_lane, cosine, sine)
        if packed.shape[0] == 3:
            packed[k] = part
        else:
            devices, rows, _ = packed.shape
            rows = rows // 3
            packed[:, k * rows : (k + 1) * rows, :] = part.reshape(devices, rows, lanes)


def rest_kernel(
    prev3, next3,
    chosen_any, classes_any, p0_any, p2_any, prev1_any, next1_any, prev2_any, next2_any, near_any, middle_any,
    rates_any, out_any, linear,
    chosen, classes, p0, p2, prev1, next1, prev2, next2, near_out, middle, rates, second, edge, out, semaphores,
):
    near_state, near_source = groups(near_out, 5), groups(near_any, 5)
    edge_rates, inner1, middle2 = near_state[:2], near_state[2:4], near_state[4]
    outer1, side2 = groups(second, 2), groups(second, 2, 2 * GRAINS)
    copies = fetch(
        (
            (prev1_any, prev1), (prev2_any, prev2), (p0_any, p0), (near_source[0], near_state[0]),
            (next1_any, next1), (next2_any, next2), (p2_any, p2), (near_source[1], near_state[1]),
            (near_source[2], near_state[2]), (middle_any, middle), (rates_any.at[0], rates.at[0]),
            (near_source[3], near_state[3]), (rates_any.at[2], rates.at[2]),
            (chosen_any, chosen), (classes_any, classes),
            (near_source[4], near_state[4]), (rates_any.at[1], rates.at[1]),
        ),
        semaphores,
    )

    def wait(first, last):
        for copy in copies[first:last]:
            copy.wait()

    wait(0, 4)
    step_plane(prev1, prev2, p0, edge_rates[0], outer1[0])
    wait(4, 8)
    step_plane(next1, p2, next2, edge_rates[1], outer1[1])
    wait(8, 11)
    step_plane(inner1[0], outer1[0], middle, rates.at[0], side2[0])
    wait(11, 13)
    step_plane(inner1[1], middle, outer1[1], rates.at[2], side2[1])
    wait(13, 17)
    other = others_of(chosen)
    pair = pair_of(chosen)
    places = [(pair[k], GRAINS + k, None) for k in range(2)] + [(other(r), None, r) for r in range(GRAINS - 2)]
    eta2 = (side2[0], middle2, side2[1])
    outs = []

    def finish(plane, entries):
        total = squares(eta2[plane])
        for k, i in entries:
            before = edge[0, k] if plane == 0 else eta2[plane - 1][i]
            after = edge[1, k] if plane == 2 else eta2[plane + 1][i]
            out[i, plane] = update(eta2[plane][i], before, after, total, rates[plane, i])
        outs.extend(fetch(((out.at[:, plane], out_any.at[:, plane]),), semaphores.at[pl.ds(17 + plane, 1)]))

    everyone = list(enumerate(place[0] for place in places))
    finish(1, everyone)
    none = jnp.zeros(p0.shape[1:], F32)
    for side, (soon, mid, near) in enumerate(((prev3, prev2, prev1), (next3, next2, next1))):
        ids = grain_of(mid)
        total0 = squares(mid)
        total1 = squares(outer1[side])
        total2 = squares(eta2[2 * side])
        for k, (i, early, late) in enumerate(places):
            known = early is not None or late < SOON
            third = none if not known else soon[late] if early is None else mid[early]
            slope = rate(classes, ids, i)
            first = update(mid[i], third, near[i], total0, slope)
            second_value = update(outer1[side][i], first, inner1[side][i], total1, edge_rates[side][i])
            edge[side, k] = second_value
            if not known:
                linear[side, 0, late - SOON] = update(
                    eta2[2 * side][i], second_value, eta2[1][i], total2, rates[2 * side, i]
                )
                linear[side, 1, late - SOON] = slope * edge_rates[side][i] * rates[2 * side, i]
        finish(2 * side, everyone[: 2 + SOON])
    for copy in outs:
        copy.wait()


def last_kernel(prev4, next4, linear, chosen_any, partial_any, out_any, chosen, values, semaphores):
    copies = fetch(((chosen_any, chosen),), semaphores.at[pl.ds(0, 1)])
    count = prev4.shape[0]
    for side, far in enumerate((prev4, next4)):
        for r in range(count):
            values[side, r] = linear[side, 0, r] + linear[side, 1, r] * far[r]
    copies[0].wait()
    other = others_of(chosen)
    pieces = [
        (values.at[side, r], out_any.at[other(SOON + r), 2 * side]) for side in range(2) for r in range(count)
    ]
    for copy in fetch(pieces, semaphores.at[pl.ds(1, 2 * count)]):
        copy.wait()


def line_kernel(lines, z_forward, z_inverse, x_both, out, wide, tall, scale):
    rows, lanes = lines.shape
    total_x = wide.shape[0] // 3
    slots = rows // total_x
    half = lanes // 2

    def over_x(pieces, chunk=2):
        results = []
        for j in range(0, slots, chunk):
            group = pieces[j : j + chunk]
            high, low = split(jnp.concatenate(group, axis=1))
            stacked = jnp.concatenate([high, low, high], axis=0)
            both = jnp.dot(x_both[...], stacked, preferred_element_type=F32)
            for k in range(len(group)):
                at = slice(k * lanes, (k + 1) * lanes)
                results.append((both[:total_x, at], both[total_x:, at]))
        return results

    def put(row, even, odd):
        at = slice(row * total_x, (row + 1) * total_x)
        for base, value in ((0, even), (lanes, odd)):
            high, low = split(value)
            tall[0, at, base : base + lanes] = high
            tall[1, at, base : base + lanes] = low

    real_lane = lax.broadcasted_iota(jnp.int32, (total_x, lanes), 1) < half
    turned = over_x([lines[pl.ds(j, total_x, stride=slots), :] for j in range(slots)])
    for j, (even, odd) in enumerate(turned):
        put(j, even, odd)
    first_even, first_odd = turned[0]
    put(slots, jnp.where(real_lane, first_even, 0.0), jnp.where(real_lane, first_odd, 0.0))
    put(
        slots + 1,
        jnp.where(real_lane, pltpu.roll(first_even, half, 1), 0.0),
        jnp.where(real_lane, pltpu.roll(first_odd, half, 1), 0.0),
    )
    step = 2 * total_x
    parts = []
    for row in range(0, (slots + 2) * total_x, step):
        at = slice(row, row + step)
        part = dot3((tall[0, at], tall[1, at]), (z_forward[0], z_forward[1]))
        part = part * part
        part = part + pltpu.roll(part, half, 1)
        parts += [part[:total_x], part[total_x:]]

    def power(j):
        return parts[j]

    first = lax.axis_index("gx") == 0
    lane = lax.broadcasted_iota(jnp.int32, (total_x, lanes), 1)
    line = lax.broadcasted_iota(jnp.int32, (total_x, lanes), 0)
    constant = jnp.logical_and(line == 0, jnp.logical_or(lane == 0, lane == half // 2))
    powers = []
    for j in range(slots):
        value = jnp.where(real_lane, power(j), 0.0) * (2.0 * scale)
        if j == 0:
            special = jnp.where(real_lane, power(slots), power(slots + 1)) * scale
            special = jnp.where(constant, 0.0, special)
            value = jnp.where(first, special, value)
        powers.append(value)
    for j, (even, odd) in enumerate(over_x(powers)):
        put(j, even, odd)
    for j in range(0, slots, 2):
        at = slice(j * total_x, (j + 2) * total_x)
        back = dot3((tall[0, at], tall[1, at]), (z_inverse[0], z_inverse[1]))
        out[pl.ds(j, total_x, stride=slots), :] = back[:total_x]
        out[pl.ds(j + 1, total_x, stride=slots), :] = back[total_x:]


def finish_kernel(returned, high, low, out_any, out, semaphores):
    fields, planes, depth, width = out.shape
    lanes = 2 * fields * depth
    half = lanes // 2
    slots = width // 2
    stacked = []
    for k in range(planes):
        if returned.shape[0] == planes:
            part = returned[k]
        else:
            devices, rows, _ = returned.shape
            rows = rows // planes
            part = returned[:, k * rows : (k + 1) * rows, :].reshape(slots, lanes)
        part = part.T
        stacked.append(jnp.concatenate([part[:half], part[half:]], axis=1))
    stacked = split(jnp.concatenate(stacked, axis=0))
    copies = []
    for piece in range(2):
        at = slice(piece * slots, (piece + 1) * slots)
        result = dot3(stacked, (high[:, at], low[:, at]))
        for k in range(planes):
            for f in range(fields):
                base = k * half + f * depth
                out[f, k, :, at] = result[base : base + depth]
        copies += fetch(((out.at[:, :, :, at], out_any.at[:, :, :, at]),), semaphores.at[pl.ds(piece, 1)])
    for copy in copies:
        copy.wait()


def call(kernel, outs, in_specs, *args, scratch=(), flops=0, moved=0, limit=12, out_specs=None):
    args = [pltpu.with_memory_space_constraint(a, pltpu.HBM) if b is ANY else a for a, b in zip(args, in_specs)]
    return pl.pallas_call(
        kernel,
        out_shape=outs,
        in_specs=in_specs,
        out_specs=out_specs or jax.tree.map(lambda _: VMEM, outs),
        scratch_shapes=scratch,
        compiler_params=pltpu.CompilerParams(vmem_limit_bytes=limit * MIB),
        cost_estimate=pl.CostEstimate(flops=flops, bytes_accessed=moved, transcendentals=0),
    )(*args)


def shards(grain_ids, jitter, class_table, chosen):
    planes, depth, width = grain_ids.shape
    devices = lax.axis_size("gx")
    total_x = planes * devices
    count = float(total_x * depth * width)
    slots = width // 2
    share = slots // devices
    lanes = 4 * depth
    up = [(i, (i + 1) % devices) for i in range(devices)]
    down = [(j, i) for i, j in up]
    aligned = share % 8 == 0

    def shape(*dims):
        return jax.ShapeDtypeStruct(dims, F32)

    plane = (GRAINS, depth, width)
    table = [jnp.asarray(part) for part in halves(y_table(width))]
    z_forward, z_inverse = z_tables(depth)
    z_parts = [jnp.asarray(np.stack(halves(matrix))) for matrix in (z_forward, z_inverse)]
    x_high, x_low = halves(np.concatenate(phases(total_x), axis=0))
    x_both = jnp.asarray(np.concatenate([x_high, x_high, x_low], axis=1))

    two = (2, *plane)
    soon, last = (SOON, depth, width), (GRAINS - 2 - SOON, depth, width)
    small = [pltpu.SMEM((2,), jnp.int32), pltpu.SMEM((GRAINS, GRAINS), jnp.int32)]
    ten = (GRAINS + 2, depth, width)
    p0, p1, p2 = call(
        start_kernel,
        (shape(*plane), shape(*plane), shape(*plane)),
        [ANY] * 2,
        jitter, grain_ids,
        scratch=[
            pltpu.VMEM(jitter.shape, jitter.dtype),
            pltpu.VMEM(grain_ids.shape, jnp.int32),
            pltpu.SemaphoreType.DMA((2 * planes,)),
        ],
        flops=2**21, moved=2**22,
    )
    prev1 = lax.ppermute(p2, "gx", up)
    next1 = lax.ppermute(p0, "gx", down)
    up2, down2, r0, r2, l0, l2, rates, middle = call(
        inner_kernel,
        (
            shape(*ten), shape(*ten), shape(*soon), shape(*soon), shape(*last), shape(*last),
            shape(planes, *plane), shape(*plane),
        ),
        [ANY] * 2 + [VMEM] * 3,
        chosen, class_table, p0, p1, p2,
        scratch=[*small, pltpu.SemaphoreType.DMA((2,))],
        flops=2**24, moved=2**22,
    )
    prev2 = lax.ppermute(up2, "gx", up)
    next2 = lax.ppermute(down2, "gx", down)
    near_out = call(
        near_kernel,
        shape(5 * GRAINS, depth, width),
        [ANY] + [VMEM] * 7,
        class_table, p0, p1, p2, prev1, next1, rates, middle,
        scratch=[small[1], pltpu.SemaphoreType.DMA((1,))],
        flops=2**25, moved=2**24,
    )
    r0, r2, near_out = lax.optimization_barrier((r0, r2, near_out))
    prev3 = lax.ppermute(r0, "gx", up)
    next3 = lax.ppermute(r2, "gx", down)
    packed_shape = (devices, planes * share, lanes) if aligned else (planes, slots, lanes)
    packed = call(
        pair_kernel,
        shape(*packed_shape),
        [ANY] * 2 + [VMEM] * 9 + [ANY] * 2,
        chosen, class_table, p0, p2, prev1, next1, prev2, next2, rates, middle, near_out, *table,
        scratch=[
            *small,
            pltpu.VMEM(table[0].shape, BF16),
            pltpu.VMEM(table[1].shape, BF16),
            pltpu.VMEM((4 * GRAINS, depth, width), F32),
            pltpu.VMEM((2, 2, depth, width), F32),
            pltpu.VMEM(((planes + 1) // 2 * lanes, width), F32),
            pltpu.SemaphoreType.DMA((4,)),
        ],
        flops=2**28, moved=2**23,
    )
    packed, prev3, next3 = lax.optimization_barrier((packed, prev3, next3))
    if aligned:
        lines = lax.all_to_all(packed, "gx", split_axis=0, concat_axis=0, tiled=True)
    else:
        lines = lax.all_to_all(packed, "gx", split_axis=1, concat_axis=0, tiled=True)
    lines = lines.reshape(total_x * share, lanes)

    def lines_body(*refs):
        line_kernel(*refs, scale=1.0 / (count * count))

    back = call(
        lines_body,
        shape(total_x * share, lanes),
        [VMEM] * 4,
        lines, *z_parts, x_both,
        scratch=[
            pltpu.VMEM((3 * total_x, share * lanes), BF16),
            pltpu.VMEM((2, total_x * (share + 2), 2 * lanes), BF16),
        ],
        flops=2**28, moved=2**22,
    )
    back = back.reshape(devices, planes * share, lanes)
    returned = lax.all_to_all(back, "gx", split_axis=0, concat_axis=0, tiled=True)
    if not aligned:
        returned = returned.reshape(devices, planes, share, lanes).transpose(1, 0, 2, 3)
        returned = returned.reshape(planes, slots, lanes)
    l0, l2, back = lax.optimization_barrier((l0, l2, back))
    prev4 = lax.ppermute(l0, "gx", up)
    next4 = lax.ppermute(l2, "gx", down)
    late = (prev3, next3, chosen, class_table, p0, p2, prev1, next1, prev2, next2, near_out, middle, rates)
    late, _ = lax.optimization_barrier((late, back))
    partial, linear = call(
        rest_kernel,
        (shape(GRAINS, planes, depth, width), shape(2, 2, *last)),
        [VMEM] * 2 + [ANY] * (len(late) - 2),
        *late,
        scratch=[
            *small,
            *[pltpu.VMEM(value.shape, F32) for value in late[4:]],
            pltpu.VMEM((4 * GRAINS, depth, width), F32),
            pltpu.VMEM((2, *plane), F32),
            pltpu.VMEM((GRAINS, planes, depth, width), F32),
            pltpu.SemaphoreType.DMA((17 + planes,)),
        ],
        out_specs=(ANY, VMEM), flops=2**26, moved=2**24, limit=24,
    )
    order_params = pl.pallas_call(
        last_kernel,
        out_shape=shape(GRAINS, planes, depth, width),
        in_specs=[VMEM] * 3 + [ANY] * 2,
        out_specs=ANY,
        scratch_shapes=[
            small[0],
            pltpu.VMEM((2, *last), F32),
            pltpu.SemaphoreType.DMA((1 + 2 * last[0],)),
        ],
        input_output_aliases={4: 0},
        compiler_params=pltpu.CompilerParams(vmem_limit_bytes=12 * MIB),
        cost_estimate=pl.CostEstimate(flops=2**20, bytes_accessed=2**21, transcendentals=0),
    )(prev4, next4, linear, pltpu.with_memory_space_constraint(chosen, pltpu.HBM), partial)
    correlation = call(
        finish_kernel,
        shape(2, planes, depth, width),
        [VMEM] * 3,
        returned, *table,
        scratch=[pltpu.VMEM((2, planes, depth, width), F32), pltpu.SemaphoreType.DMA((2,))],
        out_specs=ANY,
        flops=2**28, moved=2**22,
    )
    return (order_params, correlation)


def solution(mesh):
    in_specs = (P(("grp", "gx"), None, None), P(None, ("grp", "gx"), None, None), P(), P())
    out_specs = (P(None, ("grp", "gx"), None, None), P(None, ("grp", "gx"), None, None))
    return jax.shard_map(shards, mesh=mesh, in_specs=in_specs, out_specs=out_specs, check_vma=False)
```

```python
import math

import jax
import jax.numpy as jnp
import ml_dtypes
import numpy as np
from jax import lax
from jax.experimental import pallas as pl
from jax.experimental.pallas import tpu as pltpu
from jax.sharding import PartitionSpec as P

STEPS = 3
GRAINS = 8
F32 = jnp.float32
BF16 = jnp.bfloat16
VMEM = pl.BlockSpec(memory_space=pltpu.VMEM)
ANY = pl.BlockSpec(memory_space=pltpu.HBM)
MIB = 2**20


def halves(table):
    table = np.asarray(table, np.float32)
    high = table.astype(ml_dtypes.bfloat16)
    low = (table - high.astype(np.float32)).astype(ml_dtypes.bfloat16)
    return high, low


def phases(length, rows=None):
    index = np.arange(length)
    product = np.arange(length if rows is None else rows)[:, None] * index[None, :] % length
    angle = product * (2.0 * math.pi / length)
    return np.cos(angle), np.sin(angle)


def y_table(width):
    cos_y, sin_y = phases(width, width // 2)
    sin_y = -sin_y
    sin_y[0] = 1.0 - 2.0 * (np.arange(width) % 2)
    return np.concatenate([cos_y, sin_y], axis=0)


def z_tables(depth):
    cos_z, sin_z = phases(depth)
    two = np.eye(2)
    cos_z, sin_z = np.kron(two, cos_z), np.kron(two, sin_z)
    forward = np.block([[cos_z, -sin_z], [sin_z, cos_z]])
    half = 2 * depth
    forward_turned = np.concatenate([forward[:, half:], -forward[:, :half]], axis=1)
    inverse = np.block([[cos_z, sin_z], [-sin_z, cos_z]])
    inverse_turned = np.concatenate([-inverse[:, half:], inverse[:, :half]], axis=1)
    return (
        np.concatenate([forward, forward_turned], axis=0),
        np.concatenate([inverse, inverse_turned], axis=0),
    )


def split(value):
    high = value.astype(BF16)
    low = (value - high.astype(F32)).astype(BF16)
    return high, low


def dot3(left, right, contract=((1,), (0,))):
    def one(a, b):
        return lax.dot_general(a, b, (contract, ((), ())), preferred_element_type=F32)

    return one(left[0], right[0]) + (one(left[0], right[1]) + one(left[1], right[0]))


def fetch(pairs, semaphores):
    copies = [pltpu.make_async_copy(src, dst, semaphores.at[k]) for k, (src, dst) in enumerate(pairs)]
    for copy in copies:
        copy.start()
    return copies


def pair_of(chosen):
    first, second = chosen[0], chosen[1]
    second = jnp.where(second == first, lax.rem(first + 1, GRAINS), second)
    return first, second


def others_of(chosen):
    first, second = pair_of(chosen)
    low, high = jnp.minimum(first, second), jnp.maximum(first, second)

    def other(r):
        i = jnp.where(r >= low, r + 1, r)
        return jnp.where(i >= high, i + 1, i)

    return other


def start_kernel(jitter_any, ids_any, p0, p1, p2, jitter, grain_ids, semaphores):
    planes = grain_ids.shape[0]
    pairs = []
    for k in range(planes):
        pairs.append((jitter_any.at[:, k], jitter.at[:, k]))
        pairs.append((ids_any.at[k], grain_ids.at[k]))
    copies = fetch(pairs, semaphores)
    for k, out in enumerate((p0, p1, p2)):
        copies[2 * k].wait()
        copies[2 * k + 1].wait()
        ids = grain_ids[k]
        for i in range(GRAINS):
            base = jnp.where(ids == i, jnp.float32(0.6), jnp.float32(0.0))
            out[i] = base + jitter[i, k].astype(F32)


def grain_of(start):
    ids = jnp.where(start[1] > 0.55, 1, 0)
    for g in range(2, GRAINS):
        ids = jnp.where(start[g] > 0.55, g, ids)
    return ids


def rate(classes, ids, i):
    def level(g):
        return 0.12 * (0.4 + 0.2 * classes[g, i].astype(F32))

    value = jnp.full(ids.shape, level(0), F32)
    for g in range(1, GRAINS):
        value = jnp.where(ids == g, level(g), value)
    return value


def squares(state):
    total = state[0] * state[0]
    for i in range(1, GRAINS):
        total = total + state[i] * state[i]
    return 5.0 + 3.0 * total


def update(e, before, after, total, mobility):
    depth, width = e.shape
    near = before + after
    near = near + (pltpu.roll(e, 1, 0) + pltpu.roll(e, depth - 1, 0))
    near = near + (pltpu.roll(e, 1, 1) + pltpu.roll(e, width - 1, 1))
    return e + mobility * (near - e * (total - 2.0 * (e * e)))


def step_plane(center, before, after, mobility, out):
    total = squares(center)
    for i in range(GRAINS):
        out[i] = update(center[i], before[i], after[i], total, mobility[i])


def rates_plane(classes, start, out):
    ids = grain_of(start)
    for i in range(GRAINS):
        out[i] = rate(classes, ids, i)


def inner_kernel(
    chosen_any, classes_any, p0, p1, p2, up2, down2, r0, r2, rates, middle, chosen, classes, semaphores
):
    copies = fetch(((chosen_any, chosen), (classes_any, classes)), semaphores)
    for i in range(GRAINS):
        up2[i] = p1[i]
        down2[i] = p1[i]
    for copy in copies:
        copy.wait()
    for k, i in enumerate(pair_of(chosen)):
        up2[GRAINS + k] = p0[i]
        down2[GRAINS + k] = p2[i]
    other = others_of(chosen)
    for r in range(GRAINS - 2):
        i = other(r)
        r0[r] = p0[i]
        r2[r] = p2[i]
    for k, start in enumerate((p0, p1, p2)):
        rates_plane(classes, start, rates.at[k])
    step_plane(p1, p0, p2, rates.at[1], middle)


def groups(ref, count, base=0):
    return [ref.at[pl.ds(base + k * GRAINS, GRAINS)] for k in range(count)]


def near_kernel(classes_any, p0, p1, p2, prev1, next1, rates, middle, near_out, classes, semaphores):
    edge0, edge1, inner0, inner2, middle2 = groups(near_out, 5)
    copies = fetch(((classes_any, classes),), semaphores)
    step_plane(p0, prev1, p1, rates.at[0], inner0)
    step_plane(p2, p1, next1, rates.at[2], inner2)
    copies[0].wait()
    rates_plane(classes, prev1, edge0)
    rates_plane(classes, next1, edge1)
    step_plane(middle, inner0, inner2, rates.at[1], middle2)


def second_step(p0, p2, prev1, next1, prev2, next2, rates, middle, near_state, outer1, side2):
    edge_rates, inner1 = near_state[:2], near_state[2:4]
    step_plane(prev1, prev2, p0, edge_rates[0], outer1[0])
    step_plane(next1, p2, next2, edge_rates[1], outer1[1])
    step_plane(inner1[0], outer1[0], middle, rates.at[0], side2[0])
    step_plane(inner1[1], middle, outer1[1], rates.at[2], side2[1])


def pair_kernel(
    chosen_any, classes_any, p0, p2, prev1, next1, prev2, next2, rates, middle, near_out, high_any, low_any,
    packed, chosen, classes, high, low, second, edge, fields, semaphores,
):
    copies = fetch(
        ((chosen_any, chosen), (classes_any, classes), (high_any, high), (low_any, low)), semaphores
    )
    near_state = groups(near_out, 5)
    edge_rates, inner1, middle2 = near_state[:2], near_state[2:4], near_state[4]
    outer1, side2 = groups(second, 2), groups(second, 2, 2 * GRAINS)
    second_step(p0, p2, prev1, next1, prev2, next2, rates, middle, near_state, outer1, side2)
    eta2 = (side2[0], middle2, side2[1])
    depth, width = p0.shape[1:]
    totals = [squares(state) for state in eta2]
    copies[0].wait()
    copies[1].wait()
    pair = pair_of(chosen)
    for side, (mid, near) in enumerate(((prev2, prev1), (next2, next1))):
        ids = grain_of(mid)
        total0 = squares(mid)
        total1 = squares(outer1[side])
        for k, i in enumerate(pair):
            first = update(mid[i], mid[GRAINS + k], near[i], total0, rate(classes, ids, i))
            edge[side, k] = update(outer1[side][i], first, inner1[side][i], total1, edge_rates[side][i])
    repeated = chosen[1] == chosen[0]
    for k in range(3):
        values = []
        for f, i in enumerate(pair):
            before = edge[0, f] if k == 0 else eta2[k - 1][i]
            after = edge[1, f] if k == 2 else eta2[k + 1][i]
            value = update(eta2[k][i], before, after, totals[k], rates[k, i])
            values.append(value)
        values[1] = jnp.where(repeated, values[0], values[1])
        for f in range(2):
            base = k * 2 * depth + f * depth
            fields[base : base + depth] = values[f]
    copies[2].wait()
    copies[3].wait()
    full = dot3((high[...], low[...]), split(fields[...]), ((1,), (1,)))
    slots = width // 2
    lanes = 4 * depth
    half = lanes // 2
    real_lane = lax.broadcasted_iota(jnp.int32, (slots, lanes), 1) < half
    for k in range(3):
        at = slice(k // 2 * lanes, k // 2 * lanes + lanes)
        cosine, sine = full[:slots, at], full[slots:, at]
        if k % 2:
            cosine = pltpu.roll(cosine, half, 1)
        else:
            sine = pltpu.roll(sine, half, 1)
        part = jnp.where(real_lane, cosine, sine)
        if packed.shape[0] == 3:
            packed[k] = part
        else:
            devices, rows, _ = packed.shape
            rows = rows // 3
            packed[:, k * rows : (k + 1) * rows, :] = part.reshape(devices, rows, lanes)


def rest_kernel(
    prev3, next3,
    chosen_any, classes_any, p0_any, p2_any, prev1_any, next1_any, prev2_any, next2_any, near_any, middle_any,
    rates_any, out_any,
    chosen, classes, p0, p2, prev1, next1, prev2, next2, near_out, middle, rates, second, edge, out, semaphores,
):
    near_state, near_source = groups(near_out, 5), groups(near_any, 5)
    edge_rates, inner1, middle2 = near_state[:2], near_state[2:4], near_state[4]
    outer1, side2 = groups(second, 2), groups(second, 2, 2 * GRAINS)
    copies = fetch(
        (
            (prev1_any, prev1), (prev2_any, prev2), (p0_any, p0), (near_source[0], near_state[0]),
            (next1_any, next1), (next2_any, next2), (p2_any, p2), (near_source[1], near_state[1]),
            (near_source[2], near_state[2]), (middle_any, middle), (rates_any.at[0], rates.at[0]),
            (near_source[3], near_state[3]), (rates_any.at[2], rates.at[2]),
            (chosen_any, chosen), (classes_any, classes),
            (near_source[4], near_state[4]), (rates_any.at[1], rates.at[1]),
        ),
        semaphores,
    )

    def wait(first, last):
        for copy in copies[first:last]:
            copy.wait()

    wait(0, 4)
    step_plane(prev1, prev2, p0, edge_rates[0], outer1[0])
    wait(4, 8)
    step_plane(next1, p2, next2, edge_rates[1], outer1[1])
    wait(8, 11)
    step_plane(inner1[0], outer1[0], middle, rates.at[0], side2[0])
    wait(11, 13)
    step_plane(inner1[1], middle, outer1[1], rates.at[2], side2[1])
    wait(13, 17)
    other = others_of(chosen)
    pair = pair_of(chosen)
    places = [(pair[k], GRAINS + k, None) for k in range(2)] + [(other(r), None, r) for r in range(GRAINS - 2)]
    eta2 = (side2[0], middle2, side2[1])
    outs = []

    def finish(plane):
        total = squares(eta2[plane])
        for k, (i, _, _) in enumerate(places):
            before = edge[0, k] if plane == 0 else eta2[plane - 1][i]
            after = edge[1, k] if plane == 2 else eta2[plane + 1][i]
            out[i, plane] = update(eta2[plane][i], before, after, total, rates[plane, i])
        outs.extend(fetch(((out.at[:, plane], out_any.at[:, plane]),), semaphores.at[pl.ds(17 + plane, 1)]))

    finish(1)
    for side, (far, mid, near) in enumerate(((prev3, prev2, prev1), (next3, next2, next1))):
        ids = grain_of(mid)
        total0 = squares(mid)
        total1 = squares(outer1[side])
        for k, (i, early, late) in enumerate(places):
            third = far[late] if early is None else mid[early]
            first = update(mid[i], third, near[i], total0, rate(classes, ids, i))
            edge[side, k] = update(outer1[side][i], first, inner1[side][i], total1, edge_rates[side][i])
        finish(2 * side)
    for copy in outs:
        copy.wait()


def line_kernel(lines, z_forward, z_inverse, x_both, out, wide, tall, scale):
    rows, lanes = lines.shape
    total_x = wide.shape[0] // 3
    slots = rows // total_x
    half = lanes // 2

    def over_x(pieces, chunk=2):
        results = []
        for j in range(0, slots, chunk):
            group = pieces[j : j + chunk]
            high, low = split(jnp.concatenate(group, axis=1))
            stacked = jnp.concatenate([high, low, high], axis=0)
            both = jnp.dot(x_both[...], stacked, preferred_element_type=F32)
            for k in range(len(group)):
                at = slice(k * lanes, (k + 1) * lanes)
                results.append((both[:total_x, at], both[total_x:, at]))
        return results

    def put(row, even, odd):
        at = slice(row * total_x, (row + 1) * total_x)
        for base, value in ((0, even), (lanes, odd)):
            high, low = split(value)
            tall[0, at, base : base + lanes] = high
            tall[1, at, base : base + lanes] = low

    real_lane = lax.broadcasted_iota(jnp.int32, (total_x, lanes), 1) < half
    turned = over_x([lines[pl.ds(j, total_x, stride=slots), :] for j in range(slots)])
    for j, (even, odd) in enumerate(turned):
        put(j, even, odd)
    first_even, first_odd = turned[0]
    put(slots, jnp.where(real_lane, first_even, 0.0), jnp.where(real_lane, first_odd, 0.0))
    put(
        slots + 1,
        jnp.where(real_lane, pltpu.roll(first_even, half, 1), 0.0),
        jnp.where(real_lane, pltpu.roll(first_odd, half, 1), 0.0),
    )
    step = 2 * total_x
    parts = []
    for row in range(0, (slots + 2) * total_x, step):
        at = slice(row, row + step)
        part = dot3((tall[0, at], tall[1, at]), (z_forward[0], z_forward[1]))
        part = part * part
        part = part + pltpu.roll(part, half, 1)
        parts += [part[:total_x], part[total_x:]]

    def power(j):
        return parts[j]

    first = lax.axis_index("gx") == 0
    lane = lax.broadcasted_iota(jnp.int32, (total_x, lanes), 1)
    line = lax.broadcasted_iota(jnp.int32, (total_x, lanes), 0)
    constant = jnp.logical_and(line == 0, jnp.logical_or(lane == 0, lane == half // 2))
    powers = []
    for j in range(slots):
        value = jnp.where(real_lane, power(j), 0.0) * (2.0 * scale)
        if j == 0:
            special = jnp.where(real_lane, power(slots), power(slots + 1)) * scale
            special = jnp.where(constant, 0.0, special)
            value = jnp.where(first, special, value)
        powers.append(value)
    for j, (even, odd) in enumerate(over_x(powers)):
        put(j, even, odd)
    for j in range(0, slots, 2):
        at = slice(j * total_x, (j + 2) * total_x)
        back = dot3((tall[0, at], tall[1, at]), (z_inverse[0], z_inverse[1]))
        out[pl.ds(j, total_x, stride=slots), :] = back[:total_x]
        out[pl.ds(j + 1, total_x, stride=slots), :] = back[total_x:]


def finish_kernel(returned, high, low, out_any, out, semaphores):
    fields, planes, depth, width = out.shape
    lanes = 2 * fields * depth
    half = lanes // 2
    slots = width // 2
    stacked = []
    for k in range(planes):
        if returned.shape[0] == planes:
            part = returned[k]
        else:
            devices, rows, _ = returned.shape
            rows = rows // planes
            part = returned[:, k * rows : (k + 1) * rows, :].reshape(slots, lanes)
        part = part.T
        stacked.append(jnp.concatenate([part[:half], part[half:]], axis=1))
    stacked = split(jnp.concatenate(stacked, axis=0))
    copies = []
    for piece in range(2):
        at = slice(piece * slots, (piece + 1) * slots)
        result = dot3(stacked, (high[:, at], low[:, at]))
        for k in range(planes):
            for f in range(fields):
                base = k * half + f * depth
                out[f, k, :, at] = result[base : base + depth]
        copies += fetch(((out.at[:, :, :, at], out_any.at[:, :, :, at]),), semaphores.at[pl.ds(piece, 1)])
    for copy in copies:
        copy.wait()


def call(kernel, outs, in_specs, *args, scratch=(), flops=0, moved=0, limit=12, out_specs=None):
    args = [pltpu.with_memory_space_constraint(a, pltpu.HBM) if b is ANY else a for a, b in zip(args, in_specs)]
    return pl.pallas_call(
        kernel,
        out_shape=outs,
        in_specs=in_specs,
        out_specs=out_specs or jax.tree.map(lambda _: VMEM, outs),
        scratch_shapes=scratch,
        compiler_params=pltpu.CompilerParams(vmem_limit_bytes=limit * MIB),
        cost_estimate=pl.CostEstimate(flops=flops, bytes_accessed=moved, transcendentals=0),
    )(*args)


def shards(grain_ids, jitter, class_table, chosen):
    planes, depth, width = grain_ids.shape
    devices = lax.axis_size("gx")
    total_x = planes * devices
    count = float(total_x * depth * width)
    slots = width // 2
    share = slots // devices
    lanes = 4 * depth
    up = [(i, (i + 1) % devices) for i in range(devices)]
    down = [(j, i) for i, j in up]
    aligned = share % 8 == 0

    def shape(*dims):
        return jax.ShapeDtypeStruct(dims, F32)

    plane = (GRAINS, depth, width)
    table = [jnp.asarray(part) for part in halves(y_table(width))]
    z_forward, z_inverse = z_tables(depth)
    z_parts = [jnp.asarray(np.stack(halves(matrix))) for matrix in (z_forward, z_inverse)]
    x_high, x_low = halves(np.concatenate(phases(total_x), axis=0))
    x_both = jnp.asarray(np.concatenate([x_high, x_high, x_low], axis=1))

    two = (2, *plane)
    six = (GRAINS - 2, depth, width)
    small = [pltpu.SMEM((2,), jnp.int32), pltpu.SMEM((GRAINS, GRAINS), jnp.int32)]
    ten = (GRAINS + 2, depth, width)
    p0, p1, p2 = call(
        start_kernel,
        (shape(*plane), shape(*plane), shape(*plane)),
        [ANY] * 2,
        jitter, grain_ids,
        scratch=[
            pltpu.VMEM(jitter.shape, jitter.dtype),
            pltpu.VMEM(grain_ids.shape, jnp.int32),
            pltpu.SemaphoreType.DMA((2 * planes,)),
        ],
        flops=2**21, moved=2**22,
    )
    prev1 = lax.ppermute(p2, "gx", up)
    next1 = lax.ppermute(p0, "gx", down)
    up2, down2, r0, r2, rates, middle = call(
        inner_kernel,
        (
            shape(*ten), shape(*ten), shape(*six), shape(*six),
            shape(planes, *plane), shape(*plane),
        ),
        [ANY] * 2 + [VMEM] * 3,
        chosen, class_table, p0, p1, p2,
        scratch=[*small, pltpu.SemaphoreType.DMA((2,))],
        flops=2**24, moved=2**22,
    )
    prev2 = lax.ppermute(up2, "gx", up)
    next2 = lax.ppermute(down2, "gx", down)
    r0, r2, prev1, next1 = lax.optimization_barrier((r0, r2, prev1, next1))
    prev3 = lax.ppermute(r0, "gx", up)
    next3 = lax.ppermute(r2, "gx", down)
    near_out = call(
        near_kernel,
        shape(5 * GRAINS, depth, width),
        [ANY] + [VMEM] * 7,
        class_table, p0, p1, p2, prev1, next1, rates, middle,
        scratch=[small[1], pltpu.SemaphoreType.DMA((1,))],
        flops=2**25, moved=2**24,
    )
    packed_shape = (devices, planes * share, lanes) if aligned else (planes, slots, lanes)
    packed = call(
        pair_kernel,
        shape(*packed_shape),
        [ANY] * 2 + [VMEM] * 9 + [ANY] * 2,
        chosen, class_table, p0, p2, prev1, next1, prev2, next2, rates, middle, near_out, *table,
        scratch=[
            *small,
            pltpu.VMEM(table[0].shape, BF16),
            pltpu.VMEM(table[1].shape, BF16),
            pltpu.VMEM((4 * GRAINS, depth, width), F32),
            pltpu.VMEM((2, 2, depth, width), F32),
            pltpu.VMEM(((planes + 1) // 2 * lanes, width), F32),
            pltpu.SemaphoreType.DMA((4,)),
        ],
        flops=2**28, moved=2**23,
    )
    packed, prev3, next3 = lax.optimization_barrier((packed, prev3, next3))
    if aligned:
        lines = lax.all_to_all(packed, "gx", split_axis=0, concat_axis=0, tiled=True)
    else:
        lines = lax.all_to_all(packed, "gx", split_axis=1, concat_axis=0, tiled=True)
    lines = lines.reshape(total_x * share, lanes)

    def lines_body(*refs):
        line_kernel(*refs, scale=1.0 / (count * count))

    back = call(
        lines_body,
        shape(total_x * share, lanes),
        [VMEM] * 4,
        lines, *z_parts, x_both,
        scratch=[
            pltpu.VMEM((3 * total_x, share * lanes), BF16),
            pltpu.VMEM((2, total_x * (share + 2), 2 * lanes), BF16),
        ],
        flops=2**28, moved=2**22,
    )
    back = back.reshape(devices, planes * share, lanes)
    returned = lax.all_to_all(back, "gx", split_axis=0, concat_axis=0, tiled=True)
    if not aligned:
        returned = returned.reshape(devices, planes, share, lanes).transpose(1, 0, 2, 3)
        returned = returned.reshape(planes, slots, lanes)
    late = (
        prev3, next3,
        chosen, class_table, p0, p2, prev1, next1, prev2, next2, near_out, middle, rates,
    )
    late, _ = lax.optimization_barrier((late, back))
    order_params = call(
        rest_kernel,
        shape(GRAINS, planes, depth, width),
        [VMEM] * 2 + [ANY] * (len(late) - 2),
        *late,
        scratch=[
            *small,
            *[pltpu.VMEM(value.shape, F32) for value in late[4:]],
            pltpu.VMEM((4 * GRAINS, depth, width), F32),
            pltpu.VMEM((2, *plane), F32),
            pltpu.VMEM((GRAINS, planes, depth, width), F32),
            pltpu.SemaphoreType.DMA((17 + planes,)),
        ],
        out_specs=ANY, flops=2**37, moved=2**24, limit=24,
    )
    correlation = call(
        finish_kernel,
        shape(2, planes, depth, width),
        [VMEM] * 3,
        returned, *table,
        scratch=[pltpu.VMEM((2, planes, depth, width), F32), pltpu.SemaphoreType.DMA((2,))],
        out_specs=ANY,
        flops=2**28, moved=2**22,
    )
    return (order_params, correlation)


def solution(mesh):
    in_specs = (P(("grp", "gx"), None, None), P(None, ("grp", "gx"), None, None), P(), P())
    out_specs = (P(None, ("grp", "gx"), None, None), P(None, ("grp", "gx"), None, None))
    return jax.shard_map(shards, mesh=mesh, in_specs=in_specs, out_specs=out_specs, check_vma=False)
```

```python
import math

import jax
import jax.numpy as jnp
import ml_dtypes
import numpy as np
from jax import lax
from jax.experimental import pallas as pl
from jax.experimental.pallas import tpu as pltpu
from jax.sharding import PartitionSpec as P

STEPS = 3
GRAINS = 8
F32 = jnp.float32
BF16 = jnp.bfloat16
VMEM = pl.BlockSpec(memory_space=pltpu.VMEM)
ANY = pl.BlockSpec(memory_space=pltpu.HBM)
MIB = 2**20


def halves(table):
    table = np.asarray(table, np.float32)
    high = table.astype(ml_dtypes.bfloat16)
    low = (table - high.astype(np.float32)).astype(ml_dtypes.bfloat16)
    return high, low


def phases(length, rows=None):
    index = np.arange(length)
    product = np.arange(length if rows is None else rows)[:, None] * index[None, :] % length
    angle = product * (2.0 * math.pi / length)
    return np.cos(angle), np.sin(angle)


def y_table(width):
    cos_y, sin_y = phases(width, width // 2)
    sin_y = -sin_y
    sin_y[0] = 1.0 - 2.0 * (np.arange(width) % 2)
    return np.concatenate([cos_y, sin_y], axis=0)


def z_tables(depth):
    cos_z, sin_z = phases(depth)
    two = np.eye(2)
    cos_z, sin_z = np.kron(two, cos_z), np.kron(two, sin_z)
    forward = np.block([[cos_z, -sin_z], [sin_z, cos_z]])
    half = 2 * depth
    forward_turned = np.concatenate([forward[:, half:], -forward[:, :half]], axis=1)
    inverse = np.block([[cos_z, sin_z], [-sin_z, cos_z]])
    inverse_turned = np.concatenate([-inverse[:, half:], inverse[:, :half]], axis=1)
    return (
        np.concatenate([forward, forward_turned], axis=0),
        np.concatenate([inverse, inverse_turned], axis=0),
    )


def split(value):
    high = value.astype(BF16)
    low = (value - high.astype(F32)).astype(BF16)
    return high, low


def dot3(left, right, contract=((1,), (0,))):
    def one(a, b):
        return lax.dot_general(a, b, (contract, ((), ())), preferred_element_type=F32)

    return one(left[0], right[0]) + (one(left[0], right[1]) + one(left[1], right[0]))


def fetch(pairs, semaphores):
    copies = [pltpu.make_async_copy(src, dst, semaphores.at[k]) for k, (src, dst) in enumerate(pairs)]
    for copy in copies:
        copy.start()
    return copies


def pair_of(chosen):
    first, second = chosen[0], chosen[1]
    second = jnp.where(second == first, lax.rem(first + 1, GRAINS), second)
    return first, second


def others_of(chosen):
    first, second = pair_of(chosen)
    low, high = jnp.minimum(first, second), jnp.maximum(first, second)

    def other(r):
        i = jnp.where(r >= low, r + 1, r)
        return jnp.where(i >= high, i + 1, i)

    return other


def start_plane(jitter, grain_ids, out):
    ids = grain_ids[...]
    for i in range(GRAINS):
        base = jnp.where(ids == i, jnp.float32(0.6), jnp.float32(0.0))
        out[i] = base + jitter[i].astype(F32)


def start_kernel(jitter_any, ids_any, p0, p2, jitter, grain_ids, semaphores):
    pairs = []
    for k in range(2):
        pairs.append((jitter_any.at[:, 2 * k], jitter.at[:, k]))
        pairs.append((ids_any.at[2 * k], grain_ids.at[k]))
    copies = fetch(pairs, semaphores)
    for k, out in enumerate((p0, p2)):
        copies[2 * k].wait()
        copies[2 * k + 1].wait()
        start_plane(jitter.at[:, k], grain_ids.at[k], out)


def grain_of(start):
    ids = jnp.where(start[1] > 0.55, 1, 0)
    for g in range(2, GRAINS):
        ids = jnp.where(start[g] > 0.55, g, ids)
    return ids


def rate(classes, ids, i):
    def level(g):
        return 0.12 * (0.4 + 0.2 * classes[g, i].astype(F32))

    value = jnp.full(ids.shape, level(0), F32)
    for g in range(1, GRAINS):
        value = jnp.where(ids == g, level(g), value)
    return value


def squares(state):
    total = state[0] * state[0]
    for i in range(1, GRAINS):
        total = total + state[i] * state[i]
    return 5.0 + 3.0 * total


def update(e, before, after, total, mobility):
    depth, width = e.shape
    near = before + after
    near = near + (pltpu.roll(e, 1, 0) + pltpu.roll(e, depth - 1, 0))
    near = near + (pltpu.roll(e, 1, 1) + pltpu.roll(e, width - 1, 1))
    return e + mobility * (near - e * (total - 2.0 * (e * e)))


def step_plane(center, before, after, mobility, out):
    total = squares(center)
    for i in range(GRAINS):
        out[i] = update(center[i], before[i], after[i], total, mobility[i])


def rates_plane(classes, start, out):
    ids = grain_of(start)
    for i in range(GRAINS):
        out[i] = rate(classes, ids, i)


def inner_kernel(
    chosen_any, classes_any, jitter_any, ids_any, p0, p2,
    p1, up2, down2, r0, r2, rates, middle, chosen, classes, jitter, grain_ids, semaphores,
):
    copies = fetch(
        ((jitter_any.at[:, 1], jitter), (ids_any.at[1], grain_ids), (chosen_any, chosen), (classes_any, classes)),
        semaphores,
    )
    copies[0].wait()
    copies[1].wait()
    start_plane(jitter, grain_ids, p1)
    for i in range(GRAINS):
        up2[i] = p1[i]
        down2[i] = p1[i]
    for copy in copies[2:]:
        copy.wait()
    for k, i in enumerate(pair_of(chosen)):
        up2[GRAINS + k] = p0[i]
        down2[GRAINS + k] = p2[i]
    other = others_of(chosen)
    for r in range(GRAINS - 2):
        i = other(r)
        r0[r] = p0[i]
        r2[r] = p2[i]
    for k, start in enumerate((p0, p1, p2)):
        rates_plane(classes, start, rates.at[k])
    step_plane(p1, p0, p2, rates.at[1], middle)


def groups(ref, count, base=0):
    return [ref.at[pl.ds(base + k * GRAINS, GRAINS)] for k in range(count)]


def near_kernel(classes_any, p0, p1, p2, prev1, next1, rates, middle, near_out, classes, semaphores):
    edge0, edge1, inner0, inner2, middle2 = groups(near_out, 5)
    copies = fetch(((classes_any, classes),), semaphores)
    step_plane(p0, prev1, p1, rates.at[0], inner0)
    step_plane(p2, p1, next1, rates.at[2], inner2)
    copies[0].wait()
    rates_plane(classes, prev1, edge0)
    rates_plane(classes, next1, edge1)
    step_plane(middle, inner0, inner2, rates.at[1], middle2)


def second_step(p0, p2, prev1, next1, prev2, next2, rates, middle, near_state, outer1, side2):
    edge_rates, inner1 = near_state[:2], near_state[2:4]
    step_plane(prev1, prev2, p0, edge_rates[0], outer1[0])
    step_plane(next1, p2, next2, edge_rates[1], outer1[1])
    step_plane(inner1[0], outer1[0], middle, rates.at[0], side2[0])
    step_plane(inner1[1], middle, outer1[1], rates.at[2], side2[1])


def pair_kernel(
    chosen_any, classes_any, p0, p2, prev1, next1, prev2, next2, rates, middle, near_out, high_any, low_any,
    packed, chosen, classes, high, low, second, edge, fields, semaphores,
):
    copies = fetch(
        ((chosen_any, chosen), (classes_any, classes), (high_any, high), (low_any, low)), semaphores
    )
    near_state = groups(near_out, 5)
    edge_rates, inner1, middle2 = near_state[:2], near_state[2:4], near_state[4]
    outer1, side2 = groups(second, 2), groups(second, 2, 2 * GRAINS)
    second_step(p0, p2, prev1, next1, prev2, next2, rates, middle, near_state, outer1, side2)
    eta2 = (side2[0], middle2, side2[1])
    depth, width = p0.shape[1:]
    totals = [squares(state) for state in eta2]
    copies[0].wait()
    copies[1].wait()
    pair = pair_of(chosen)
    for side, (mid, near) in enumerate(((prev2, prev1), (next2, next1))):
        ids = grain_of(mid)
        total0 = squares(mid)
        total1 = squares(outer1[side])
        for k, i in enumerate(pair):
            first = update(mid[i], mid[GRAINS + k], near[i], total0, rate(classes, ids, i))
            edge[side, k] = update(outer1[side][i], first, inner1[side][i], total1, edge_rates[side][i])
    repeated = chosen[1] == chosen[0]
    for k in range(3):
        values = []
        for f, i in enumerate(pair):
            before = edge[0, f] if k == 0 else eta2[k - 1][i]
            after = edge[1, f] if k == 2 else eta2[k + 1][i]
            value = update(eta2[k][i], before, after, totals[k], rates[k, i])
            values.append(value)
        values[1] = jnp.where(repeated, values[0], values[1])
        for f in range(2):
            base = k * 2 * depth + f * depth
            fields[base : base + depth] = values[f]
    copies[2].wait()
    copies[3].wait()
    full = dot3((high[...], low[...]), split(fields[...]), ((1,), (1,)))
    slots = width // 2
    lanes = 4 * depth
    half = lanes // 2
    real_lane = lax.broadcasted_iota(jnp.int32, (slots, lanes), 1) < half
    for k in range(3):
        at = slice(k // 2 * lanes, k // 2 * lanes + lanes)
        cosine, sine = full[:slots, at], full[slots:, at]
        if k % 2:
            cosine = pltpu.roll(cosine, half, 1)
        else:
            sine = pltpu.roll(sine, half, 1)
        part = jnp.where(real_lane, cosine, sine)
        if packed.shape[0] == 3:
            packed[k] = part
        else:
            devices, rows, _ = packed.shape
            rows = rows // 3
            packed[:, k * rows : (k + 1) * rows, :] = part.reshape(devices, rows, lanes)


def rest_kernel(
    prev3, next3,
    chosen_any, classes_any, p0_any, p2_any, prev1_any, next1_any, prev2_any, next2_any, near_any, middle_any,
    rates_any, out_any,
    chosen, classes, p0, p2, prev1, next1, prev2, next2, near_out, middle, rates, second, edge, out, semaphores,
):
    near_state, near_source = groups(near_out, 5), groups(near_any, 5)
    edge_rates, inner1, middle2 = near_state[:2], near_state[2:4], near_state[4]
    outer1, side2 = groups(second, 2), groups(second, 2, 2 * GRAINS)
    copies = fetch(
        (
            (prev1_any, prev1), (prev2_any, prev2), (p0_any, p0), (near_source[0], near_state[0]),
            (next1_any, next1), (next2_any, next2), (p2_any, p2), (near_source[1], near_state[1]),
            (near_source[2], near_state[2]), (middle_any, middle), (rates_any.at[0], rates.at[0]),
            (near_source[3], near_state[3]), (rates_any.at[2], rates.at[2]),
            (chosen_any, chosen), (classes_any, classes),
            (near_source[4], near_state[4]), (rates_any.at[1], rates.at[1]),
        ),
        semaphores,
    )

    def wait(first, last):
        for copy in copies[first:last]:
            copy.wait()

    wait(0, 4)
    step_plane(prev1, prev2, p0, edge_rates[0], outer1[0])
    wait(4, 8)
    step_plane(next1, p2, next2, edge_rates[1], outer1[1])
    wait(8, 11)
    step_plane(inner1[0], outer1[0], middle, rates.at[0], side2[0])
    wait(11, 13)
    step_plane(inner1[1], middle, outer1[1], rates.at[2], side2[1])
    wait(13, 17)
    other = others_of(chosen)
    pair = pair_of(chosen)
    places = [(pair[k], GRAINS + k, None) for k in range(2)] + [(other(r), None, r) for r in range(GRAINS - 2)]
    eta2 = (side2[0], middle2, side2[1])
    outs = []

    def finish(plane):
        total = squares(eta2[plane])
        for k, (i, _, _) in enumerate(places):
            before = edge[0, k] if plane == 0 else eta2[plane - 1][i]
            after = edge[1, k] if plane == 2 else eta2[plane + 1][i]
            out[i, plane] = update(eta2[plane][i], before, after, total, rates[plane, i])
        outs.extend(fetch(((out.at[:, plane], out_any.at[:, plane]),), semaphores.at[pl.ds(17 + plane, 1)]))

    finish(1)
    for side, (far, mid, near) in enumerate(((prev3, prev2, prev1), (next3, next2, next1))):
        ids = grain_of(mid)
        total0 = squares(mid)
        total1 = squares(outer1[side])
        for k, (i, early, late) in enumerate(places):
            third = far[late] if early is None else mid[early]
            first = update(mid[i], third, near[i], total0, rate(classes, ids, i))
            edge[side, k] = update(outer1[side][i], first, inner1[side][i], total1, edge_rates[side][i])
        finish(2 * side)
    for copy in outs:
        copy.wait()


def line_kernel(lines, z_forward, z_inverse, x_both, out, wide, tall, scale):
    rows, lanes = lines.shape
    total_x = wide.shape[0] // 3
    slots = rows // total_x
    half = lanes // 2

    def over_x(pieces, chunk=2):
        results = []
        for j in range(0, slots, chunk):
            group = pieces[j : j + chunk]
            high, low = split(jnp.concatenate(group, axis=1))
            stacked = jnp.concatenate([high, low, high], axis=0)
            both = jnp.dot(x_both[...], stacked, preferred_element_type=F32)
            for k in range(len(group)):
                at = slice(k * lanes, (k + 1) * lanes)
                results.append((both[:total_x, at], both[total_x:, at]))
        return results

    def put(row, even, odd):
        at = slice(row * total_x, (row + 1) * total_x)
        for base, value in ((0, even), (lanes, odd)):
            high, low = split(value)
            tall[0, at, base : base + lanes] = high
            tall[1, at, base : base + lanes] = low

    real_lane = lax.broadcasted_iota(jnp.int32, (total_x, lanes), 1) < half
    turned = over_x([lines[pl.ds(j, total_x, stride=slots), :] for j in range(slots)])
    for j, (even, odd) in enumerate(turned):
        put(j, even, odd)
    first_even, first_odd = turned[0]
    put(slots, jnp.where(real_lane, first_even, 0.0), jnp.where(real_lane, first_odd, 0.0))
    put(
        slots + 1,
        jnp.where(real_lane, pltpu.roll(first_even, half, 1), 0.0),
        jnp.where(real_lane, pltpu.roll(first_odd, half, 1), 0.0),
    )
    step = 2 * total_x
    parts = []
    for row in range(0, (slots + 2) * total_x, step):
        at = slice(row, row + step)
        part = dot3((tall[0, at], tall[1, at]), (z_forward[0], z_forward[1]))
        part = part * part
        part = part + pltpu.roll(part, half, 1)
        parts += [part[:total_x], part[total_x:]]

    def power(j):
        return parts[j]

    first = lax.axis_index("gx") == 0
    lane = lax.broadcasted_iota(jnp.int32, (total_x, lanes), 1)
    line = lax.broadcasted_iota(jnp.int32, (total_x, lanes), 0)
    constant = jnp.logical_and(line == 0, jnp.logical_or(lane == 0, lane == half // 2))
    powers = []
    for j in range(slots):
        value = jnp.where(real_lane, power(j), 0.0) * (2.0 * scale)
        if j == 0:
            special = jnp.where(real_lane, power(slots), power(slots + 1)) * scale
            special = jnp.where(constant, 0.0, special)
            value = jnp.where(first, special, value)
        powers.append(value)
    for j, (even, odd) in enumerate(over_x(powers)):
        put(j, even, odd)
    for j in range(0, slots, 2):
        at = slice(j * total_x, (j + 2) * total_x)
        back = dot3((tall[0, at], tall[1, at]), (z_inverse[0], z_inverse[1]))
        out[pl.ds(j, total_x, stride=slots), :] = back[:total_x]
        out[pl.ds(j + 1, total_x, stride=slots), :] = back[total_x:]


def finish_kernel(returned, high, low, out_any, out, semaphores):
    fields, planes, depth, width = out.shape
    lanes = 2 * fields * depth
    half = lanes // 2
    slots = width // 2
    stacked = []
    for k in range(planes):
        if returned.shape[0] == planes:
            part = returned[k]
        else:
            devices, rows, _ = returned.shape
            rows = rows // planes
            part = returned[:, k * rows : (k + 1) * rows, :].reshape(slots, lanes)
        part = part.T
        stacked.append(jnp.concatenate([part[:half], part[half:]], axis=1))
    stacked = split(jnp.concatenate(stacked, axis=0))
    copies = []
    for piece in range(2):
        at = slice(piece * slots, (piece + 1) * slots)
        result = dot3(stacked, (high[:, at], low[:, at]))
        for k in range(planes):
            for f in range(fields):
                base = k * half + f * depth
                out[f, k, :, at] = result[base : base + depth]
        copies += fetch(((out.at[:, :, :, at], out_any.at[:, :, :, at]),), semaphores.at[pl.ds(piece, 1)])
    for copy in copies:
        copy.wait()


def call(kernel, outs, in_specs, *args, scratch=(), flops=0, moved=0, limit=12, out_specs=None):
    args = [pltpu.with_memory_space_constraint(a, pltpu.HBM) if b is ANY else a for a, b in zip(args, in_specs)]
    return pl.pallas_call(
        kernel,
        out_shape=outs,
        in_specs=in_specs,
        out_specs=out_specs or jax.tree.map(lambda _: VMEM, outs),
        scratch_shapes=scratch,
        compiler_params=pltpu.CompilerParams(vmem_limit_bytes=limit * MIB),
        cost_estimate=pl.CostEstimate(flops=flops, bytes_accessed=moved, transcendentals=0),
    )(*args)


def shards(grain_ids, jitter, class_table, chosen):
    planes, depth, width = grain_ids.shape
    devices = lax.axis_size("gx")
    total_x = planes * devices
    count = float(total_x * depth * width)
    slots = width // 2
    share = slots // devices
    lanes = 4 * depth
    up = [(i, (i + 1) % devices) for i in range(devices)]
    down = [(j, i) for i, j in up]
    aligned = share % 8 == 0

    def shape(*dims):
        return jax.ShapeDtypeStruct(dims, F32)

    plane = (GRAINS, depth, width)
    table = [jnp.asarray(part) for part in halves(y_table(width))]
    z_forward, z_inverse = z_tables(depth)
    z_parts = [jnp.asarray(np.stack(halves(matrix))) for matrix in (z_forward, z_inverse)]
    x_high, x_low = halves(np.concatenate(phases(total_x), axis=0))
    x_both = jnp.asarray(np.concatenate([x_high, x_high, x_low], axis=1))

    two = (2, *plane)
    six = (GRAINS - 2, depth, width)
    small = [pltpu.SMEM((2,), jnp.int32), pltpu.SMEM((GRAINS, GRAINS), jnp.int32)]
    ten = (GRAINS + 2, depth, width)
    p0, p2 = call(
        start_kernel,
        (shape(*plane), shape(*plane)),
        [ANY] * 2,
        jitter, grain_ids,
        scratch=[
            pltpu.VMEM((GRAINS, 2, depth, width), jitter.dtype),
            pltpu.VMEM((2, depth, width), jnp.int32),
            pltpu.SemaphoreType.DMA((4,)),
        ],
        flops=2**21, moved=2**22,
    )
    prev1 = lax.ppermute(p2, "gx", up)
    next1 = lax.ppermute(p0, "gx", down)
    p1, up2, down2, r0, r2, rates, middle = call(
        inner_kernel,
        (
            shape(*plane), shape(*ten), shape(*ten), shape(*six), shape(*six),
            shape(planes, *plane), shape(*plane),
        ),
        [ANY] * 4 + [VMEM] * 2,
        chosen, class_table, jitter, grain_ids, p0, p2,
        scratch=[
            *small,
            pltpu.VMEM((GRAINS, depth, width), jitter.dtype),
            pltpu.VMEM((depth, width), jnp.int32),
            pltpu.SemaphoreType.DMA((4,)),
        ],
        flops=2**24, moved=2**22,
    )
    prev2 = lax.ppermute(up2, "gx", up)
    next2 = lax.ppermute(down2, "gx", down)
    r0, r2, prev1, next1 = lax.optimization_barrier((r0, r2, prev1, next1))
    prev3 = lax.ppermute(r0, "gx", up)
    next3 = lax.ppermute(r2, "gx", down)
    near_out = call(
        near_kernel,
        shape(5 * GRAINS, depth, width),
        [ANY] + [VMEM] * 7,
        class_table, p0, p1, p2, prev1, next1, rates, middle,
        scratch=[small[1], pltpu.SemaphoreType.DMA((1,))],
        flops=2**25, moved=2**24,
    )
    packed_shape = (devices, planes * share, lanes) if aligned else (planes, slots, lanes)
    packed = call(
        pair_kernel,
        shape(*packed_shape),
        [ANY] * 2 + [VMEM] * 9 + [ANY] * 2,
        chosen, class_table, p0, p2, prev1, next1, prev2, next2, rates, middle, near_out, *table,
        scratch=[
            *small,
            pltpu.VMEM(table[0].shape, BF16),
            pltpu.VMEM(table[1].shape, BF16),
            pltpu.VMEM((4 * GRAINS, depth, width), F32),
            pltpu.VMEM((2, 2, depth, width), F32),
            pltpu.VMEM(((planes + 1) // 2 * lanes, width), F32),
            pltpu.SemaphoreType.DMA((4,)),
        ],
        flops=2**28, moved=2**23,
    )
    packed, prev3, next3 = lax.optimization_barrier((packed, prev3, next3))
    if aligned:
        lines = lax.all_to_all(packed, "gx", split_axis=0, concat_axis=0, tiled=True)
    else:
        lines = lax.all_to_all(packed, "gx", split_axis=1, concat_axis=0, tiled=True)
    lines = lines.reshape(total_x * share, lanes)

    def lines_body(*refs):
        line_kernel(*refs, scale=1.0 / (count * count))

    back = call(
        lines_body,
        shape(total_x * share, lanes),
        [VMEM] * 4,
        lines, *z_parts, x_both,
        scratch=[
            pltpu.VMEM((3 * total_x, share * lanes), BF16),
            pltpu.VMEM((2, total_x * (share + 2), 2 * lanes), BF16),
        ],
        flops=2**28, moved=2**22,
    )
    back = back.reshape(devices, planes * share, lanes)
    returned = lax.all_to_all(back, "gx", split_axis=0, concat_axis=0, tiled=True)
    if not aligned:
        returned = returned.reshape(devices, planes, share, lanes).transpose(1, 0, 2, 3)
        returned = returned.reshape(planes, slots, lanes)
    late = (
        prev3, next3,
        chosen, class_table, p0, p2, prev1, next1, prev2, next2, near_out, middle, rates,
    )
    late, _ = lax.optimization_barrier((late, back))
    order_params = call(
        rest_kernel,
        shape(GRAINS, planes, depth, width),
        [VMEM] * 2 + [ANY] * (len(late) - 2),
        *late,
        scratch=[
            *small,
            *[pltpu.VMEM(value.shape, F32) for value in late[4:]],
            pltpu.VMEM((4 * GRAINS, depth, width), F32),
            pltpu.VMEM((2, *plane), F32),
            pltpu.VMEM((GRAINS, planes, depth, width), F32),
            pltpu.SemaphoreType.DMA((17 + planes,)),
        ],
        out_specs=ANY, flops=2**37, moved=2**24, limit=24,
    )
    correlation = call(
        finish_kernel,
        shape(2, planes, depth, width),
        [VMEM] * 3,
        returned, *table,
        scratch=[pltpu.VMEM((2, planes, depth, width), F32), pltpu.SemaphoreType.DMA((2,))],
        out_specs=ANY,
        flops=2**28, moved=2**22,
    )
    return (order_params, correlation)


def solution(mesh):
    in_specs = (P(("grp", "gx"), None, None), P(None, ("grp", "gx"), None, None), P(), P())
    out_specs = (P(None, ("grp", "gx"), None, None), P(None, ("grp", "gx"), None, None))
    return jax.shard_map(shards, mesh=mesh, in_specs=in_specs, out_specs=out_specs, check_vma=False)
```

```python
import math

import jax
import jax.numpy as jnp
import ml_dtypes
import numpy as np
from jax import lax
from jax.experimental import pallas as pl
from jax.experimental.pallas import tpu as pltpu
from jax.sharding import PartitionSpec as P

STEPS = 3
GRAINS = 8
F32 = jnp.float32
BF16 = jnp.bfloat16
VMEM = pl.BlockSpec(memory_space=pltpu.VMEM)
ANY = pl.BlockSpec(memory_space=pltpu.HBM)
MIB = 2**20


def halves(table):
    table = np.asarray(table, np.float32)
    high = table.astype(ml_dtypes.bfloat16)
    low = (table - high.astype(np.float32)).astype(ml_dtypes.bfloat16)
    return high, low


def phases(length, rows=None):
    index = np.arange(length)
    product = np.arange(length if rows is None else rows)[:, None] * index[None, :] % length
    angle = product * (2.0 * math.pi / length)
    return np.cos(angle), np.sin(angle)


def y_table(width):
    cos_y, sin_y = phases(width, width // 2)
    sin_y = -sin_y
    sin_y[0] = 1.0 - 2.0 * (np.arange(width) % 2)
    return np.concatenate([cos_y, sin_y], axis=0)


def z_tables(depth):
    cos_z, sin_z = phases(depth)
    two = np.eye(2)
    cos_z, sin_z = np.kron(two, cos_z), np.kron(two, sin_z)
    forward = np.block([[cos_z, -sin_z], [sin_z, cos_z]])
    half = 2 * depth
    forward_turned = np.concatenate([forward[:, half:], -forward[:, :half]], axis=1)
    inverse = np.block([[cos_z, sin_z], [-sin_z, cos_z]])
    inverse_turned = np.concatenate([-inverse[:, half:], inverse[:, :half]], axis=1)
    return (
        np.concatenate([forward, forward_turned], axis=0),
        np.concatenate([inverse, inverse_turned], axis=0),
    )


def split(value):
    high = value.astype(BF16)
    low = (value - high.astype(F32)).astype(BF16)
    return high, low


def dot3(left, right, contract=((1,), (0,))):
    def one(a, b):
        return lax.dot_general(a, b, (contract, ((), ())), preferred_element_type=F32)

    return one(left[0], right[0]) + (one(left[0], right[1]) + one(left[1], right[0]))


def fetch(pairs, semaphores):
    copies = [pltpu.make_async_copy(src, dst, semaphores.at[k]) for k, (src, dst) in enumerate(pairs)]
    for copy in copies:
        copy.start()
    return copies


def pair_of(chosen):
    first, second = chosen[0], chosen[1]
    second = jnp.where(second == first, lax.rem(first + 1, GRAINS), second)
    return first, second


def others_of(chosen):
    first, second = pair_of(chosen)
    low, high = jnp.minimum(first, second), jnp.maximum(first, second)

    def other(r):
        i = jnp.where(r >= low, r + 1, r)
        return jnp.where(i >= high, i + 1, i)

    return other


def start_kernel(jitter_any, ids_any, p0, p1, p2, jitter, grain_ids, semaphores):
    planes = grain_ids.shape[0]
    pairs = []
    for k in range(planes):
        pairs.append((jitter_any.at[:, k], jitter.at[:, k]))
        pairs.append((ids_any.at[k], grain_ids.at[k]))
    copies = fetch(pairs, semaphores)
    for k, out in enumerate((p0, p1, p2)):
        copies[2 * k].wait()
        copies[2 * k + 1].wait()
        ids = grain_ids[k]
        for i in range(GRAINS):
            base = jnp.where(ids == i, jnp.float32(0.6), jnp.float32(0.0))
            out[i] = base + jitter[i, k].astype(F32)


def grain_of(start):
    ids = jnp.where(start[1] > 0.55, 1, 0)
    for g in range(2, GRAINS):
        ids = jnp.where(start[g] > 0.55, g, ids)
    return ids


def rate(classes, ids, i):
    def level(g):
        return 0.12 * (0.4 + 0.2 * classes[g, i].astype(F32))

    value = jnp.full(ids.shape, level(0), F32)
    for g in range(1, GRAINS):
        value = jnp.where(ids == g, level(g), value)
    return value


def squares(state):
    total = state[0] * state[0]
    for i in range(1, GRAINS):
        total = total + state[i] * state[i]
    return 5.0 + 3.0 * total


def update(e, before, after, total, mobility):
    depth, width = e.shape
    near = before + after
    near = near + (pltpu.roll(e, 1, 0) + pltpu.roll(e, depth - 1, 0))
    near = near + (pltpu.roll(e, 1, 1) + pltpu.roll(e, width - 1, 1))
    return e + mobility * (near - e * (total - 2.0 * (e * e)))


def step_plane(center, before, after, mobility, out):
    total = squares(center)
    for i in range(GRAINS):
        out[i] = update(center[i], before[i], after[i], total, mobility[i])


def rates_plane(classes, start, out):
    ids = grain_of(start)
    for i in range(GRAINS):
        out[i] = rate(classes, ids, i)


def inner_kernel(
    chosen_any, classes_any, p0, p1, p2, up2, down2, r0, r2, rates, middle, chosen, classes, semaphores
):
    copies = fetch(((chosen_any, chosen), (classes_any, classes)), semaphores)
    for i in range(GRAINS):
        up2[i] = p1[i]
        down2[i] = p1[i]
    for copy in copies:
        copy.wait()
    for k, i in enumerate(pair_of(chosen)):
        up2[GRAINS + k] = p0[i]
        down2[GRAINS + k] = p2[i]
    other = others_of(chosen)
    for r in range(GRAINS - 2):
        i = other(r)
        r0[r] = p0[i]
        r2[r] = p2[i]
    for k, start in enumerate((p0, p1, p2)):
        rates_plane(classes, start, rates.at[k])
    step_plane(p1, p0, p2, rates.at[1], middle)


def groups(ref, count, base=0):
    return [ref.at[pl.ds(base + k * GRAINS, GRAINS)] for k in range(count)]


def near_kernel(classes_any, p0, p1, p2, prev1, next1, rates, middle, near_out, classes, semaphores):
    edge0, edge1, inner0, inner2, middle2 = groups(near_out, 5)
    copies = fetch(((classes_any, classes),), semaphores)
    step_plane(p0, prev1, p1, rates.at[0], inner0)
    step_plane(p2, p1, next1, rates.at[2], inner2)
    copies[0].wait()
    rates_plane(classes, prev1, edge0)
    rates_plane(classes, next1, edge1)
    step_plane(middle, inner0, inner2, rates.at[1], middle2)


def second_step(p0, p2, prev1, next1, prev2, next2, rates, middle, near_state, outer1, side2):
    edge_rates, inner1 = near_state[:2], near_state[2:4]
    step_plane(prev1, prev2, p0, edge_rates[0], outer1[0])
    step_plane(next1, p2, next2, edge_rates[1], outer1[1])
    step_plane(inner1[0], outer1[0], middle, rates.at[0], side2[0])
    step_plane(inner1[1], middle, outer1[1], rates.at[2], side2[1])


def pair_kernel(
    chosen_any, classes_any, p0, p2, prev1, next1, prev2, next2, rates, middle, near_out, high_any, low_any,
    packed, chosen, classes, high, low, second, edge, fields, semaphores,
):
    copies = fetch(
        ((chosen_any, chosen), (classes_any, classes), (high_any, high), (low_any, low)), semaphores
    )
    near_state = groups(near_out, 5)
    edge_rates, inner1, middle2 = near_state[:2], near_state[2:4], near_state[4]
    outer1, side2 = groups(second, 2), groups(second, 2, 2 * GRAINS)
    second_step(p0, p2, prev1, next1, prev2, next2, rates, middle, near_state, outer1, side2)
    eta2 = (side2[0], middle2, side2[1])
    depth, width = p0.shape[1:]
    totals = [squares(state) for state in eta2]
    copies[0].wait()
    copies[1].wait()
    pair = pair_of(chosen)
    for side, (mid, near) in enumerate(((prev2, prev1), (next2, next1))):
        ids = grain_of(mid)
        total0 = squares(mid)
        total1 = squares(outer1[side])
        for k, i in enumerate(pair):
            first = update(mid[i], mid[GRAINS + k], near[i], total0, rate(classes, ids, i))
            edge[side, k] = update(outer1[side][i], first, inner1[side][i], total1, edge_rates[side][i])
    repeated = chosen[1] == chosen[0]
    for k in range(3):
        values = []
        for f, i in enumerate(pair):
            before = edge[0, f] if k == 0 else eta2[k - 1][i]
            after = edge[1, f] if k == 2 else eta2[k + 1][i]
            value = update(eta2[k][i], before, after, totals[k], rates[k, i])
            values.append(value)
        values[1] = jnp.where(repeated, values[0], values[1])
        for f in range(2):
            base = k * 2 * depth + f * depth
            fields[base : base + depth] = values[f]
    copies[2].wait()
    copies[3].wait()
    full = dot3((high[...], low[...]), split(fields[...]), ((1,), (1,)))
    slots = width // 2
    lanes = 4 * depth
    half = lanes // 2
    real_lane = lax.broadcasted_iota(jnp.int32, (slots, lanes), 1) < half
    for k in range(3):
        at = slice(k // 2 * lanes, k // 2 * lanes + lanes)
        cosine, sine = full[:slots, at], full[slots:, at]
        if k % 2:
            cosine = pltpu.roll(cosine, half, 1)
        else:
            sine = pltpu.roll(sine, half, 1)
        part = jnp.where(real_lane, cosine, sine)
        if packed.shape[0] == 3:
            packed[k] = part
        else:
            devices, rows, _ = packed.shape
            rows = rows // 3
            packed[:, k * rows : (k + 1) * rows, :] = part.reshape(devices, rows, lanes)


def rest_kernel(
    prev3, next3,
    chosen_any, classes_any, p0_any, p2_any, prev1_any, next1_any, prev2_any, next2_any, near_any, middle_any,
    rates_any, out_any,
    chosen, classes, p0, p2, prev1, next1, prev2, next2, near_out, middle, rates, second, edge, out, semaphores,
):
    near_state, near_source = groups(near_out, 5), groups(near_any, 5)
    edge_rates, inner1, middle2 = near_state[:2], near_state[2:4], near_state[4]
    outer1, side2 = groups(second, 2), groups(second, 2, 2 * GRAINS)
    copies = fetch(
        (
            (prev1_any, prev1), (prev2_any, prev2), (p0_any, p0), (near_source[0], near_state[0]),
            (next1_any, next1), (next2_any, next2), (p2_any, p2), (near_source[1], near_state[1]),
            (near_source[2], near_state[2]), (middle_any, middle), (rates_any.at[0], rates.at[0]),
            (near_source[3], near_state[3]), (rates_any.at[2], rates.at[2]),
            (chosen_any, chosen), (classes_any, classes),
            (near_source[4], near_state[4]), (rates_any.at[1], rates.at[1]),
        ),
        semaphores,
    )

    def wait(first, last):
        for copy in copies[first:last]:
            copy.wait()

    wait(0, 4)
    step_plane(prev1, prev2, p0, edge_rates[0], outer1[0])
    wait(4, 8)
    step_plane(next1, p2, next2, edge_rates[1], outer1[1])
    wait(8, 11)
    step_plane(inner1[0], outer1[0], middle, rates.at[0], side2[0])
    wait(11, 13)
    step_plane(inner1[1], middle, outer1[1], rates.at[2], side2[1])
    wait(13, 17)
    other = others_of(chosen)
    pair = pair_of(chosen)
    places = [(pair[k], GRAINS + k, None) for k in range(2)] + [(other(r), None, r) for r in range(GRAINS - 2)]
    eta2 = (side2[0], middle2, side2[1])
    outs = []

    def finish(plane):
        total = squares(eta2[plane])
        for k, (i, _, _) in enumerate(places):
            before = edge[0, k] if plane == 0 else eta2[plane - 1][i]
            after = edge[1, k] if plane == 2 else eta2[plane + 1][i]
            out[i, plane] = update(eta2[plane][i], before, after, total, rates[plane, i])
        outs.extend(fetch(((out.at[:, plane], out_any.at[:, plane]),), semaphores.at[pl.ds(17 + plane, 1)]))

    finish(1)
    for side, (far, mid, near) in enumerate(((prev3, prev2, prev1), (next3, next2, next1))):
        ids = grain_of(mid)
        total0 = squares(mid)
        total1 = squares(outer1[side])
        for k, (i, early, late) in enumerate(places):
            third = far[late] if early is None else mid[early]
            first = update(mid[i], third, near[i], total0, rate(classes, ids, i))
            edge[side, k] = update(outer1[side][i], first, inner1[side][i], total1, edge_rates[side][i])
        finish(2 * side)
    for copy in outs:
        copy.wait()


def line_kernel(lines, z_forward, z_inverse, x_both, out, wide, tall, scale):
    rows, lanes = lines.shape
    total_x = wide.shape[0] // 3
    slots = rows // total_x
    half = lanes // 2

    def over_x(pieces, chunk=4):
        results = []
        for j in range(0, slots, chunk):
            group = pieces[j : j + chunk]
            high, low = split(jnp.concatenate(group, axis=1))
            stacked = jnp.concatenate([high, low, high], axis=0)
            both = jnp.dot(x_both[...], stacked, preferred_element_type=F32)
            for k in range(len(group)):
                at = slice(k * lanes, (k + 1) * lanes)
                results.append((both[:total_x, at], both[total_x:, at]))
        return results

    def put(row, even, odd):
        at = slice(row * total_x, (row + 1) * total_x)
        for base, value in ((0, even), (lanes, odd)):
            high, low = split(value)
            tall[0, at, base : base + lanes] = high
            tall[1, at, base : base + lanes] = low

    real_lane = lax.broadcasted_iota(jnp.int32, (total_x, lanes), 1) < half
    turned = over_x([lines[pl.ds(j, total_x, stride=slots), :] for j in range(slots)])
    for j, (even, odd) in enumerate(turned):
        put(j, even, odd)
    first_even, first_odd = turned[0]
    put(slots, jnp.where(real_lane, first_even, 0.0), jnp.where(real_lane, first_odd, 0.0))
    put(
        slots + 1,
        jnp.where(real_lane, pltpu.roll(first_even, half, 1), 0.0),
        jnp.where(real_lane, pltpu.roll(first_odd, half, 1), 0.0),
    )
    step = 2 * total_x
    parts = []
    for row in range(0, (slots + 2) * total_x, step):
        at = slice(row, row + step)
        part = dot3((tall[0, at], tall[1, at]), (z_forward[0], z_forward[1]))
        part = part * part
        part = part + pltpu.roll(part, half, 1)
        parts += [part[:total_x], part[total_x:]]

    def power(j):
        return parts[j]

    first = lax.axis_index("gx") == 0
    lane = lax.broadcasted_iota(jnp.int32, (total_x, lanes), 1)
    line = lax.broadcasted_iota(jnp.int32, (total_x, lanes), 0)
    constant = jnp.logical_and(line == 0, jnp.logical_or(lane == 0, lane == half // 2))
    powers = []
    for j in range(slots):
        value = jnp.where(real_lane, power(j), 0.0) * (2.0 * scale)
        if j == 0:
            special = jnp.where(real_lane, power(slots), power(slots + 1)) * scale
            special = jnp.where(constant, 0.0, special)
            value = jnp.where(first, special, value)
        powers.append(value)
    for j, (even, odd) in enumerate(over_x(powers)):
        put(j, even, odd)
    for j in range(0, slots, 2):
        at = slice(j * total_x, (j + 2) * total_x)
        back = dot3((tall[0, at], tall[1, at]), (z_inverse[0], z_inverse[1]))
        out[pl.ds(j, total_x, stride=slots), :] = back[:total_x]
        out[pl.ds(j + 1, total_x, stride=slots), :] = back[total_x:]


def finish_kernel(returned, high, low, out_any, out, semaphores):
    fields, planes, depth, width = out.shape
    lanes = 2 * fields * depth
    half = lanes // 2
    slots = width // 2
    stacked = []
    for k in range(planes):
        if returned.shape[0] == planes:
            part = returned[k]
        else:
            devices, rows, _ = returned.shape
            rows = rows // planes
            part = returned[:, k * rows : (k + 1) * rows, :].reshape(slots, lanes)
        part = part.T
        stacked.append(jnp.concatenate([part[:half], part[half:]], axis=1))
    stacked = split(jnp.concatenate(stacked, axis=0))
    copies = []
    for piece in range(2):
        at = slice(piece * slots, (piece + 1) * slots)
        result = dot3(stacked, (high[:, at], low[:, at]))
        for k in range(planes):
            for f in range(fields):
                base = k * half + f * depth
                out[f, k, :, at] = result[base : base + depth]
        copies += fetch(((out.at[:, :, :, at], out_any.at[:, :, :, at]),), semaphores.at[pl.ds(piece, 1)])
    for copy in copies:
        copy.wait()


def call(kernel, outs, in_specs, *args, scratch=(), flops=0, moved=0, limit=12, out_specs=None):
    args = [pltpu.with_memory_space_constraint(a, pltpu.HBM) if b is ANY else a for a, b in zip(args, in_specs)]
    return pl.pallas_call(
        kernel,
        out_shape=outs,
        in_specs=in_specs,
        out_specs=out_specs or jax.tree.map(lambda _: VMEM, outs),
        scratch_shapes=scratch,
        compiler_params=pltpu.CompilerParams(vmem_limit_bytes=limit * MIB),
        cost_estimate=pl.CostEstimate(flops=flops, bytes_accessed=moved, transcendentals=0),
    )(*args)


def shards(grain_ids, jitter, class_table, chosen):
    planes, depth, width = grain_ids.shape
    devices = lax.axis_size("gx")
    total_x = planes * devices
    count = float(total_x * depth * width)
    slots = width // 2
    share = slots // devices
    lanes = 4 * depth
    up = [(i, (i + 1) % devices) for i in range(devices)]
    down = [(j, i) for i, j in up]
    aligned = share % 8 == 0

    def shape(*dims):
        return jax.ShapeDtypeStruct(dims, F32)

    plane = (GRAINS, depth, width)
    table = [jnp.asarray(part) for part in halves(y_table(width))]
    z_forward, z_inverse = z_tables(depth)
    z_parts = [jnp.asarray(np.stack(halves(matrix))) for matrix in (z_forward, z_inverse)]
    x_high, x_low = halves(np.concatenate(phases(total_x), axis=0))
    x_both = jnp.asarray(np.concatenate([x_high, x_high, x_low], axis=1))

    two = (2, *plane)
    six = (GRAINS - 2, depth, width)
    small = [pltpu.SMEM((2,), jnp.int32), pltpu.SMEM((GRAINS, GRAINS), jnp.int32)]
    ten = (GRAINS + 2, depth, width)
    p0, p1, p2 = call(
        start_kernel,
        (shape(*plane), shape(*plane), shape(*plane)),
        [ANY] * 2,
        jitter, grain_ids,
        scratch=[
            pltpu.VMEM(jitter.shape, jitter.dtype),
            pltpu.VMEM(grain_ids.shape, jnp.int32),
            pltpu.SemaphoreType.DMA((2 * planes,)),
        ],
        flops=2**21, moved=2**22,
    )
    prev1 = lax.ppermute(p2, "gx", up)
    next1 = lax.ppermute(p0, "gx", down)
    up2, down2, r0, r2, rates, middle = call(
        inner_kernel,
        (
            shape(*ten), shape(*ten), shape(*six), shape(*six),
            shape(planes, *plane), shape(*plane),
        ),
        [ANY] * 2 + [VMEM] * 3,
        chosen, class_table, p0, p1, p2,
        scratch=[*small, pltpu.SemaphoreType.DMA((2,))],
        flops=2**24, moved=2**22,
    )
    prev2 = lax.ppermute(up2, "gx", up)
    next2 = lax.ppermute(down2, "gx", down)
    r0, r2, prev1, next1 = lax.optimization_barrier((r0, r2, prev1, next1))
    prev3 = lax.ppermute(r0, "gx", up)
    next3 = lax.ppermute(r2, "gx", down)
    near_out = call(
        near_kernel,
        shape(5 * GRAINS, depth, width),
        [ANY] + [VMEM] * 7,
        class_table, p0, p1, p2, prev1, next1, rates, middle,
        scratch=[small[1], pltpu.SemaphoreType.DMA((1,))],
        flops=2**25, moved=2**24,
    )
    packed_shape = (devices, planes * share, lanes) if aligned else (planes, slots, lanes)
    packed = call(
        pair_kernel,
        shape(*packed_shape),
        [ANY] * 2 + [VMEM] * 9 + [ANY] * 2,
        chosen, class_table, p0, p2, prev1, next1, prev2, next2, rates, middle, near_out, *table,
        scratch=[
            *small,
            pltpu.VMEM(table[0].shape, BF16),
            pltpu.VMEM(table[1].shape, BF16),
            pltpu.VMEM((4 * GRAINS, depth, width), F32),
            pltpu.VMEM((2, 2, depth, width), F32),
            pltpu.VMEM(((planes + 1) // 2 * lanes, width), F32),
            pltpu.SemaphoreType.DMA((4,)),
        ],
        flops=2**28, moved=2**23,
    )
    packed, prev3, next3 = lax.optimization_barrier((packed, prev3, next3))
    if aligned:
        lines = lax.all_to_all(packed, "gx", split_axis=0, concat_axis=0, tiled=True)
    else:
        lines = lax.all_to_all(packed, "gx", split_axis=1, concat_axis=0, tiled=True)
    lines = lines.reshape(total_x * share, lanes)

    def lines_body(*refs):
        line_kernel(*refs, scale=1.0 / (count * count))

    back = call(
        lines_body,
        shape(total_x * share, lanes),
        [VMEM] * 4,
        lines, *z_parts, x_both,
        scratch=[
            pltpu.VMEM((3 * total_x, share * lanes), BF16),
            pltpu.VMEM((2, total_x * (share + 2), 2 * lanes), BF16),
        ],
        flops=2**28, moved=2**22,
    )
    back = back.reshape(devices, planes * share, lanes)
    returned = lax.all_to_all(back, "gx", split_axis=0, concat_axis=0, tiled=True)
    if not aligned:
        returned = returned.reshape(devices, planes, share, lanes).transpose(1, 0, 2, 3)
        returned = returned.reshape(planes, slots, lanes)
    late = (
        prev3, next3,
        chosen, class_table, p0, p2, prev1, next1, prev2, next2, near_out, middle, rates,
    )
    late, _ = lax.optimization_barrier((late, back))
    order_params = call(
        rest_kernel,
        shape(GRAINS, planes, depth, width),
        [VMEM] * 2 + [ANY] * (len(late) - 2),
        *late,
        scratch=[
            *small,
            *[pltpu.VMEM(value.shape, F32) for value in late[4:]],
            pltpu.VMEM((4 * GRAINS, depth, width), F32),
            pltpu.VMEM((2, *plane), F32),
            pltpu.VMEM((GRAINS, planes, depth, width), F32),
            pltpu.SemaphoreType.DMA((17 + planes,)),
        ],
        out_specs=ANY, flops=2**37, moved=2**24, limit=24,
    )
    correlation = call(
        finish_kernel,
        shape(2, planes, depth, width),
        [VMEM] * 3,
        returned, *table,
        scratch=[pltpu.VMEM((2, planes, depth, width), F32), pltpu.SemaphoreType.DMA((2,))],
        out_specs=ANY,
        flops=2**28, moved=2**22,
    )
    return (order_params, correlation)


def solution(mesh):
    in_specs = (P(("grp", "gx"), None, None), P(None, ("grp", "gx"), None, None), P(), P())
    out_specs = (P(None, ("grp", "gx"), None, None), P(None, ("grp", "gx"), None, None))
    return jax.shard_map(shards, mesh=mesh, in_specs=in_specs, out_specs=out_specs, check_vma=False)
```
